32 devices in a mesh: th: 4 (over z), ph: 8 (over y, x, core).
Axes of the slice: x: 2, y: 2, z: 4, core: 2. Of those that a mesh axis runs over, the one named last changes fastest.
Arguments:
- state: float32 [8, 96, 192, 256], P(None, 'th', 'ph'), may hold values from -1 to 7.5, as said below
- cotangent: float32 [8, 96, 192, 256], P(None, 'th', 'ph'), may hold values from -6 to 6
Outputs:
- sensitivity: float32 [8, 96, 192, 256], P(None, 'th', 'ph')
The draws below stay inside these ranges and needn't reach their ends.
Inputs may be any that keep to these rules, and one draw needn't show every extreme that they name: `state`: component 0 is density in 0.5 to 2, components 1 to 3 momenta and 5 to 7 magnetic face fields in -1 to 1, component 4 total energy, which exceeds the kinetic energy by 2 or more.
All inputs are finite; a program needn't handle non-finite values.
Results may differ from the reference program's by a relative error of at most 0.0003.
Values sent between devices are 32-bit elements; how exact they have to be, the bound alone decides.
No kernel may reach another device: no remote copies, remote signals or barrier semaphores. Data moves between devices by JAX's collectives and lax.ppermute only.
A program may use at most 512 MiB of HBM per device.

```python
import math
import jax
import jax.numpy as jnp
from jax import lax

NR = 256
TH_DEV = 24
NTH = 96
NPH = 192
N_TH = 4


GAMMA = 5.0 / 3.0


def draw_state(key, part):
    keys = jax.random.split(key, 5)
    shape = (NTH, NPH, NR)
    density = jax.random.uniform(keys[0], shape, jnp.float32, 0.5, 2.0)
    momentum = jax.random.uniform(keys[1], (3,) + shape, jnp.float32, -1.0, 1.0)
    magnet = jax.random.uniform(keys[2], (3,) + shape, jnp.float32, -1.0, 1.0)
    pressure = jax.random.uniform(keys[3], shape, jnp.float32, 0.5, 2.0)
    energy = 0.5 * jnp.sum(momentum * momentum, 0) / density + 1.5 + pressure / (GAMMA - 1.0)
    return jnp.concatenate([density[None], momentum, energy[None], magnet], 0)


def block_scale(rng, extent, cuts, low, top_value):
    gain = 1.0
    for position, shards_of in cuts:
        draws = jax.random.uniform(jax.random.fold_in(jax.random.fold_in(rng, 6), position), (shards_of,), jnp.float32, low / len(cuts), top_value / len(cuts))
        gain = gain * jnp.repeat(jnp.exp(draws), extent[position] // shards_of).reshape((-1,) + (1,) * (len(extent) - 1 - position))
    return gain


def scatter_about(rng, extent, scale, reach, shards=(), kind=jnp.bfloat16):
    drawn = jax.random.normal(rng, extent, jnp.float32) * scale
    if len(shards) > 0:
        drawn = block_scale(rng, extent, shards, -0.22, 0.18) * drawn
    return jnp.clip(drawn, min=-reach, max=reach).astype(kind)


def setup_inputs(seed: int = 0) -> dict:
    key_list = jax.random.split(jax.random.key(seed), 3)
    state = draw_state(jax.random.fold_in(key_list[2], 71), 0)
    cotangent = scatter_about(key_list[1], (8, NTH, NPH, NR), 1.0, 6.0, ((1, 4), (2, 8)), jnp.float32)
    return {"state": state, "cotangent": cotangent}


GAMMA = 5.0 / 3.0
R_INNER = 1.0
R_OUTER = 3.0
COURANT = 0.4
SPEED_BOUND = 5.0
PRESSURE_SOFT = 0.05
THETA_CUT = 0.1

def lower_part(values, dim_index):
    return lax.slice_in_dim(values, 0, values.shape[dim_index] - 1, axis=dim_index)

def upper_part(values, dim_index):
    return lax.slice_in_dim(values, 1, values.shape[dim_index], axis=dim_index)

def time_step(total_rows, total_cols, rad_count):
    step_phi = 2.0 * math.pi / total_cols
    step_radius = (R_OUTER - R_INNER) / rad_count
    return COURANT * min(step_radius, R_INNER * math.sin(THETA_CUT) * step_phi) / SPEED_BOUND

def section_rate(padded, row_start, total_rows, total_cols):
    row_count = padded.shape[1] - 4
    col_count = padded.shape[2] - 4
    rad_count = padded.shape[3]
    step_theta = (math.pi - 2.0 * THETA_CUT) / total_rows
    step_phi = 2.0 * math.pi / total_cols
    step_radius = (R_OUTER - R_INNER) / rad_count
    grid_vals = jnp.pad(padded, ((0, 0), (0, 0), (0, 0), (2, 2)), mode='edge')
    face_rows = row_start + jnp.arange(row_count + 4, dtype=jnp.int32) - 2
    keep_mask = jnp.where((face_rows != 0) & (face_rows != total_rows), 1.0, 0.0).astype(jnp.float32)
    polar_faces = grid_vals[6] * keep_mask[:, None, None]
    density = grid_vals[0, :-1, :-1, :-1]
    momentum = grid_vals[1:4, :-1, :-1, :-1]
    energy = grid_vals[4, :-1, :-1, :-1]
    b_radial = 0.5 * (grid_vals[5, :-1, :-1, :-1] + grid_vals[5, :-1, :-1, 1:])
    b_polar = 0.5 * (polar_faces[:-1, :-1, :-1] + polar_faces[1:, :-1, :-1])
    b_azimuth = 0.5 * (grid_vals[7, :-1, :-1, :-1] + grid_vals[7, :-1, 1:, :-1])
    magnet = jnp.stack([b_radial, b_polar, b_azimuth])
    velocity = momentum / density
    field_square = lax.optimization_barrier(jnp.sum(magnet * magnet, 0))
    pressure = (GAMMA - 1.0) * (energy - 0.5 * lax.optimization_barrier(jnp.sum(momentum * velocity, 0)) - 0.5 * field_square)
    total_p = pressure + 0.5 * field_square
    sound_sq = (GAMMA * jnp.sqrt(pressure * pressure + PRESSURE_SOFT * PRESSURE_SOFT) + field_square) / density
    vel_dot_field = lax.optimization_barrier(jnp.sum(velocity * magnet, 0))
    conserved = jnp.concatenate([density[None], momentum, energy[None]], 0)

    def face_flux(normal):
        dim_index = (3, 1, 2)[normal]
        normal_vel = velocity[normal]
        normal_field = magnet[normal]
        pieces = [density * normal_vel]
        for component in range(3):
            addend = momentum[component] * normal_vel - magnet[component] * normal_field
            if component == normal:
                addend = addend + total_p
            pieces.append(addend)
        pieces.append((energy + total_p) * normal_vel - normal_field * vel_dot_field)
        flux_vals = jnp.stack(pieces)
        speed_sq = normal_vel * normal_vel + sound_sq
        viscosity = jnp.sqrt(0.5 * (lower_part(speed_sq, dim_index - 1) + upper_part(speed_sq, dim_index - 1)))
        return 0.5 * (lower_part(flux_vals, dim_index) + upper_part(flux_vals, dim_index)) - 0.5 * viscosity * (upper_part(conserved, dim_index) - lower_part(conserved, dim_index))
    flux_radial = face_flux(0)
    flux_polar = face_flux(1)
    flux_azimuth = face_flux(2)
    jrow, kcol, irad = (row_count, col_count, rad_count)
    row_pos = (row_start + jnp.arange(row_count, dtype=jnp.int32)).astype(jnp.float32)
    theta_low = (THETA_CUT + row_pos * step_theta)[:, None, None]
    theta_high = theta_low + step_theta
    theta_mid = theta_low + 0.5 * step_theta
    radius_low = (R_INNER + jnp.arange(rad_count, dtype=jnp.float32) * step_radius)[None, None, :]
    radius_high = radius_low + step_radius
    radius_mid = radius_low + 0.5 * step_radius
    sine_low = jnp.sin(theta_low)
    sine_high = jnp.sin(theta_high)
    cos_diff = jnp.cos(theta_low) - jnp.cos(theta_high)
    shell_area = 0.5 * (radius_high * radius_high - radius_low * radius_low)
    volume = (radius_high ** 3 - radius_low ** 3) / 3.0 * cos_diff * step_phi
    area_rad_low = radius_low * radius_low * cos_diff * step_phi
    area_rad_high = radius_high * radius_high * cos_diff * step_phi
    area_pol_low = sine_low * shell_area * step_phi
    area_pol_high = sine_high * shell_area * step_phi
    area_azim = shell_area * step_theta
    net_flow = area_rad_high * flux_radial[:, 2:jrow + 2, 2:kcol + 2, 2:irad + 2] - area_rad_low * flux_radial[:, 2:jrow + 2, 2:kcol + 2, 1:irad + 1] + area_pol_high * flux_polar[:, 2:jrow + 2, 2:kcol + 2, 2:irad + 2] - area_pol_low * flux_polar[:, 1:jrow + 1, 2:kcol + 2, 2:irad + 2] + area_azim * (flux_azimuth[:, 2:jrow + 2, 2:kcol + 2, 2:irad + 2] - flux_azimuth[:, 2:jrow + 2, 1:kcol + 1, 2:irad + 2])

    def interior(values):
        return values[..., 2:jrow + 2, 2:kcol + 2, 2:irad + 2]
    rho_in = interior(density)
    vel_in = interior(velocity)
    mag_in = interior(magnet)
    press_in = interior(total_p)
    cotan_mid = jnp.cos(theta_mid) / jnp.sin(theta_mid)
    source_rad = (rho_in * (vel_in[1] ** 2 + vel_in[2] ** 2) - (mag_in[1] ** 2 + mag_in[2] ** 2) + 2.0 * press_in) / radius_mid
    source_pol = ((rho_in * vel_in[2] ** 2 - mag_in[2] ** 2 + press_in) * cotan_mid - rho_in * vel_in[0] * vel_in[1] + mag_in[0] * mag_in[1]) / radius_mid
    source_azim = -(rho_in * vel_in[0] * vel_in[2] - mag_in[0] * mag_in[2] + cotan_mid * (rho_in * vel_in[1] * vel_in[2] - mag_in[1] * mag_in[2])) / radius_mid
    zeroes = jnp.zeros_like(source_rad)
    hydro = -net_flow / volume + jnp.stack([zeroes, source_rad, source_pol, source_azim, zeroes])
    e_radial = velocity[2] * magnet[1] - velocity[1] * magnet[2]
    e_polar = velocity[0] * magnet[2] - velocity[2] * magnet[0]
    e_azimuth = velocity[1] * magnet[0] - velocity[0] * magnet[1]
    edge_radial = 0.25 * (e_radial[:-1, :-1] + e_radial[1:, :-1] + e_radial[:-1, 1:] + e_radial[1:, 1:])
    edge_polar = 0.25 * (e_polar[:, :-1, :-1] + e_polar[:, 1:, :-1] + e_polar[:, :-1, 1:] + e_polar[:, 1:, 1:])
    edge_azimuth = 0.25 * (e_azimuth[:-1, :, :-1] + e_azimuth[1:, :, :-1] + e_azimuth[:-1, :, 1:] + e_azimuth[1:, :, 1:])
    azim_at_low = edge_azimuth[1:jrow + 1, 2:kcol + 2, 1:irad + 1]
    azim_high_theta = edge_azimuth[2:jrow + 2, 2:kcol + 2, 1:irad + 1]
    azim_high_radius = edge_azimuth[1:jrow + 1, 2:kcol + 2, 2:irad + 2]
    polar_at_low = edge_polar[2:jrow + 2, 1:kcol + 1, 1:irad + 1]
    polar_high_phi = edge_polar[2:jrow + 2, 2:kcol + 2, 1:irad + 1]
    polar_high_radius = edge_polar[2:jrow + 2, 1:kcol + 1, 2:irad + 2]
    radial_at_low = edge_radial[1:jrow + 1, 1:kcol + 1, 2:irad + 2]
    radial_high_phi = edge_radial[1:jrow + 1, 2:kcol + 2, 2:irad + 2]
    radial_high_theta = edge_radial[2:jrow + 2, 1:kcol + 1, 2:irad + 2]
    circ_radial = radius_low * step_phi * (azim_high_theta * sine_high - azim_at_low * sine_low) - radius_low * step_theta * (polar_high_phi - polar_at_low)
    rate_radial = -circ_radial / area_rad_low
    circ_polar = step_radius * (radial_high_phi - radial_at_low) - step_phi * sine_low * (radius_high * azim_high_radius - radius_low * azim_at_low)
    keep_inner = keep_mask[2:jrow + 2][:, None, None]
    rate_polar = -circ_polar * keep_inner / jnp.where(keep_inner > 0.5, area_pol_low, 1.0)
    circ_azim = step_theta * (radius_high * polar_high_radius - radius_low * polar_at_low) - step_radius * (radial_high_theta - radial_at_low)
    rate_azim = -circ_azim / area_azim
    return jnp.concatenate([hydro, jnp.stack([rate_radial, rate_polar, rate_azim])], 0)

def advance(padded, row_start, total_rows, total_cols):
    rate = section_rate(padded, row_start, total_rows, total_cols)
    delta = time_step(total_rows, total_cols, padded.shape[3])
    return padded[:, 2:-2, 2:-2] + delta * rate

def pole_ghosts(received, width):
    flip_signs = jnp.array([1.0, 1.0, -1.0, -1.0, 1.0, 1.0, -1.0, -1.0], jnp.float32)[:, None, None, None]
    first_rows = received[:, :width + 2]
    last_rows = received[:, width + 2:]
    cells_low = first_rows[:, width - 1::-1]
    face_low = first_rows[6:7, width + 1:1:-1]
    cells_high = last_rows[:, ::-1]
    face_high = jnp.concatenate([last_rows[6:7, width - 1:width], last_rows[6:7, width - 1:0:-1]], 1)
    low_ghost = jnp.concatenate([cells_low[:6], face_low, cells_low[7:]], 0) * flip_signs
    high_ghost = jnp.concatenate([cells_high[:6], face_high, cells_high[7:]], 0) * flip_signs
    return (low_ghost, high_ghost)

def wrap_columns(values):
    return jnp.concatenate([values[:, :, -2:], values, values[:, :, :2]], 2)

def pad_whole(grid_vals):
    side_pad = wrap_columns(grid_vals)
    turned = wrap_columns(jnp.roll(grid_vals, NPH // 2, axis=2))
    received = jnp.concatenate([turned[:, 0:4], turned[:, NTH - 2:NTH]], 1)
    low_ghost, high_ghost = pole_ghosts(received, 2)
    return jnp.concatenate([low_ghost, side_pad, high_ghost], 1)

def advance_whole(grid_vals):
    padded = pad_whole(grid_vals)

    def one_block(block_index):
        row_block = lax.dynamic_slice_in_dim(padded, block_index * TH_DEV, TH_DEV + 4, 1)
        return advance(row_block, block_index * TH_DEV, NTH, NPH)
    blocks = lax.map(jax.checkpoint(one_block), jnp.arange(N_TH, dtype=jnp.int32))
    return jnp.moveaxis(blocks, 0, 1).reshape(grid_vals.shape)

def full_step(grid_vals):
    first_section = advance_whole(grid_vals)
    return 0.5 * grid_vals + 0.5 * advance_whole(first_section)

def reference(state, cotangent):
    _, pull_back = jax.vjp(full_step, state)
    return pull_back(cotangent)[0]
```

```python
import functools
import math

import jax
import jax.numpy as jnp
import numpy as np
from jax import lax
from jax.experimental import pallas as pl
from jax.experimental.pallas import tpu as pltpu
from jax.sharding import PartitionSpec as P

GAMMA = 5.0 / 3.0
R_INNER = 1.0
R_OUTER = 3.0
COURANT = 0.4
SPEED_BOUND = 5.0
PRESSURE_SOFT = 0.05
THETA_CUT = 0.1

G1 = GAMMA - 1.0
LANES = 128
PAD = 16
FLIPS = (1.0, 1.0, -1.0, -1.0, 1.0, 1.0, -1.0, -1.0)
SH, SL, AZ, COT, AK, KEEP, N_ROW = 0, 1, 2, 3, 4, 5, 6
INV_V, R_HI2, K_V, INV_MID, INV_LO, LO, HI, INV_SHELL, HALF_HI2, HALF_KV, HALF_LO2, TOP, OPEN = range(13)


class Grid:
    def __init__(self, rows, cols, rads, total_rows, total_cols):
        self.rows, self.cols, self.rads = rows, cols, rads
        self.width = cols + 8
        self.tiles = self.width // 8
        self.slots = PAD + (rows + 4) * self.width + PAD
        self.dth = (math.pi - 2.0 * THETA_CUT) / total_rows
        self.dph = 2.0 * math.pi / total_cols
        self.dr = (R_OUTER - R_INNER) / rads
        self.dt = COURANT * min(self.dr, R_INNER * math.sin(THETA_CUT) * self.dph) / SPEED_BOUND
        self.total_rows = total_rows

    def at(self, j, k):
        return PAD + (j + 2) * self.width + k

    def row_table(self):
        j = np.arange(-2, self.total_rows + 3, dtype=np.float64)
        low = THETA_CUT + j * self.dth
        high, mid = low + self.dth, low + 0.5 * self.dth
        drop = np.cos(low) - np.cos(high)
        keep = np.where((j == 0) | (j == self.total_rows), 0.0, 1.0)
        safe = np.where(np.abs(np.sin(low)) < 1e-6, 1.0, np.sin(low))
        table = np.zeros((len(j), N_ROW))
        table[:, SH] = np.sin(high) / drop
        table[:, SL] = np.sin(low) / drop
        table[:, AZ] = self.dth / (drop * self.dph)
        table[:, COT] = np.cos(mid) / np.sin(mid)
        table[:, AK] = keep / (safe * self.dph)
        table[:, KEEP] = keep
        return table.astype(np.float32)

    def radial_planes(self):
        i = np.arange(self.rads, dtype=np.float64)
        low = R_INNER + i * self.dr
        high, mid = low + self.dr, low + 0.5 * self.dr
        vol = (high**3 - low**3) / 3.0
        shell = 0.5 * (high**2 - low**2)
        top = np.where(i == self.rads - 1, 2.0, 1.0)
        planes = [None] * 13
        planes[INV_V] = 1.0 / vol
        planes[R_HI2] = high**2
        planes[K_V] = shell / vol
        planes[INV_MID] = 1.0 / mid
        planes[INV_LO] = 1.0 / low
        planes[LO] = low
        planes[HI] = high
        planes[INV_SHELL] = 1.0 / shell
        planes[HALF_HI2] = 0.5 * self.dt * high**2
        planes[HALF_KV] = 0.5 * self.dt * shell / vol
        planes[HALF_LO2] = 0.5 * self.dt * low**2
        planes[TOP] = top
        planes[OPEN] = 2.0 - top
        stack = np.stack(planes).astype(np.float32).reshape(13, 2, 1, LANES)
        return np.broadcast_to(stack, (13, 2, 8, LANES)).copy()


def lane_index():
    return lax.broadcasted_iota(jnp.int32, (2, 8, LANES), 2)


def next_r(x, last=None):
    turned = pltpu.roll(x, LANES - 1, 2)
    end = x[1:2] if last is None else last
    return jnp.where(lane_index() == LANES - 1, jnp.concatenate([turned[1:2], end], 0), turned)


def prev_r(x, first):
    turned = pltpu.roll(x, 1, 2)
    return jnp.where(lane_index() == 0, jnp.concatenate([first, turned[0:1]], 0), turned)


def split(x):
    return jnp.stack([x[:, :LANES], x[:, LANES:]])


def load(ref, field, slot):
    return ref[field, :, pl.ds(slot, 8), :]


def put(ref, field, slot, value):
    ref[field, :, pl.ds(slot, 8), :] = value


def put_line(ref, field, slot, line):
    ref[field, 0, pl.ds(slot, 1), :] = line[:, :LANES]
    ref[field, 1, pl.ds(slot, 1), :] = line[:, LANES:]


def get_line(ref, field, slot):
    return jnp.concatenate([ref[field, 0, pl.ds(slot, 1), :], ref[field, 1, pl.ds(slot, 1), :]], 1)


def fill_state(g, us, row_ref, own, phlo, phhi, thlo, thhi):
    rows, cols = g.rows, g.cols

    def keep(j):
        return row_ref[(j + 2) * N_ROW + KEEP]

    def ends(j, fetch):
        for c in range(8):
            scale = keep(j) if c == 6 else None
            for which, k in ((0, -1), (1, cols)):
                line = fetch(c, which)
                put_line(us, c, g.at(j, k), line if scale is None else line * scale)
        put_line(us, 7, g.at(j, cols + 1), fetch(7, 2))

    def body_row(j, tile_of):
        for c in range(8):
            for t in range(cols // 8):
                x = split(tile_of(c, t))
                if c == 6:
                    x = x * keep(j)
                put(us, c, g.at(j, t * 8), x)
                if t == 0:
                    put(us, c, g.at(j, cols), x)

    for c in range(8):
        put(us, c, g.at(-1, -8), split(thlo[c, 0:8, :]))
    body_row(-1, lambda c, t: thlo[c, t * 8 : t * 8 + 8, :])
    ends(-1, lambda c, w: thlo[9, (c, 9 + c, 18)[w] : (c, 9 + c, 18)[w] + 1, :])

    def step(j, carry):
        body_row(j, lambda c, t: own[c, j, t * 8 : t * 8 + 8, :])
        ends(j, lambda c, w: (phlo[c, pl.ds(j, 1), :], phhi[c, pl.ds(j, 1), :], phhi[8, pl.ds(j, 1), :])[w])
        return carry

    lax.fori_loop(0, rows, step, 0)
    body_row(rows, lambda c, t: thhi[c, t * 8 : t * 8 + 8, :])
    ends(rows, lambda c, w: thhi[9, (c, 9 + c, 18)[w] : (c, 9 + c, 18)[w] + 1, :])
    far = keep(rows + 1)
    for t in range(g.tiles):
        x = split(thhi[8, t * 8 : t * 8 + 8, :]) if t < cols // 8 else jnp.zeros((2, 8, LANES), jnp.float32)
        put(us, 6, g.at(rows + 1, t * 8), x * far)
    put_line(us, 6, g.at(rows + 1, -1), thhi[9, 8:9, :] * far)
    put_line(us, 6, g.at(rows + 1, cols), thhi[9, 17:18, :] * far)


def cell_values(g, us, p):
    rho, m0, m1, m2, energy, u5, u6, u7 = [load(us, c, p) for c in range(8)]
    b0 = 0.5 * (u5 + next_r(u5))
    b1 = 0.5 * (u6 + load(us, 6, p + g.width))
    b2 = 0.5 * (u7 + load(us, 7, p + 1))
    q = 1.0 / rho
    v0, v1, v2 = m0 * q, m1 * q, m2 * q
    square = b0 * b0 + b1 * b1 + b2 * b2
    pressure = G1 * (energy - 0.5 * (m0 * v0 + m1 * v1 + m2 * v2) - 0.5 * square)
    total = pressure + 0.5 * square
    soft = pressure * pressure + PRESSURE_SOFT * PRESSURE_SOFT
    inv_soft = lax.rsqrt(soft)
    c2 = (GAMMA * (soft * inv_soft) + square) * q
    return (m0, m1, m2), (v0, v1, v2), (b0, b1, b2), u5, q, pressure, total, energy + total, inv_soft, c2


def forward_kernel(g, row_ref, own, phlo, phhi, thlo, thhi, rc, out, us, cf, gf, ff):
    fill_state(g, us, row_ref, own, phlo, phhi, thlo, thhi)
    w = g.width

    def cells(n, carry):
        p = pl.multiple_of(g.at(-1, -8) + n * 8, 8)
        m, v, b, u5, q, pressure, total, h, inv_soft, c2 = cell_values(g, us, p)
        put(cf, 0, p, m[0] * v[0] - b[0] * b[0] + total)
        put(cf, 1, p, m[0] * v[1] - b[0] * b[1])
        put(cf, 2, p, m[0] * v[2] - b[0] * b[2])
        put(cf, 3, p, m[1] * v[1] - b[1] * b[1] + total)
        put(cf, 4, p, m[1] * v[2] - b[1] * b[2])
        put(cf, 5, p, m[2] * v[2] - b[2] * b[2] + total)
        vb = v[0] * b[0] + v[1] * b[1] + v[2] * b[2]
        for d in range(3):
            put(cf, 6 + d, p, h * v[d] - b[d] * vb)
            put(cf, 9 + d, p, v[d] * v[d] + c2)
        put(cf, 12, p, v[2] * b[1] - v[1] * b[2])
        put(cf, 13, p, v[0] * b[2] - v[2] * b[0])
        put(cf, 14, p, v[1] * b[0] - v[0] * b[1])
        m, v, b = [[x[0:1] for x in y] for y in (m, v, b)]
        bg = u5[0:1]
        gain = (1.0 - 0.5 * GAMMA) * (bg * bg - b[0] * b[0])
        vbg = vb[0:1] + v[0] * (bg - b[0])
        ghost = (
            m[0] * v[0] - bg * bg + total[0:1] + gain,
            m[0] * v[1] - bg * b[1],
            m[0] * v[2] - bg * b[2],
            (h[0:1] + gain) * v[0] - bg * vbg,
            v[0] * b[2] - v[2] * bg,
            v[1] * bg - v[0] * b[1],
        )
        for f, x in enumerate(ghost):
            gf[f, pl.ds(p, 8), :] = x[0]
        return carry

    lax.fori_loop(0, (g.rows + 2) * g.tiles + 1, cells, 0)

    index = ((0, 1, 2), (1, 3, 4), (2, 4, 5))

    def face(d, p, shift):
        fluxes = [load(us, 1 + d, p)] + [load(cf, index[d][c], p) for c in range(3)] + [load(cf, 6 + d, p)]
        speed = load(cf, 9 + d, p)
        state = [load(us, c, p) for c in range(5)]
        if shift is None:
            other = [next_r(x) for x in fluxes]
            speed2 = next_r(speed)
            state2 = [other[0] if c == 1 else next_r(state[c]) for c in range(5)]
        else:
            r = p + shift
            other = [load(us, 1 + d, r)] + [load(cf, index[d][c], r) for c in range(3)] + [load(cf, 6 + d, r)]
            speed2 = load(cf, 9 + d, r)
            state2 = [load(us, c, r) for c in range(5)]
        total = 0.5 * (speed + speed2)
        half = 0.5 * (total * lax.rsqrt(total))
        return fluxes, [0.5 * (fluxes[c] + other[c]) - half * (state2[c] - state[c]) for c in range(5)]

    def faces(n, carry):
        p = pl.multiple_of(g.at(-1, 0) + n * 8, 8)
        for d, shift, base in ((1, w, 0), (2, 1, 5)):
            _, flux = face(d, p, shift)
            for c in range(5):
                put(ff, base + c, p, flux[c])
        return carry

    lax.fori_loop(0, (g.rows + 1) * g.tiles, faces, 0)

    own_tiles = g.cols // 8

    def combine(n, carry):
        j = n // own_tiles
        t = n - j * own_tiles
        p = pl.multiple_of(g.at(j, t * 8), 8)
        row = (j + 2) * N_ROW
        sh, sl, az, cot, ak, keep = [row_ref[row + i] for i in range(N_ROW)]
        cells_here, flux_r = face(0, p, None)
        ghost = [load(us, 1, p)[0:1]] + [gf[f, pl.ds(p, 8), :][None] for f in range(4)]
        inv_v, kv = rc[INV_V], rc[K_V]
        rates = []
        for c in range(5):
            high = rc[R_HI2] * flux_r[c]
            first = 0.5 * rc[HALF_LO2][0:1] * (2.0 / g.dt) * (ghost[c] + cells_here[c][0:1])
            low = prev_r(high, first)
            th = sh * load(ff, c, p) - sl * load(ff, c, p - w)
            ph = az * (load(ff, 5 + c, p) - load(ff, 5 + c, p - 1))
            rates.append(-(inv_v * (high - low) + kv * (th + ph)))
        tt = [load(cf, f, p) for f in range(1, 6)]
        mid = rc[INV_MID]
        rates[1] = rates[1] + (tt[2] + tt[4]) * mid
        rates[2] = rates[2] + (cot * tt[4] - tt[0]) * mid
        rates[3] = rates[3] - (tt[1] + cot * tt[3]) * mid
        ep, ept = load(cf, 14, p), load(cf, 14, p + w)
        x0 = load(cf, 14, p - w) + ep
        x1 = ep + ept
        g_here = gf[5, pl.ds(p, 8), :][None]
        x0m = prev_r(x0, gf[5, pl.ds(p - w, 8), :][None] + g_here)
        x1m = prev_r(x1, g_here + gf[5, pl.ds(p + w, 8), :][None])
        z0 = 0.25 * (x0 + x0m)
        zr = 0.25 * (next_r(x0) + x0)
        z1 = 0.25 * (x1 + x1m)
        et = load(cf, 13, p)
        y0 = load(cf, 13, p - 1) + et
        y1 = et + load(cf, 13, p + 1)
        g_here = gf[4, pl.ds(p, 8), :][None]
        y0m = prev_r(y0, gf[4, pl.ds(p - 1, 8), :][None] + g_here)
        y1m = prev_r(y1, g_here + gf[4, pl.ds(p + 1, 8), :][None])
        p0 = 0.25 * (y0 + y0m)
        pr = 0.25 * (next_r(y0) + y0)
        p1 = 0.25 * (y1 + y1m)
        er, era, erb = load(cf, 12, p), load(cf, 12, p - 1), load(cf, 12, p - w)
        r0 = 0.25 * (er + era + erb + load(cf, 12, p - w - 1))
        r1 = 0.25 * (load(cf, 12, p + 1) + er + load(cf, 12, p - w + 1) + erb)
        rt = 0.25 * (load(cf, 12, p + w) + load(cf, 12, p + w - 1) + er + era)
        lo, hi, shell = rc[LO], rc[HI], rc[INV_SHELL]
        rates.append(-rc[INV_LO] * (sh * z1 - sl * z0 - az * (p1 - p0)))
        rates.append(-shell * (g.dr * ak * (r1 - r0) - keep * (hi * zr - lo * z0)))
        rates.append(shell * ((g.dr / g.dth) * (rt - r0) - (hi * pr - lo * p0)))
        for c in range(8):
            new = own[c, j, pl.ds(pl.multiple_of(t * 8, 8), 8), :] + g.dt * jnp.concatenate([rates[c][0], rates[c][1]], 1)
            out[c, j, pl.ds(pl.multiple_of(t * 8, 8), 8), :] = new
        return carry

    lax.fori_loop(0, g.rows * own_tiles, combine, 0)


def adjoint_kernel(
    g, row_ref, own, phlo, phhi, thlo, thhi, cot_ref, rc, out, gphlo, gphhi, gthlo, gthhi, us, cs, cf, ef, zf, ft, fp
):
    fill_state(g, us, row_ref, own, phlo, phhi, thlo, thhi)
    w, rows, cols = g.width, g.rows, g.cols
    zero = jnp.zeros((2, 8, LANES), jnp.float32)

    def clear(n, carry):
        p = pl.multiple_of(n * 8, 8)
        for c in range(8):
            put(cs, c, p, zero)
        return carry

    lax.fori_loop(0, g.slots // 8, clear, 0)

    def take(j, carry):
        for c in range(8):
            for t in range(cols // 8):
                put(cs, c, g.at(j, t * 8), split(cot_ref[c, j, t * 8 : t * 8 + 8, :]))
        return carry

    lax.fori_loop(0, rows, take, 0)

    def cells(n, carry):
        p = pl.multiple_of(g.at(-1, -8) + n * 8, 8)
        m, v, b, u5, q, pressure, total, h, inv_soft, c2 = cell_values(g, us, p)
        for d in range(3):
            put(cf, d, p, v[d])
            put(cf, 3 + d, p, b[d])
            put(cf, 6 + d, p, v[d] * v[d] + c2)
        put(cf, 9, p, h)
        put(cf, 10, p, q)
        put(cf, 11, p, GAMMA * q * (pressure * inv_soft))
        put(cf, 12, p, c2 * q)
        return carry

    lax.fori_loop(0, (rows + 2) * g.tiles + 1, cells, 0)

    none = jnp.zeros((1, 8, LANES), jnp.float32)

    def edges(n, carry):
        p = pl.multiple_of(g.at(-1, -8) + n * 8, 8)
        j = (n + g.tiles - 1) // g.tiles - 2
        row = (j + 2) * N_ROW
        sl, az, ak, keep = [row_ref[row + i] for i in (SL, AZ, AK, KEEP)]
        sh_below = row_ref[jnp.maximum(row - N_ROW, 0) + SH]
        shell, lo, hi = rc[INV_SHELL], rc[LO], rc[HI]
        c5, c6, c7 = load(cs, 5, p), load(cs, 6, p), load(cs, 7, p)
        rb = ak * (c6 - load(cs, 6, p - 1)) + (1.0 / g.dth) * (load(cs, 7, p - w) - c7)
        put(ef, 0, p, (0.25 * g.dt * g.dr) * shell * rb)
        q6 = keep * c6 * shell
        zb = rc[INV_LO] * (sl * c5 - sh_below * load(cs, 5, p - w)) + prev_r(hi * q6, none) - lo * q6
        q7 = c7 * shell
        hq7 = hi * q7
        pb = rc[INV_LO] * az * (load(cs, 5, p - 1) - c5) + lo * q7 - prev_r(hq7, none)
        zl = 2.0 * hi[1:2] * q6[1:2]
        plast = -2.0 * hq7[1:2]
        put(ef, 1, p, (0.25 * g.dt) * (zb + next_r(zb, zl)))
        put(ef, 2, p, (0.25 * g.dt) * (pb + next_r(pb, plast)))
        zf[0, pl.ds(p, 8), :] = (0.25 * g.dt) * zb[0]
        zf[1, pl.ds(p, 8), :] = (0.25 * g.dt) * pb[0]
        return carry

    lax.fori_loop(0, (rows + 3) * g.tiles + 1, edges, 0)

    for f in range(11):
        for t in range(g.tiles):
            put(ft, f, t * 8, zero)
        for t in range(2):
            put(fp, f, t * 8, zero)

    def face_pull(halves, state, state2, speed, speed2, closed=None):
        total = 0.5 * (speed + speed2)
        inv = lax.rsqrt(total)
        a = total * inv
        if closed is not None:
            a = a * closed
        dot = halves[0] * (state2[0] - state[0])
        for c in range(1, 5):
            dot = dot + halves[c] * (state2[c] - state[c])
        return halves + [a * x for x in halves] + [-0.25 * inv * dot]

    def pull(n, carry):
        p = pl.multiple_of(g.at(-1, -8) + n * 8, 8)
        j = n // g.tiles - 1
        slot = pl.multiple_of(lax.rem(n + g.tiles - 1, g.tiles) * 8, 8)
        row = (j + 2) * N_ROW
        sh, az, cot = [row_ref[row + i] for i in (SH, AZ, COT)]
        sl_above = row_ref[row + N_ROW + SL]
        state = [load(us, c, p) for c in range(5)]
        cc = [load(cs, c, p) for c in range(5)]
        kd = rc[HALF_KV]
        sides = []
        up = kd * sl_above
        down = kd * sh
        pw = pl.multiple_of(p + jnp.where(n > (rows + 1) * g.tiles, 0, w), 8)
        high = face_pull(
            [up * load(cs, c, pw) - down * cc[c] for c in range(5)],
            state,
            [load(us, c, pw) for c in range(5)],
            load(cf, 7, p),
            load(cf, 7, pw),
        )
        low = [load(ft, f, slot) for f in range(11)]
        for f in range(11):
            put(ft, f, slot, high[f])
        sides.append((high, low))
        kaz = kd * az
        high_p = face_pull(
            [kaz * (load(cs, c, p + 1) - cc[c]) for c in range(5)],
            state,
            [load(us, c, p + 1) for c in range(5)],
            load(cf, 8, p),
            load(cf, 8, p + 1),
        )
        for f in range(11):
            put(fp, f, 8, high_p[f])
        per_volume = [rc[INV_V] * x for x in cc]
        half_hi = rc[HALF_HI2]
        speed = load(cf, 6, p)
        high_r = face_pull(
            [half_hi * (next_r(x, none) - x) for x in per_volume],
            state,
            [next_r(x) for x in state],
            speed,
            next_r(speed),
            rc[OPEN],
        )
        first = [rc[HALF_LO2][0:1] * x[0:1] for x in per_volume]
        low_r = [prev_r(high_r[f], first[f] if f < 5 else none) for f in range(11)]
        low_p = [load(fp, f, 7) for f in range(11)]
        for f in range(11):
            fp[f, :, 7:8, :] = fp[f, :, 15:16, :]
        sides.append((high_p, low_p))
        ft_, fp_ = [[hi_[c] + lo_[c] for c in range(5)] for hi_, lo_ in sides]
        fr_ = [rc[TOP] * high_r[c] + low_r[c] for c in range(5)]
        both = [(high_r, low_r)] + sides
        ub = []
        for c in range(5):
            ub.append(
                cc[c]
                + (both[0][0][5 + c] - both[0][1][5 + c])
                + (both[1][0][5 + c] - both[1][1][5 + c])
                + (both[2][0][5 + c] - both[2][1][5 + c])
            )
        sb = [hi_[10] + lo_[10] for hi_, lo_ in both]
        mid = rc[INV_MID] * g.dt
        w1, w2, w3 = cc[1] * mid, cc[2] * mid, cc[3] * mid
        s00, s11 = fr_[1], ft_[2] + w1
        s22 = fp_[3] + w1 + cot * w2
        s01 = fr_[2] + ft_[1] - w2
        s02 = fr_[3] + fp_[1] - w3
        s12 = ft_[3] + fp_[2] - cot * w3
        e0 = load(ef, 0, p) + load(ef, 0, p + 1) + load(ef, 0, p + w) + load(ef, 0, p + w + 1)
        e2 = load(ef, 1, p) + load(ef, 1, p + w)
        e1 = load(ef, 2, p) + load(ef, 2, p + 1)
        v = [load(cf, d, p) for d in range(3)]
        b = [load(cf, 3 + d, p) for d in range(3)]
        h, q = load(cf, 9, p), load(cf, 10, p)
        gg = (fr_[4], ft_[4], fp_[4])
        flow = v[0] * gg[0] + v[1] * gg[1] + v[2] * gg[2]
        beta = b[0] * gg[0] + b[1] * gg[1] + b[2] * gg[2]
        vb = v[0] * b[0] + v[1] * b[1] + v[2] * b[2]
        d00, d11, d22 = s00 + s00, s11 + s11, s22 + s22
        sv = (
            d00 * v[0] + s01 * v[1] + s02 * v[2],
            s01 * v[0] + d11 * v[1] + s12 * v[2],
            s02 * v[0] + s12 * v[1] + d22 * v[2],
        )
        sbm = (
            d00 * b[0] + s01 * b[1] + s02 * b[2],
            s01 * b[0] + d11 * b[1] + s12 * b[2],
            s02 * b[0] + s12 * b[1] + d22 * b[2],
        )
        c2b = sb[0] + sb[1] + sb[2]
        ptb = s00 + s11 + s22 + flow
        pb = c2b * load(cf, 11, p) + ptb
        pg = G1 * pb
        bbb = 2.0 * (c2b * q) + ptb - pg
        bxe = (b[1] * e2 - b[2] * e1, b[2] * e0 - b[0] * e2, b[0] * e1 - b[1] * e0)
        exv = (e1 * v[2] - e2 * v[1], e2 * v[0] - e0 * v[2], e0 * v[1] - e1 * v[0])
        rho_bar = ub[0] - c2b * load(cf, 12, p)
        m_bar, b_bar = [], []
        for d in range(3):
            vbar = h * gg[d] - beta * b[d] + 2.0 * (v[d] * sb[d]) - bxe[d]
            turn = q * vbar - pg * v[d]
            f0 = (fr_[0], ft_[0], fp_[0])[d]
            m_bar.append(ub[1 + d] + f0 + sv[d] + turn)
            rho_bar = rho_bar - v[d] * (0.5 * sv[d] + turn + 0.5 * (pg * v[d]))
            b_bar.append(b[d] * bbb - sbm[d] - vb * gg[d] - beta * v[d] - exv[d])
        e_bar = ub[4] + flow + pg

        first_lane = lax.broadcasted_iota(jnp.int32, (1, 8, LANES), 2) == 0
        v, b = [[x[0:1] for x in y] for y in (v, b)]
        q, h = q[0:1], h[0:1]
        bg = load(us, 5, p)[0:1]
        h = h + (1.0 - 0.5 * GAMMA) * (bg * bg - b[0] * b[0])
        vbg = vb[0:1] + v[0] * (bg - b[0])
        s00, s01, s02, g0 = first[1], first[2], first[3], first[4]
        e2 = (zf[0, pl.ds(p, 8), :] + zf[0, pl.ds(p + w, 8), :])[None]
        e1 = (zf[1, pl.ds(p, 8), :] + zf[1, pl.ds(p + 1, 8), :])[None]
        flow = v[0] * g0
        beta = bg * g0
        pb = s00 + flow
        pg = G1 * pb
        bbb = pb - pg
        d00 = s00 + s00
        sv = (d00 * v[0] + s01 * v[1] + s02 * v[2], s01 * v[0], s02 * v[0])
        sbm = (d00 * bg + s01 * b[1] + s02 * b[2], s01 * bg, s02 * bg)
        vbar = (
            h * g0 - beta * bg - (b[1] * e2 - b[2] * e1),
            bg * e2 - beta * b[1],
            -(beta * b[2]) - bg * e1,
        )
        exv = (e1 * v[2] - e2 * v[1], e2 * v[0], -(e1 * v[0]))
        more = [None] * 8
        rho_more = none
        for d in range(3):
            turn = q * vbar[d] - pg * v[d]
            more[1 + d] = sv[d] + turn + (first[0] if d == 0 else 0.0)
            rho_more = rho_more - v[d] * (0.5 * sv[d] + turn + 0.5 * (pg * v[d]))
            bd = bg if d == 0 else b[d]
            more[5 + d] = bd * bbb - sbm[d] - beta * v[d] - exv[d]
        more[5] = more[5] - vbg * g0
        more[0] = rho_more
        more[4] = flow + pg

        def with_first(x, extra):
            return x + jnp.concatenate([jnp.where(first_lane, extra, 0.0), none], 0)

        put(us, 0, p, with_first(rho_bar, more[0]))
        for d in range(3):
            put(us, 1 + d, p, with_first(m_bar[d], more[1 + d]))
        put(us, 4, p, with_first(e_bar, more[4]))
        put(us, 5, p, load(cs, 5, p) + 0.5 * (rc[TOP] * b_bar[0] + prev_r(b_bar[0], 2.0 * more[5])))
        put(us, 6, p, with_first(b_bar[1], more[6]))
        put(us, 7, p, with_first(b_bar[2], more[7]))
        return carry

    lax.fori_loop(0, (rows + 2) * g.tiles + 1, pull, 0)

    def keep_of(j):
        return 0.5 * row_ref[(j + 2) * N_ROW + KEEP]

    def tile6(j, p):
        return keep_of(j) * (load(us, 6, p) + load(us, 6, p - w))

    def tile7(p):
        return 0.5 * (load(us, 7, p) + load(us, 7, p - 1))

    def join(x):
        return jnp.concatenate([x[0], x[1]], 1)

    def line_of(c, j, k):
        p = g.at(j, k)
        if c < 6:
            return get_line(us, c, p)
        if c == 6:
            here = get_line(us, 6, p)
            if isinstance(j, int) and j == -1:
                return keep_of(j) * here
            return keep_of(j) * (here + get_line(us, 6, p - w))
        here = get_line(us, 7, p)
        return 0.5 * here if k == -1 else 0.5 * (here + get_line(us, 7, p - 1))

    def give(j, carry):
        for t in range(cols // 8):
            p = g.at(j, t * 8)
            at = (j, slice(t * 8, t * 8 + 8))
            for c in range(6):
                out[(c,) + at] = join(load(us, c, p))
            out[(6,) + at] = join(load(cs, 6, p) + tile6(j, p))
            out[(7,) + at] = join(load(cs, 7, p) + tile7(p))
        for c in range(8):
            gphlo[c, pl.ds(j, 1), :] = line_of(c, j, -1)
            gphhi[c, pl.ds(j, 1), :] = line_of(c, j, cols)
        gphhi[8, pl.ds(j, 1), :] = 0.5 * get_line(us, 7, g.at(j, cols))
        return carry

    lax.fori_loop(0, rows, give, 0)

    for ref, j in ((gthlo, -1), (gthhi, rows)):
        for t in range(cols // 8):
            p = g.at(j, t * 8)
            at = slice(t * 8, t * 8 + 8)
            for c in range(6):
                ref[c, at] = join(load(us, c, p))
            ref[6, at] = join(keep_of(j) * load(us, 6, p) if j < 0 else tile6(j, p))
            ref[7, at] = join(tile7(p))
            ref[8, at] = jnp.zeros((8, 2 * LANES), jnp.float32) if j < 0 else join(keep_of(j + 1) * load(us, 6, p))
        ref[9] = jnp.zeros((cols, 2 * LANES), jnp.float32)
        for k, base in ((-1, 0), (cols, 9)):
            for c in range(8):
                ref[9, base + c : base + c + 1] = line_of(c, j, k)
            if j > 0:
                ref[9, base + 8 : base + 9] = keep_of(j + 1) * get_line(us, 6, g.at(j, k))
        ref[9, 18:19] = 0.5 * get_line(us, 7, g.at(j, cols))


def call(kernel, outs, scratch, n_in, flops, interpret=False):
    vmem = pl.BlockSpec(memory_space=pltpu.VMEM)
    return pl.pallas_call(
        kernel,
        out_shape=[jax.ShapeDtypeStruct(s, jnp.float32) for s in outs],
        in_specs=[pl.BlockSpec(memory_space=pltpu.SMEM)] + [vmem] * n_in,
        out_specs=[vmem] * len(outs),
        scratch_shapes=[pltpu.VMEM(s, jnp.float32) for s in scratch],
        compiler_params=pltpu.CompilerParams(vmem_limit_bytes=62 << 20),
        cost_estimate=pl.CostEstimate(flops=flops, bytes_accessed=16 << 20, transcendentals=0),
        interpret=interpret,
    )


def forward(g, table, own, halos, planes, interpret=False):
    n = g.slots
    shape = (8, g.rows, g.cols, g.rads)
    scratch = [(8, 2, n, LANES), (15, 2, n, LANES), (6, n, LANES), (10, 2, n, LANES)]
    run = call(functools.partial(forward_kernel, g), [shape], scratch, 6, 10**8, interpret)
    return run(table, own, *halos, planes)[0]


def adjoint(g, table, own, halos, cot, planes, interpret=False):
    n = g.slots
    shape = (8, g.rows, g.cols, g.rads)
    outs = [shape, (8, g.rows, g.rads), (9, g.rows, g.rads), (10, g.cols, g.rads), (10, g.cols, g.rads)]
    scratch = [
        (8, 2, n, LANES),
        (8, 2, n, LANES),
        (13, 2, n, LANES),
        (3, 2, n, LANES),
        (2, n, LANES),
        (11, 2, g.width, LANES),
        (11, 2, 16, LANES),
    ]
    run = call(functools.partial(adjoint_kernel, g), outs, scratch, 7, 3 * 10**8, interpret)
    return run(table, own, *halos, cot, planes)


class Place:
    def __init__(self):
        self.n_th, self.n_ph = lax.axis_size("th"), lax.axis_size("ph")
        n_th, n_ph = self.n_th, self.n_ph
        half = n_ph // 2
        self.th, self.ph = lax.axis_index("th"), lax.axis_index("ph")
        self.at_bottom, self.at_top = self.th == 0, self.th == n_th - 1
        self.near = self.ph < half
        self.right = [(i, (i + 1) % n_ph) for i in range(n_ph)]
        self.left = [(j, i) for i, j in self.right]
        self.round = []
        for t in range(n_th):
            for p in range(half):
                self.round.append((t * n_ph + p, (t + 1) * n_ph + p if t < n_th - 1 else t * n_ph + p + half))
                self.round.append((t * n_ph + p + half, (t - 1) * n_ph + p + half if t > 0 else p))
        self.back = [(j, i) for i, j in self.round]

    def polar_exchange(self, low, high):
        ahead = lax.ppermute(jnp.where(self.near, high, low), ("th", "ph"), self.round)
        behind = lax.ppermute(jnp.where(self.near, low, high), ("th", "ph"), self.back)
        return jnp.where(self.near, ahead, behind), jnp.where(self.near, behind, ahead)


def flipped(rows, signs=FLIPS):
    return rows * jnp.array(signs, jnp.float32).reshape((-1,) + (1,) * (rows.ndim - 1))


def halos_of(place, state):
    rows, cols, rads = state.shape[1:]
    last = state[:, :, cols - 1]
    first = jnp.concatenate([state[:, :, 0], state[7:8, :, 1]], 0)
    phlo = lax.ppermute(last, "ph", place.right)
    phhi = lax.ppermute(first, "ph", place.left)

    def row_set(j, jface):
        plane = [phlo[:, j], phlo[6:7, jface], phhi[:8, j], phhi[6:7, jface], phhi[8:9, j], jnp.zeros((cols - 19, rads), jnp.float32)]
        return jnp.concatenate([state[:, j], state[6:7, jface], jnp.concatenate(plane, 0)[None]], 0)

    def corner_signs(s):
        return np.array(s + s + (-1.0,) + (1.0,) * (cols - 19), np.float32)[:, None]

    nine = FLIPS + (-1.0,)
    low = row_set(0, 1)
    high = row_set(rows - 1, rows - 1)

    def across(pack, bottom):
        body, plane = flipped(pack[:9], nine), pack[9] * corner_signs(nine)
        if bottom:
            body = jnp.concatenate([body[:6], body[8:9], body[7:]], 0)
            plane = jnp.concatenate([plane[:6], plane[8:9], plane[7:15], plane[17:18], plane[16:]], 0)
        return jnp.concatenate([body, plane[None]], 0)

    low = jnp.where(place.at_bottom, across(row_set(0, 2), True), low)
    high = jnp.where(place.at_top, across(high, False), high)
    thlo, thhi = place.polar_exchange(low, high)
    return phlo, phhi, thlo, thhi


def fold(place, parts):
    cot, gphlo, gphhi, gthlo, gthhi = parts
    rows, cols = cot.shape[1:3]
    body = gthlo[:9]
    plane = gthlo[9]
    body_b = jnp.concatenate([flipped(body[:6], FLIPS[:6]), 0.0 * body[6:7], -body[7:8], -body[6:7]], 0)
    signs6 = np.array(FLIPS[:6], np.float32)[:, None]

    def corner_b(x):
        return [x[:6] * signs6, 0.0 * x[6:7], -x[7:8], -x[6:7]]

    plane_b = jnp.concatenate(corner_b(plane[:9]) + corner_b(plane[9:18]) + [-plane[18:19], plane[19:]], 0)
    low = jnp.where(place.at_bottom, jnp.concatenate([body_b, plane_b[None]], 0), gthlo)
    body, plane = gthhi[:9], gthhi[9]
    body_t = jnp.concatenate([flipped(body[:6], FLIPS[:6]), -body[8:9], -body[7:8], 0.0 * body[8:9]], 0)

    def corner_t(x):
        return [x[:6] * signs6, -x[8:9], -x[7:8], 0.0 * x[8:9]]

    plane_t = jnp.concatenate(corner_t(plane[:9]) + corner_t(plane[9:18]) + [-plane[18:19], plane[19:]], 0)
    high = jnp.where(place.at_top, jnp.concatenate([body_t, plane_t[None]], 0), gthhi)
    from_low, from_high = place.polar_exchange(low, high)

    one = jnp.where(place.at_bottom, 0.0, 1.0)
    for got, j in ((from_low, 0), (from_high, rows - 1)):
        cot = cot.at[:, j].add(got[:8])
        plane = got[9]
        gphlo = gphlo.at[:, j].add(plane[:8])
        gphhi = gphhi.at[:, j].add(jnp.concatenate([plane[9:17], plane[18:19]], 0))
    for jface, share in ((1, one), (2, 1.0 - one)):
        cot = cot.at[6, jface].add(share * from_low[8])
        gphlo = gphlo.at[6, jface].add(share * from_low[9, 8])
        gphhi = gphhi.at[6, jface].add(share * from_low[9, 17])
    from_right = lax.ppermute(gphlo, "ph", place.left)
    from_left = lax.ppermute(gphhi, "ph", place.right)
    cot = cot.at[:, :, cols - 1].add(from_right)
    cot = cot.at[:, :, 0].add(from_left[:8])
    return cot.at[7, :, 1].add(from_left[8])


def shards(state, cotangent):
    place = Place()
    _, rows, cols, rads = state.shape
    g = Grid(rows, cols, rads, rows * place.n_th, cols * place.n_ph)
    table = lax.dynamic_slice_in_dim(jnp.asarray(g.row_table()), place.th * rows, rows + 5, 0).reshape(-1)
    planes = jnp.asarray(g.radial_planes())
    half_cot = 0.5 * cotangent
    halos_zero = halos_of(place, state)
    moved = forward(g, table, state, halos_zero, planes)
    halos_one = halos_of(place, moved)
    cot_one = fold(place, adjoint(g, table, moved, halos_one, half_cot, planes))
    last = fold(place, adjoint(g, table, state, halos_zero, cot_one, planes))
    return half_cot + last


def solution(mesh):
    placed = (P(None, "th", "ph", None), P(None, "th", "ph", None))
    return jax.shard_map(
        shards, mesh=mesh, in_specs=placed, out_specs=P(None, "th", "ph", None), check_vma=False
    )
```

```python
import functools
import math

import jax
import jax.numpy as jnp
import numpy as np
from jax import lax
from jax.experimental import pallas as pl
from jax.experimental.pallas import tpu as pltpu
from jax.sharding import PartitionSpec as P

GAMMA = 5.0 / 3.0
R_INNER = 1.0
R_OUTER = 3.0
COURANT = 0.4
SPEED_BOUND = 5.0
PRESSURE_SOFT = 0.05
THETA_CUT = 0.1

G1 = GAMMA - 1.0
LANES = 128
PAD = 32
FACE_SLOTS, PULL_SLOTS = 16, 16
FLIPS = (1.0, 1.0, -1.0, -1.0, 1.0, 1.0, -1.0, -1.0)
SH, SL, AZ, COT, AK, KEEP, N_ROW = 0, 1, 2, 3, 4, 5, 6
BOTTOM, TOP_END, NEAR = 0, 1, 2
INV_V, R_HI2, K_V, INV_MID, INV_LO, LO, HI, INV_SHELL, HALF_HI2, HALF_KV, HALF_LO2, TOP, OPEN = range(13)


class Grid:
    def __init__(self, rows, cols, rads, total_rows, total_cols):
        self.rows, self.cols, self.rads = rows, cols, rads
        self.width = cols + 8
        self.tiles = self.width // 8
        self.slots = PAD + (rows + 4) * self.width + PAD
        self.dth = (math.pi - 2.0 * THETA_CUT) / total_rows
        self.dph = 2.0 * math.pi / total_cols
        self.dr = (R_OUTER - R_INNER) / rads
        self.dt = COURANT * min(self.dr, R_INNER * math.sin(THETA_CUT) * self.dph) / SPEED_BOUND
        self.total_rows = total_rows

    def at(self, j, k):
        return PAD + (j + 2) * self.width + k

    def row_table(self):
        j = np.arange(-2, self.total_rows + 3, dtype=np.float64)
        low = THETA_CUT + j * self.dth
        high, mid = low + self.dth, low + 0.5 * self.dth
        drop = np.cos(low) - np.cos(high)
        keep = np.where((j == 0) | (j == self.total_rows), 0.0, 1.0)
        safe = np.where(np.abs(np.sin(low)) < 1e-6, 1.0, np.sin(low))
        table = np.zeros((len(j), N_ROW))
        table[:, SH] = np.sin(high) / drop
        table[:, SL] = np.sin(low) / drop
        table[:, AZ] = self.dth / (drop * self.dph)
        table[:, COT] = np.cos(mid) / np.sin(mid)
        table[:, AK] = keep / (safe * self.dph)
        table[:, KEEP] = keep
        return table.astype(np.float32)

    @property
    def flags(self):
        return (self.rows + 5) * N_ROW

    def radial_planes(self):
        i = np.arange(self.rads, dtype=np.float64)
        low = R_INNER + i * self.dr
        high, mid = low + self.dr, low + 0.5 * self.dr
        vol = (high**3 - low**3) / 3.0
        shell = 0.5 * (high**2 - low**2)
        top = np.where(i == self.rads - 1, 2.0, 1.0)
        planes = [None] * 13
        planes[INV_V] = 1.0 / vol
        planes[R_HI2] = high**2
        planes[K_V] = shell / vol
        planes[INV_MID] = 1.0 / mid
        planes[INV_LO] = 1.0 / low
        planes[LO] = low
        planes[HI] = high
        planes[INV_SHELL] = 1.0 / shell
        planes[HALF_HI2] = 0.5 * self.dt * high**2
        planes[HALF_KV] = 0.5 * self.dt * shell / vol
        planes[HALF_LO2] = 0.5 * self.dt * low**2
        planes[TOP] = top
        planes[OPEN] = 2.0 - top
        stack = np.stack(planes).astype(np.float32).reshape(13, 2, 1, LANES)
        return np.broadcast_to(stack, (13, 2, 8, LANES)).copy()


def lane_index(x):
    return lax.broadcasted_iota(jnp.int32, x.shape, 2)


def next_r(x, last=None):
    turned = pltpu.roll(x, LANES - 1, 2)
    end = x[1:2] if last is None else last
    return jnp.where(lane_index(x) == LANES - 1, jnp.concatenate([turned[1:2], end], 0), turned)


def prev_r(x, first):
    turned = pltpu.roll(x, 1, 2)
    return jnp.where(lane_index(x) == 0, jnp.concatenate([first, turned[0:1]], 0), turned)


def split(x):
    return jnp.stack([x[:, :LANES], x[:, LANES:]])


def load(ref, field, slot, size=8):
    return ref[field, :, pl.ds(slot, size), :]


def put(ref, field, slot, value):
    ref[field, :, pl.ds(slot, value.shape[1]), :] = value


def loader(size):
    return lambda ref, field, slot: load(ref, field, slot, size)


def planes_of(rc, size):
    return lambda i: jnp.concatenate([rc[i]] * (size // 8), 1)


def put_line(ref, field, slot, line):
    ref[field, 0, pl.ds(slot, 1), :] = line[:, :LANES]
    ref[field, 1, pl.ds(slot, 1), :] = line[:, LANES:]


def get_line(ref, field, slot):
    return jnp.concatenate([ref[field, 0, pl.ds(slot, 1), :], ref[field, 1, pl.ds(slot, 1), :]], 1)


def picker(g, row_ref, ahead, behind):
    near = row_ref[g.flags + NEAR] > 0.5

    def low(*at):
        return jnp.where(near, ahead[at], behind[at])

    def high(*at):
        return jnp.where(near, behind[at], ahead[at])

    return low, high


def row_copies(g, hbm, ref, sem):
    for j in range(g.rows):
        for h in range(2):
            yield pltpu.make_async_copy(
                hbm.at[:, j, :, pl.ds(h * LANES, LANES)], ref.at[:, h, pl.ds(g.at(j, 0), g.cols), :], sem.at[j, h]
            )


def fill_state(g, us, row_ref, own, sem, phlo, phhi, ahead, behind):
    rows, cols = g.rows, g.cols
    low, high = picker(g, row_ref, ahead, behind)
    calm = [jnp.full((2, 8, LANES), 1.0 if c == 0 else 0.0, jnp.float32) for c in range(8)]

    def keep(j):
        return row_ref[(j + 2) * N_ROW + KEEP]

    def ends(j, fetch):
        for c in range(8):
            scale = keep(j) if c == 6 else None
            for which, k in ((0, -1), (1, cols)):
                line = fetch(c, which)
                put_line(us, c, g.at(j, k), line if scale is None else line * scale)
        put_line(us, 7, g.at(j, cols + 1), fetch(7, 2))

    def body_row(j, side):
        for c in range(8):
            for t in range(cols // 8):
                x = split(side(c, slice(t * 8, t * 8 + 8)))
                put(us, c, g.at(j, t * 8), x * keep(j) if c == 6 else x)
            put(us, c, g.at(j, cols), calm[c])

    for c in range(8):
        put(us, c, g.at(-1, -8), calm[c])
    body_row(-1, low)
    ends(-1, lambda c, w: low(9, slice((c, 9 + c, 18)[w], (c, 9 + c, 18)[w] + 1)))

    def step(j, carry):
        for c in range(8):
            put(us, c, g.at(j, cols), calm[c])
        ends(j, lambda c, w: (phlo[c, pl.ds(j, 1), :], phhi[c, pl.ds(j, 1), :], phhi[8, pl.ds(j, 1), :])[w])
        return carry

    lax.fori_loop(0, rows, step, 0)
    body_row(rows, high)
    ends(rows, lambda c, w: high(9, slice((c, 9 + c, 18)[w], (c, 9 + c, 18)[w] + 1)))
    far = keep(rows + 1)
    for t in range(g.tiles):
        x = split(high(8, slice(t * 8, t * 8 + 8))) if t < cols // 8 else calm[1]
        put(us, 6, g.at(rows + 1, t * 8), x * far)
    put_line(us, 6, g.at(rows + 1, -1), high(9, slice(8, 9)) * far)
    put_line(us, 6, g.at(rows + 1, cols), high(9, slice(17, 18)) * far)
    for copy in row_copies(g, own, us, sem):
        copy.wait()
    for t in range(cols // 8):
        put(us, 6, g.at(0, t * 8), load(us, 6, g.at(0, t * 8)) * keep(0))


def cell_values(g, us, p, size):
    load = loader(size)
    rho, m0, m1, m2, energy, u5, u6, u7 = [load(us, c, p) for c in range(8)]
    b0 = 0.5 * (u5 + next_r(u5))
    b1 = 0.5 * (u6 + load(us, 6, p + g.width))
    b2 = 0.5 * (u7 + load(us, 7, p + 1))
    q = 1.0 / rho
    v0, v1, v2 = m0 * q, m1 * q, m2 * q
    square = b0 * b0 + b1 * b1 + b2 * b2
    pressure = G1 * (energy - 0.5 * (m0 * v0 + m1 * v1 + m2 * v2) - 0.5 * square)
    total = pressure + 0.5 * square
    soft = pressure * pressure + PRESSURE_SOFT * PRESSURE_SOFT
    inv_soft = lax.rsqrt(soft)
    c2 = (GAMMA * (soft * inv_soft) + square) * q
    return (m0, m1, m2), (v0, v1, v2), (b0, b1, b2), u5, q, pressure, total, energy + total, inv_soft, c2


def forward_kernel(
    g, row_ref, own, phlo, phhi, ahead, behind, rc, out, last_col, first_col, us, cf, gf, ff, stage, sem, sem_out
):
    for copy in row_copies(g, own, us, sem):
        copy.start()
    fill_state(g, us, row_ref, own, sem, phlo, phhi, ahead, behind)
    w = g.width
    wide = g.cols

    def cells(n, carry):
        p = pl.multiple_of(g.at(-1, -8) + n * wide, 8)
        m, v, b, u5, q, pressure, total, h, inv_soft, c2 = cell_values(g, us, p, wide)
        put(cf, 0, p, m[0] * v[0] - b[0] * b[0] + total)
        put(cf, 1, p, m[0] * v[1] - b[0] * b[1])
        put(cf, 2, p, m[0] * v[2] - b[0] * b[2])
        put(cf, 3, p, m[1] * v[1] - b[1] * b[1] + total)
        put(cf, 4, p, m[1] * v[2] - b[1] * b[2])
        put(cf, 5, p, m[2] * v[2] - b[2] * b[2] + total)
        vb = v[0] * b[0] + v[1] * b[1] + v[2] * b[2]
        for d in range(3):
            put(cf, 6 + d, p, h * v[d] - b[d] * vb)
            put(cf, 9 + d, p, v[d] * v[d] + c2)
        put(cf, 12, p, v[2] * b[1] - v[1] * b[2])
        put(cf, 13, p, v[0] * b[2] - v[2] * b[0])
        put(cf, 14, p, v[1] * b[0] - v[0] * b[1])
        m, v, b = [[x[0:1] for x in y] for y in (m, v, b)]
        bg = u5[0:1]
        gain = (1.0 - 0.5 * GAMMA) * (bg * bg - b[0] * b[0])
        vbg = vb[0:1] + v[0] * (bg - b[0])
        ghost = (
            m[0] * v[0] - bg * bg + total[0:1] + gain,
            m[0] * v[1] - bg * b[1],
            m[0] * v[2] - bg * b[2],
            (h[0:1] + gain) * v[0] - bg * vbg,
            v[0] * b[2] - v[2] * bg,
            v[1] * bg - v[0] * b[1],
        )
        for f, x in enumerate(ghost):
            gf[f, pl.ds(p, wide), :] = x[0]
        return carry

    lax.fori_loop(0, pl.cdiv((g.rows + 2) * g.width + 8, wide), cells, 0)

    index = ((0, 1, 2), (1, 3, 4), (2, 4, 5))

    def face(d, p, shift, size):
        load = loader(size)
        fluxes = [load(us, 1 + d, p)] + [load(cf, index[d][c], p) for c in range(3)] + [load(cf, 6 + d, p)]
        speed = load(cf, 9 + d, p)
        state = [load(us, c, p) for c in range(5)]
        if shift is None:
            other = [next_r(x) for x in fluxes]
            speed2 = next_r(speed)
            state2 = [other[0] if c == 1 else next_r(state[c]) for c in range(5)]
        else:
            r = p + shift
            other = [load(us, 1 + d, r)] + [load(cf, index[d][c], r) for c in range(3)] + [load(cf, 6 + d, r)]
            speed2 = load(cf, 9 + d, r)
            state2 = [load(us, c, r) for c in range(5)]
        total = 0.5 * (speed + speed2)
        half = 0.5 * (total * lax.rsqrt(total))
        return fluxes, [0.5 * (fluxes[c] + other[c]) - half * (state2[c] - state[c]) for c in range(5)]

    def faces(n, carry):
        p = pl.multiple_of(g.at(-1, 0) + n * FACE_SLOTS, 8)
        for d, shift, base in ((1, w, 0), (2, 1, 5)):
            _, flux = face(d, p, shift, FACE_SLOTS)
            for c in range(5):
                put(ff, base + c, p, flux[c])
        return carry

    lax.fori_loop(0, (g.rows + 1) * g.width // FACE_SLOTS, faces, 0)

    size = g.cols
    load = loader(size)
    plane = planes_of(rc, size)

    def leave(j):
        return pltpu.make_async_copy(stage.at[:, j], out.at[:, j], sem_out.at[j])

    def combine(j, carry):
        p = pl.multiple_of(g.at(j, 0), 8)
        row = (j + 2) * N_ROW
        sh, sl, az, cot, ak, keep = [row_ref[row + i] for i in range(N_ROW)]
        cells_here, flux_r = face(0, p, None, size)
        ghost = [load(us, 1, p)[0:1]] + [gf[f, pl.ds(p, size), :][None] for f in range(4)]
        inv_v, kv = plane(INV_V), plane(K_V)
        rates = []
        for c in range(5):
            high = plane(R_HI2) * flux_r[c]
            first = 0.5 * plane(HALF_LO2)[0:1] * (2.0 / g.dt) * (ghost[c] + cells_here[c][0:1])
            low = prev_r(high, first)
            th = sh * load(ff, c, p) - sl * load(ff, c, p - w)
            ph = az * (load(ff, 5 + c, p) - load(ff, 5 + c, p - 1))
            rates.append(-(inv_v * (high - low) + kv * (th + ph)))
        tt = [load(cf, f, p) for f in range(1, 6)]
        mid = plane(INV_MID)
        rates[1] = rates[1] + (tt[2] + tt[4]) * mid
        rates[2] = rates[2] + (cot * tt[4] - tt[0]) * mid
        rates[3] = rates[3] - (tt[1] + cot * tt[3]) * mid
        ep, ept = load(cf, 14, p), load(cf, 14, p + w)
        x0 = load(cf, 14, p - w) + ep
        x1 = ep + ept
        g_here = gf[5, pl.ds(p, size), :][None]
        x0m = prev_r(x0, gf[5, pl.ds(p - w, size), :][None] + g_here)
        x1m = prev_r(x1, g_here + gf[5, pl.ds(p + w, size), :][None])
        z0 = 0.25 * (x0 + x0m)
        zr = 0.25 * (next_r(x0) + x0)
        z1 = 0.25 * (x1 + x1m)
        et = load(cf, 13, p)
        y0 = load(cf, 13, p - 1) + et
        y1 = et + load(cf, 13, p + 1)
        g_here = gf[4, pl.ds(p, size), :][None]
        y0m = prev_r(y0, gf[4, pl.ds(p - 1, size), :][None] + g_here)
        y1m = prev_r(y1, g_here + gf[4, pl.ds(p + 1, size), :][None])
        p0 = 0.25 * (y0 + y0m)
        pr = 0.25 * (next_r(y0) + y0)
        p1 = 0.25 * (y1 + y1m)
        er, era, erb = load(cf, 12, p), load(cf, 12, p - 1), load(cf, 12, p - w)
        r0 = 0.25 * (er + era + erb + load(cf, 12, p - w - 1))
        r1 = 0.25 * (load(cf, 12, p + 1) + er + load(cf, 12, p - w + 1) + erb)
        rt = 0.25 * (load(cf, 12, p + w) + load(cf, 12, p + w - 1) + er + era)
        lo, hi, shell = plane(LO), plane(HI), plane(INV_SHELL)
        rates.append(-plane(INV_LO) * (sh * z1 - sl * z0 - az * (p1 - p0)))
        rates.append(-shell * (g.dr * ak * (r1 - r0) - keep * (hi * zr - lo * z0)))
        rates.append(shell * ((g.dr / g.dth) * (rt - r0) - (hi * pr - lo * p0)))
        for c in range(8):
            new = load(us, c, p) + g.dt * rates[c]
            stage[c, j] = jnp.concatenate([new[0], new[1]], 1)
        leave(j).start()
        for c in range(8):
            last_col[c, pl.ds(j, 1), :] = stage[c, j, g.cols - 1 : g.cols, :]
            first_col[c, pl.ds(j, 1), :] = stage[c, j, 0:1, :]
        first_col[8, pl.ds(j, 1), :] = stage[7, j, 1:2, :]
        return carry

    lax.fori_loop(0, g.rows, combine, 0)

    def settle(j, carry):
        leave(j).wait()
        return carry

    lax.fori_loop(0, g.rows, settle, 0)


def adjoint_kernel(g, received, row_ref, own, phlo, phhi, ahead, behind, cot, *refs):
    if received:
        back_ahead, back_behind, from_right, from_left = refs[:4]
        refs = refs[4:]
    rc, out, gphlo, gphhi, go_ahead, go_behind, us, cs, cf, ef, zf, ft, fp, stage, sem, sem_cot, sem_out = refs
    w, rows, cols = g.width, g.rows, g.cols
    load = loader(8)
    for copy in row_copies(g, own, us, sem):
        copy.start()
    for copy in row_copies(g, cot, cs, sem_cot):
        copy.start()
    zero = jnp.zeros((2, 8, LANES), jnp.float32)
    for j in (-2, -1, rows, rows + 1):
        for c in range(8):
            for t in range(g.tiles):
                put(cs, c, g.at(j, t * 8), zero)
    for c in range(8):
        put(cs, c, g.at(-2, -8), zero)

    def clear(j, carry):
        for c in range(8):
            put(cs, c, g.at(j, cols), zero)
        return carry

    lax.fori_loop(0, rows, clear, 0)
    fill_state(g, us, row_ref, own, sem, phlo, phhi, ahead, behind)
    for copy in row_copies(g, cot, cs, sem_cot):
        copy.wait()
    if received:
        low, high = picker(g, row_ref, back_ahead, back_behind)
        bottom = row_ref[g.flags + BOTTOM]

        def add_line(c, slot, line):
            put_line(cs, c, slot, get_line(cs, c, slot) + line)

        def columns(j, carry):
            for c in range(8):
                add_line(c, g.at(j, 0), from_left[c, pl.ds(j, 1), :])
                add_line(c, g.at(j, cols - 1), from_right[c, pl.ds(j, 1), :])
            add_line(7, g.at(j, 1), from_left[8, pl.ds(j, 1), :])
            return carry

        lax.fori_loop(0, rows, columns, 0)
        for t in range(cols // 8):
            at = slice(t * 8, t * 8 + 8)
            for c in range(8):
                p = g.at(0, t * 8)
                put(cs, c, p, load(cs, c, p) + split(low(c, at)))
                p = g.at(rows - 1, t * 8)
                put(cs, c, p, load(cs, c, p) + split(high(c, at)))
            for j, share in ((1, 1.0 - bottom), (2, bottom)):
                p = g.at(j, t * 8)
                put(cs, 6, p, load(cs, 6, p) + share * split(low(8, at)))

    def cells(n, carry):
        p = pl.multiple_of(g.at(-1, -8) + n * cols, 8)
        m, v, b, u5, q, pressure, total, h, inv_soft, c2 = cell_values(g, us, p, cols)
        for d in range(3):
            put(cf, d, p, v[d])
            put(cf, 3 + d, p, b[d])
            put(cf, 6 + d, p, v[d] * v[d] + c2)
        put(cf, 9, p, h)
        put(cf, 10, p, q)
        put(cf, 11, p, GAMMA * q * (pressure * inv_soft))
        put(cf, 12, p, c2 * q)
        return carry

    lax.fori_loop(0, pl.cdiv((rows + 2) * w + 8, cols), cells, 0)

    for f in range(3):
        put(ef, f, g.at(-1, -8), zero)
    for f in range(2):
        zf[f, pl.ds(g.at(-1, -8), 8), :] = zero[0]

    def edges(n, carry):
        load = loader(w)
        plane = planes_of(rc, w)
        none = jnp.zeros((1, w, LANES), jnp.float32)
        p = pl.multiple_of(g.at(-1, 0) + n * w, 8)
        j = n - 1
        row = (j + 2) * N_ROW
        sl, az, ak, keep = [row_ref[row + i] for i in (SL, AZ, AK, KEEP)]
        sh_below = row_ref[row - N_ROW + SH]
        shell, lo, hi = plane(INV_SHELL), plane(LO), plane(HI)
        c5, c6, c7 = load(cs, 5, p), load(cs, 6, p), load(cs, 7, p)
        rb = ak * (c6 - load(cs, 6, p - 1)) + (1.0 / g.dth) * (load(cs, 7, p - w) - c7)
        put(ef, 0, p, (0.25 * g.dt * g.dr) * shell * rb)
        q6 = keep * c6 * shell
        zb = plane(INV_LO) * (sl * c5 - sh_below * load(cs, 5, p - w)) + prev_r(hi * q6, none) - lo * q6
        q7 = c7 * shell
        hq7 = hi * q7
        pb = plane(INV_LO) * az * (load(cs, 5, p - 1) - c5) + lo * q7 - prev_r(hq7, none)
        zl = 2.0 * hi[1:2] * q6[1:2]
        plast = -2.0 * hq7[1:2]
        put(ef, 1, p, (0.25 * g.dt) * (zb + next_r(zb, zl)))
        put(ef, 2, p, (0.25 * g.dt) * (pb + next_r(pb, plast)))
        zf[0, pl.ds(p, w), :] = (0.25 * g.dt) * zb[0]
        zf[1, pl.ds(p, w), :] = (0.25 * g.dt) * pb[0]
        return carry

    lax.fori_loop(0, rows + 3, edges, 0)

    size = PULL_SLOTS
    load = loader(size)
    plane = planes_of(rc, size)
    none = jnp.zeros((1, size, LANES), jnp.float32)
    groups = w // size
    for f in range(11):
        for t in range(g.tiles):
            put(ft, f, t * 8, zero)
        put(fp, f, 0, zero)

    def face_pull(halves, state, state2, speed, speed2, closed=None):
        total = 0.5 * (speed + speed2)
        inv = lax.rsqrt(total)
        a = total * inv
        if closed is not None:
            a = a * closed
        dot = halves[0] * (state2[0] - state[0])
        for c in range(1, 5):
            dot = dot + halves[c] * (state2[c] - state[c])
        return halves + [a * x for x in halves] + [-0.25 * inv * dot]

    def pull(n, carry):
        p = pl.multiple_of(g.at(-1, -8) + n * size, 8)
        j = n // groups - 1
        slot = pl.multiple_of(lax.rem(n, groups) * size, 8)
        row = (j + 2) * N_ROW
        sh, az, cot = [row_ref[row + i] for i in (SH, AZ, COT)]
        sl_above = row_ref[row + N_ROW + SL]
        state = [load(us, c, p) for c in range(5)]
        cc = [load(cs, c, p) for c in range(5)]
        kd = plane(HALF_KV)
        sides = []
        up = kd * sl_above
        down = kd * sh
        pw = pl.multiple_of(p + jnp.where(n >= (rows + 1) * groups, 0, w), 8)
        high = face_pull(
            [up * load(cs, c, pw) - down * cc[c] for c in range(5)],
            state,
            [load(us, c, pw) for c in range(5)],
            load(cf, 7, p),
            load(cf, 7, pw),
        )
        low = [load(ft, f, slot) for f in range(11)]
        for f in range(11):
            put(ft, f, slot, high[f])
        sides.append((high, low))
        kaz = kd * az
        high_p = face_pull(
            [kaz * (load(cs, c, p + 1) - cc[c]) for c in range(5)],
            state,
            [load(us, c, p + 1) for c in range(5)],
            load(cf, 8, p),
            load(cf, 8, p + 1),
        )
        for f in range(11):
            put(fp, f, 8, high_p[f])
        per_volume = [plane(INV_V) * x for x in cc]
        half_hi = plane(HALF_HI2)
        speed = load(cf, 6, p)
        high_r = face_pull(
            [half_hi * (next_r(x, none) - x) for x in per_volume],
            state,
            [next_r(x) for x in state],
            speed,
            next_r(speed),
            plane(OPEN),
        )
        first = [plane(HALF_LO2)[0:1] * x[0:1] for x in per_volume]
        low_r = [prev_r(high_r[f], first[f] if f < 5 else none) for f in range(11)]
        low_p = [load(fp, f, 7) for f in range(11)]
        for f in range(11):
            fp[f, :, 7:8, :] = fp[f, :, size + 7 : size + 8, :]
        sides.append((high_p, low_p))
        ft_, fp_ = [[hi_[c] + lo_[c] for c in range(5)] for hi_, lo_ in sides]
        fr_ = [plane(TOP) * high_r[c] + low_r[c] for c in range(5)]
        both = [(high_r, low_r)] + sides
        ub = []
        for c in range(5):
            ub.append(
                cc[c]
                + (both[0][0][5 + c] - both[0][1][5 + c])
                + (both[1][0][5 + c] - both[1][1][5 + c])
                + (both[2][0][5 + c] - both[2][1][5 + c])
            )
        sb = [hi_[10] + lo_[10] for hi_, lo_ in both]
        mid = plane(INV_MID) * g.dt
        w1, w2, w3 = cc[1] * mid, cc[2] * mid, cc[3] * mid
        s00, s11 = fr_[1], ft_[2] + w1
        s22 = fp_[3] + w1 + cot * w2
        s01 = fr_[2] + ft_[1] - w2
        s02 = fr_[3] + fp_[1] - w3
        s12 = ft_[3] + fp_[2] - cot * w3
        e0 = load(ef, 0, p) + load(ef, 0, p + 1) + load(ef, 0, p + w) + load(ef, 0, p + w + 1)
        e2 = load(ef, 1, p) + load(ef, 1, p + w)
        e1 = load(ef, 2, p) + load(ef, 2, p + 1)
        v = [load(cf, d, p) for d in range(3)]
        b = [load(cf, 3 + d, p) for d in range(3)]
        h, q = load(cf, 9, p), load(cf, 10, p)
        gg = (fr_[4], ft_[4], fp_[4])
        flow = v[0] * gg[0] + v[1] * gg[1] + v[2] * gg[2]
        beta = b[0] * gg[0] + b[1] * gg[1] + b[2] * gg[2]
        vb = v[0] * b[0] + v[1] * b[1] + v[2] * b[2]
        d00, d11, d22 = s00 + s00, s11 + s11, s22 + s22
        sv = (
            d00 * v[0] + s01 * v[1] + s02 * v[2],
            s01 * v[0] + d11 * v[1] + s12 * v[2],
            s02 * v[0] + s12 * v[1] + d22 * v[2],
        )
        sbm = (
            d00 * b[0] + s01 * b[1] + s02 * b[2],
            s01 * b[0] + d11 * b[1] + s12 * b[2],
            s02 * b[0] + s12 * b[1] + d22 * b[2],
        )
        c2b = sb[0] + sb[1] + sb[2]
        ptb = s00 + s11 + s22 + flow
        pb = c2b * load(cf, 11, p) + ptb
        pg = G1 * pb
        bbb = 2.0 * (c2b * q) + ptb - pg
        bxe = (b[1] * e2 - b[2] * e1, b[2] * e0 - b[0] * e2, b[0] * e1 - b[1] * e0)
        exv = (e1 * v[2] - e2 * v[1], e2 * v[0] - e0 * v[2], e0 * v[1] - e1 * v[0])
        rho_bar = ub[0] - c2b * load(cf, 12, p)
        m_bar, b_bar = [], []
        for d in range(3):
            vbar = h * gg[d] - beta * b[d] + 2.0 * (v[d] * sb[d]) - bxe[d]
            turn = q * vbar - pg * v[d]
            f0 = (fr_[0], ft_[0], fp_[0])[d]
            m_bar.append(ub[1 + d] + f0 + sv[d] + turn)
            rho_bar = rho_bar - v[d] * (0.5 * sv[d] + turn + 0.5 * (pg * v[d]))
            b_bar.append(b[d] * bbb - sbm[d] - vb * gg[d] - beta * v[d] - exv[d])
        e_bar = ub[4] + flow + pg

        first_lane = lax.broadcasted_iota(jnp.int32, (1, size, LANES), 2) == 0
        v, b = [[x[0:1] for x in y] for y in (v, b)]
        q, h = q[0:1], h[0:1]
        bg = load(us, 5, p)[0:1]
        h = h + (1.0 - 0.5 * GAMMA) * (bg * bg - b[0] * b[0])
        vbg = vb[0:1] + v[0] * (bg - b[0])
        s00, s01, s02, g0 = first[1], first[2], first[3], first[4]
        e2 = (zf[0, pl.ds(p, size), :] + zf[0, pl.ds(p + w, size), :])[None]
        e1 = (zf[1, pl.ds(p, size), :] + zf[1, pl.ds(p + 1, size), :])[None]
        flow = v[0] * g0
        beta = bg * g0
        pb = s00 + flow
        pg = G1 * pb
        bbb = pb - pg
        d00 = s00 + s00
        sv = (d00 * v[0] + s01 * v[1] + s02 * v[2], s01 * v[0], s02 * v[0])
        sbm = (d00 * bg + s01 * b[1] + s02 * b[2], s01 * bg, s02 * bg)
        vbar = (
            h * g0 - beta * bg - (b[1] * e2 - b[2] * e1),
            bg * e2 - beta * b[1],
            -(beta * b[2]) - bg * e1,
        )
        exv = (e1 * v[2] - e2 * v[1], e2 * v[0], -(e1 * v[0]))
        more = [None] * 8
        rho_more = none
        for d in range(3):
            turn = q * vbar[d] - pg * v[d]
            more[1 + d] = sv[d] + turn + (first[0] if d == 0 else 0.0)
            rho_more = rho_more - v[d] * (0.5 * sv[d] + turn + 0.5 * (pg * v[d]))
            bd = bg if d == 0 else b[d]
            more[5 + d] = bd * bbb - sbm[d] - beta * v[d] - exv[d]
        more[5] = more[5] - vbg * g0
        more[0] = rho_more
        more[4] = flow + pg

        def with_first(x, extra):
            return x + jnp.concatenate([jnp.where(first_lane, extra, 0.0), none], 0)

        put(us, 0, p, with_first(rho_bar, more[0]))
        for d in range(3):
            put(us, 1 + d, p, with_first(m_bar[d], more[1 + d]))
        put(us, 4, p, with_first(e_bar, more[4]))
        put(us, 5, p, load(cs, 5, p) + 0.5 * (plane(TOP) * b_bar[0] + prev_r(b_bar[0], 2.0 * more[5])))
        put(us, 6, p, with_first(b_bar[1], more[6]))
        put(us, 7, p, with_first(b_bar[2], more[7]))
        return carry

    lax.fori_loop(0, (rows + 2) * groups + 1, pull, 0)
    load = loader(8)

    def keep_of(j):
        return 0.5 * row_ref[(j + 2) * N_ROW + KEEP]

    def tile6(j, p):
        return keep_of(j) * (load(us, 6, p) + load(us, 6, p - w))

    def tile7(p):
        return 0.5 * (load(us, 7, p) + load(us, 7, p - 1))

    def join(x):
        return jnp.concatenate([x[0], x[1]], 1)

    def line_of(c, j, k):
        p = g.at(j, k)
        if c < 6:
            return get_line(us, c, p)
        if c == 6:
            here = get_line(us, 6, p)
            if isinstance(j, int) and j == -1:
                return keep_of(j) * here
            return keep_of(j) * (here + get_line(us, 6, p - w))
        here = get_line(us, 7, p)
        return 0.5 * here if k == -1 else 0.5 * (here + get_line(us, 7, p - 1))

    def leave(j):
        return pltpu.make_async_copy(stage.at[:, j], out.at[:, j], sem_out.at[j])

    def give(j, carry):
        for t in range(cols // 8):
            p = g.at(j, t * 8)
            at = (j, slice(t * 8, t * 8 + 8))
            for c in range(6):
                stage[(c,) + at] = join(load(us, c, p))
            stage[(6,) + at] = join(load(cs, 6, p) + tile6(j, p))
            stage[(7,) + at] = join(load(cs, 7, p) + tile7(p))
        leave(j).start()
        for c in range(8):
            gphlo[c, pl.ds(j, 1), :] = line_of(c, j, -1)
            gphhi[c, pl.ds(j, 1), :] = line_of(c, j, cols)
        gphhi[8, pl.ds(j, 1), :] = 0.5 * get_line(us, 7, g.at(j, cols))
        return carry

    lax.fori_loop(0, rows, give, 0)

    bottom, top = row_ref[g.flags + BOTTOM], row_ref[g.flags + TOP_END]
    near = row_ref[g.flags + NEAR] > 0.5

    def toward_low(of):
        signs = [1.0 if f > 0 else 1.0 - 2.0 * bottom for f in FLIPS]
        face = of(6)
        return [of(c) * signs[c] for c in range(6)] + [face * (1.0 - bottom), of(7) * signs[7], face * -bottom]

    def toward_high(of, far):
        signs = [1.0 if f > 0 else 1.0 - 2.0 * top for f in FLIPS]
        face = of(6) * (1.0 - top) - far * top
        return [of(c) * signs[c] for c in range(6)] + [face, of(7) * signs[7], far * (1.0 - top)]

    def send(at, low_value, high_value):
        go_ahead[at] = jnp.where(near, high_value, low_value)
        go_behind[at] = jnp.where(near, low_value, high_value)

    for t in range(cols // 8):
        p0, p1 = g.at(-1, t * 8), g.at(rows, t * 8)

        def tile_low(c):
            if c == 6:
                return join(keep_of(-1) * load(us, 6, p0))
            return join(load(us, c, p0) if c < 6 else tile7(p0))

        def tile_high(c):
            return join(load(us, c, p1) if c < 6 else tile6(rows, p1) if c == 6 else tile7(p1))

        lows = toward_low(tile_low)
        highs = toward_high(tile_high, join(keep_of(rows + 1) * load(us, 6, p1)))
        for c in range(9):
            send((c, slice(t * 8, t * 8 + 8)), lows[c], highs[c])
    for k, base in ((-1, 0), (cols, 9)):
        lows = toward_low(lambda c: line_of(c, -1, k))
        highs = toward_high(lambda c: line_of(c, rows, k), keep_of(rows + 1) * get_line(us, 6, g.at(rows, k)))
        for c in range(9):
            send((9, slice(base + c, base + c + 1)), lows[c], highs[c])
    send(
        (9, slice(18, 19)),
        (0.5 - bottom) * get_line(us, 7, g.at(-1, cols)),
        (0.5 - top) * get_line(us, 7, g.at(rows, cols)),
    )

    def settle(j, carry):
        leave(j).wait()
        return carry

    lax.fori_loop(0, rows, settle, 0)


def pack_kernel(g, row_ref, state, phlo, phhi, go_ahead, go_behind, edge, sem):
    rows, cols = g.rows, g.cols
    copies = [
        pltpu.make_async_copy(state.at[:, pl.ds(j0, n)], edge.at[:, pl.ds(e0, n)], sem.at[i])
        for i, (j0, n, e0) in enumerate(((0, 3, 0), (rows - 1, 1, 3)))
    ]
    for copy in copies:
        copy.start()
    bottom, top = row_ref[g.flags + BOTTOM], row_ref[g.flags + TOP_END]
    near = row_ref[g.flags + NEAR] > 0.5

    def nine(of, low):
        pole = bottom if low else top
        signs = [1.0 if f > 0 else 1.0 - 2.0 * pole for f in FLIPS]
        j = 0 if low else rows - 1
        values = [of(c, j) * signs[c] for c in range(8)]
        if low:
            values[6] = of(6, 0) * (1.0 - bottom) - of(6, 2) * bottom
            return values + [of(6, 1)]
        return values + [-of(6, rows - 1)]

    def send(at, low_value, high_value):
        go_ahead[at] = jnp.where(near, high_value, low_value)
        go_behind[at] = jnp.where(near, low_value, high_value)

    for ref, base in ((phlo, 0), (phhi, 9)):
        of = lambda c, j: ref[c, j : j + 1, :]
        for c, (x, y) in enumerate(zip(nine(of, True), nine(of, False))):
            send((9, slice(base + c, base + c + 1)), x, y)
    send(
        (9, slice(18, 19)),
        (1.0 - 2.0 * bottom) * phhi[8, 0:1, :],
        (1.0 - 2.0 * top) * phhi[8, rows - 1 : rows, :],
    )
    for copy in copies:
        copy.wait()
    of = lambda c, j: edge[c, j if j < 3 else 3]
    for c, (x, y) in enumerate(zip(nine(of, True), nine(of, False))):
        send((c,), x, y)


def corner_kernel(g, row_ref, gphlo, gphhi, ahead, behind, to_left, to_right):
    low, high = picker(g, row_ref, ahead, behind)
    bottom = row_ref[g.flags + BOTTOM]
    for ref, got, base in ((to_left, gphlo, 0), (to_right, gphhi, 9)):
        ref[...] = got[...]
        for c in range(8):
            for side, j in ((low, 0), (high, g.rows - 1)):
                ref[c, j : j + 1, :] += side(9, slice(base + c, base + c + 1))
        for j, share in ((1, 1.0 - bottom), (2, bottom)):
            ref[6, j : j + 1, :] += share * low(9, slice(base + 8, base + 9))
    for side, j in ((low, 0), (high, g.rows - 1)):
        to_right[8, j : j + 1, :] += side(9, slice(18, 19))


def finish_kernel(g, block, row_ref, cot, part, ahead, behind, from_right, from_left, out):
    low, high = picker(g, row_ref, ahead, behind)
    bottom = row_ref[g.flags + BOTTOM]
    for c in range(8):
        for j in range(block):
            out[c, j] = 0.5 * (cot[c, j] + part[c, j])

    def columns(j, carry):
        for c in range(8):
            out[c, j, 0:1, :] += 0.5 * from_left[c, pl.ds(j, 1), :]
            out[c, j, g.cols - 1 : g.cols, :] += 0.5 * from_right[c, pl.ds(j, 1), :]
        out[7, j, 1:2, :] += 0.5 * from_left[8, pl.ds(j, 1), :]
        return carry

    lax.fori_loop(0, block, columns, 0)

    @pl.when(pl.program_id(0) == 0)
    def _():
        for c in range(8):
            out[c, 0] += 0.5 * low(c)
        out[6, 1] += (0.5 - 0.5 * bottom) * low(8)
        out[6, 2] += (0.5 * bottom) * low(8)

    @pl.when(pl.program_id(0) == pl.num_programs(0) - 1)
    def _():
        for c in range(8):
            out[c, block - 1] += 0.5 * high(c)


ANY = pl.BlockSpec(memory_space=pl.ANY)
VMEM = pl.BlockSpec(memory_space=pltpu.VMEM)
SMEM = pl.BlockSpec(memory_space=pltpu.SMEM)


def call(kernel, ins, outs, scratch, flops, limit, interpret=False):
    return pl.pallas_call(
        kernel,
        out_shape=[jax.ShapeDtypeStruct(s, jnp.float32) for _, s in outs],
        in_specs=[SMEM] + ins,
        out_specs=[s for s, _ in outs],
        scratch_shapes=scratch,
        compiler_params=pltpu.CompilerParams(vmem_limit_bytes=limit << 20),
        cost_estimate=pl.CostEstimate(flops=flops, bytes_accessed=16 << 20, transcendentals=0),
        interpret=interpret,
    )


def buffers(*shapes):
    return [pltpu.VMEM(s, jnp.float32) for s in shapes]


def forward(g, table, own, halos, planes, interpret=False):
    n = g.slots
    shape = (8, g.rows, g.cols, g.rads)
    scratch = buffers((8, 2, n, LANES), (15, 2, n, LANES), (6, n, LANES), (10, 2, n, LANES), shape)
    scratch += [pltpu.SemaphoreType.DMA((g.rows, 2)), pltpu.SemaphoreType.DMA((g.rows,))]
    outs = [(ANY, shape), (VMEM, (8, g.rows, g.rads)), (VMEM, (9, g.rows, g.rads))]
    run = call(functools.partial(forward_kernel, g), [ANY] + [VMEM] * 5, outs, scratch, 10**8, 58, interpret)
    return run(table, own, *halos, planes)


def adjoint(g, table, own, halos, cot, planes, received=(), interpret=False):
    n = g.slots
    shape = (8, g.rows, g.cols, g.rads)
    message = (10, g.cols, g.rads)
    outs = [(ANY, shape), (VMEM, (8, g.rows, g.rads)), (VMEM, (9, g.rows, g.rads)), (VMEM, message), (VMEM, message)]
    scratch = buffers(
        (8, 2, n, LANES),
        (8, 2, n, LANES),
        (13, 2, n, LANES),
        (3, 2, n, LANES),
        (2, n, LANES),
        (11, 2, g.width, LANES),
        (11, 2, 8 + PULL_SLOTS, LANES),
        shape,
    )
    rows_sem = pltpu.SemaphoreType.DMA((g.rows, 2))
    scratch += [rows_sem, rows_sem, pltpu.SemaphoreType.DMA((g.rows,))]
    ins = [ANY] + [VMEM] * 4 + [ANY] + [VMEM] * (len(received) + 1)
    run = call(functools.partial(adjoint_kernel, g, bool(received)), ins, outs, scratch, 3 * 10**8, 58, interpret)
    return run(table, own, *halos, cot, *received, planes)


def pack(g, table, state, phlo, phhi):
    message = (10, g.cols, g.rads)
    scratch = buffers((8, 4, g.cols, g.rads)) + [pltpu.SemaphoreType.DMA((2,))]
    run = call(functools.partial(pack_kernel, g), [ANY, VMEM, VMEM], [(VMEM, message)] * 2, scratch, 10**6, 16)
    return run(table, state, phlo, phhi)


def corners(g, table, gphlo, gphhi, ahead, behind):
    outs = [(VMEM, gphlo.shape), (VMEM, gphhi.shape)]
    run = call(functools.partial(corner_kernel, g), [VMEM] * 4, outs, [], 10**6, 16)
    return run(table, gphlo, gphhi, ahead, behind)


def finish(g, table, cot, part, ahead, behind, from_right, from_left):
    block = 8
    body = pl.BlockSpec((8, block, g.cols, g.rads), lambda n: (0, n, 0, 0))
    message = pl.BlockSpec((10, g.cols, g.rads), lambda n: (0, 0, 0))
    side = [pl.BlockSpec((m, block, g.rads), lambda n: (0, n, 0)) for m in (8, 9)]
    return pl.pallas_call(
        functools.partial(finish_kernel, g, block),
        grid=(g.rows // block,),
        out_shape=jax.ShapeDtypeStruct(cot.shape, jnp.float32),
        in_specs=[SMEM, body, body, message, message] + side,
        out_specs=body,
        compiler_params=pltpu.CompilerParams(vmem_limit_bytes=32 << 20),
        cost_estimate=pl.CostEstimate(flops=10**6, bytes_accessed=14 << 20, transcendentals=0),
    )(table, cot, part, ahead, behind, from_right, from_left)


class Place:
    def __init__(self):
        self.n_th, self.n_ph = lax.axis_size("th"), lax.axis_size("ph")
        n_th, n_ph = self.n_th, self.n_ph
        half = n_ph // 2
        self.th, self.ph = lax.axis_index("th"), lax.axis_index("ph")
        self.at_bottom, self.at_top = self.th == 0, self.th == n_th - 1
        self.near = self.ph < half
        self.right = [(i, (i + 1) % n_ph) for i in range(n_ph)]
        self.left = [(j, i) for i, j in self.right]
        self.round = []
        for t in range(n_th):
            for p in range(half):
                self.round.append((t * n_ph + p, (t + 1) * n_ph + p if t < n_th - 1 else t * n_ph + p + half))
                self.round.append((t * n_ph + p + half, (t - 1) * n_ph + p + half if t > 0 else p))
        self.back = [(j, i) for i, j in self.round]

    def polar(self, ahead, behind):
        both = ("th", "ph")
        return lax.ppermute(ahead, both, self.round), lax.ppermute(behind, both, self.back)

    def sideways(self, to_right, to_left):
        return lax.ppermute(to_right, "ph", self.right), lax.ppermute(to_left, "ph", self.left)


def shards(state, cotangent):
    place = Place()
    _, rows, cols, rads = state.shape
    g = Grid(rows, cols, rads, rows * place.n_th, cols * place.n_ph)
    flags = jnp.stack([place.at_bottom, place.at_top, place.near]).astype(jnp.float32)
    table = lax.dynamic_slice_in_dim(jnp.asarray(g.row_table()), place.th * rows, rows + 5, 0).reshape(-1)
    table = jnp.concatenate([table, flags])
    planes = jnp.asarray(g.radial_planes())

    def halos_of(value, last, first):
        phlo, phhi = place.sideways(last, first)
        return (phlo, phhi) + tuple(place.polar(*pack(g, table, value, phlo, phhi)))

    def give_back(parts):
        gphlo, gphhi, ahead, behind = parts
        ahead, behind = place.polar(ahead, behind)
        to_left, to_right = corners(g, table, gphlo, gphhi, ahead, behind)
        from_left, from_right = place.sideways(to_right, to_left)
        return ahead, behind, from_right, from_left

    first = jnp.concatenate([state[:, :, 0], state[7:8, :, 1]], 0)
    halos_zero = halos_of(state, state[:, :, cols - 1], first)
    moved, last, first = forward(g, table, state, halos_zero, planes)
    halos_one = halos_of(moved, last, first)
    part, *ghosts = adjoint(g, table, moved, halos_one, cotangent, planes)
    part, *ghosts = adjoint(g, table, state, halos_zero, part, planes, give_back(ghosts))
    return finish(g, table, cotangent, part, *give_back(ghosts))


def solution(mesh):
    placed = (P(None, "th", "ph", None), P(None, "th", "ph", None))
    return jax.shard_map(
        shards, mesh=mesh, in_specs=placed, out_specs=P(None, "th", "ph", None), check_vma=False
    )
```

```python
import functools
import math

import jax
import jax.numpy as jnp
import numpy as np
from jax import lax
from jax.experimental import pallas as pl
from jax.experimental.pallas import tpu as pltpu
from jax.sharding import PartitionSpec as P

GAMMA = 5.0 / 3.0
R_INNER = 1.0
R_OUTER = 3.0
COURANT = 0.4
SPEED_BOUND = 5.0
PRESSURE_SOFT = 0.05
THETA_CUT = 0.1

G1 = GAMMA - 1.0
LANES = 128
PAD = 32
FACE_SLOTS, PULL_SLOTS = 32, 32
FLIPS = (1.0, 1.0, -1.0, -1.0, 1.0, 1.0, -1.0, -1.0)
SH, SL, AZ, COT, AK, KEEP, N_ROW = 0, 1, 2, 3, 4, 5, 6
BOTTOM, TOP_END, NEAR = 0, 1, 2
INV_V, R_HI2, K_V, INV_MID, INV_LO, LO, HI, INV_SHELL, HALF_HI2, HALF_KV, HALF_LO2, TOP, OPEN = range(13)


class Grid:
    def __init__(self, rows, cols, rads, total_rows, total_cols):
        self.rows, self.cols, self.rads = rows, cols, rads
        self.width = cols + 8
        self.tiles = self.width // 8
        self.slots = PAD + (rows + 4) * self.width + PAD
        self.dth = (math.pi - 2.0 * THETA_CUT) / total_rows
        self.dph = 2.0 * math.pi / total_cols
        self.dr = (R_OUTER - R_INNER) / rads
        self.dt = COURANT * min(self.dr, R_INNER * math.sin(THETA_CUT) * self.dph) / SPEED_BOUND
        self.total_rows = total_rows

    def at(self, j, k):
        return PAD + (j + 2) * self.width + k

    def row_table(self):
        j = np.arange(-2, self.total_rows + 3, dtype=np.float64)
        low = THETA_CUT + j * self.dth
        high, mid = low + self.dth, low + 0.5 * self.dth
        drop = np.cos(low) - np.cos(high)
        keep = np.where((j == 0) | (j == self.total_rows), 0.0, 1.0)
        safe = np.where(np.abs(np.sin(low)) < 1e-6, 1.0, np.sin(low))
        table = np.zeros((len(j), N_ROW))
        table[:, SH] = np.sin(high) / drop
        table[:, SL] = np.sin(low) / drop
        table[:, AZ] = self.dth / (drop * self.dph)
        table[:, COT] = np.cos(mid) / np.sin(mid)
        table[:, AK] = keep / (safe * self.dph)
        table[:, KEEP] = keep
        return table.astype(np.float32)

    @property
    def flags(self):
        return (self.rows + 5) * N_ROW

    def radial_planes(self):
        i = np.arange(self.rads, dtype=np.float64)
        low = R_INNER + i * self.dr
        high, mid = low + self.dr, low + 0.5 * self.dr
        vol = (high**3 - low**3) / 3.0
        shell = 0.5 * (high**2 - low**2)
        top = np.where(i == self.rads - 1, 2.0, 1.0)
        planes = [None] * 13
        planes[INV_V] = 1.0 / vol
        planes[R_HI2] = high**2
        planes[K_V] = shell / vol
        planes[INV_MID] = 1.0 / mid
        planes[INV_LO] = 1.0 / low
        planes[LO] = low
        planes[HI] = high
        planes[INV_SHELL] = 1.0 / shell
        planes[HALF_HI2] = 0.5 * self.dt * high**2
        planes[HALF_KV] = 0.5 * self.dt * shell / vol
        planes[HALF_LO2] = 0.5 * self.dt * low**2
        planes[TOP] = top
        planes[OPEN] = 2.0 - top
        stack = np.stack(planes).astype(np.float32).reshape(13, 2, 1, LANES)
        return np.broadcast_to(stack, (13, 2, 8, LANES)).copy()


def lane_index(x):
    return lax.broadcasted_iota(jnp.int32, x.shape, 2)


def next_r(x, last=None):
    turned = pltpu.roll(x, LANES - 1, 2)
    end = x[1:2] if last is None else last
    return jnp.where(lane_index(x) == LANES - 1, jnp.concatenate([turned[1:2], end], 0), turned)


def prev_r(x, first):
    turned = pltpu.roll(x, 1, 2)
    return jnp.where(lane_index(x) == 0, jnp.concatenate([first, turned[0:1]], 0), turned)


def split(x):
    return jnp.stack([x[:, :LANES], x[:, LANES:]])


def load(ref, field, slot, size=8):
    return ref[field, :, pl.ds(slot, size), :]


def put(ref, field, slot, value):
    ref[field, :, pl.ds(slot, value.shape[1]), :] = value


def loader(size):
    return lambda ref, field, slot: load(ref, field, slot, size)


def planes_of(rc, size):
    return lambda i: jnp.concatenate([rc[i]] * (size // 8), 1)


def put_line(ref, field, slot, line):
    ref[field, 0, pl.ds(slot, 1), :] = line[:, :LANES]
    ref[field, 1, pl.ds(slot, 1), :] = line[:, LANES:]


def get_line(ref, field, slot):
    return jnp.concatenate([ref[field, 0, pl.ds(slot, 1), :], ref[field, 1, pl.ds(slot, 1), :]], 1)


def picker(g, row_ref, ahead, behind):
    near = row_ref[g.flags + NEAR] > 0.5

    def low(*at):
        return jnp.where(near, ahead[at], behind[at])

    def high(*at):
        return jnp.where(near, behind[at], ahead[at])

    return low, high


def row_copies(g, hbm, ref, sem, row=None):
    for j in range(g.rows) if row is None else (row,):
        for h in range(2):
            yield pltpu.make_async_copy(
                hbm.at[:, j, :, pl.ds(h * LANES, LANES)], ref.at[:, h, pl.ds(g.at(j, 0), g.cols), :], sem.at[j, h]
            )


def fill_state(g, us, row_ref, halos):
    rows, cols = g.rows, g.cols
    phlo, phhi, ahead, behind, corner_ahead, corner_behind = halos
    low, high = picker(g, row_ref, ahead, behind)
    corner_low, corner_high = picker(g, row_ref, corner_ahead, corner_behind)
    calm = [jnp.full((2, 8, LANES), 1.0 if c == 0 else 0.0, jnp.float32) for c in range(8)]

    def keep(j):
        return row_ref[(j + 2) * N_ROW + KEEP]

    def ends(j, fetch):
        for c in range(8):
            scale = keep(j) if c == 6 else None
            for which, k in ((0, -1), (1, cols)):
                line = fetch(c, which)
                put_line(us, c, g.at(j, k), line if scale is None else line * scale)
        put_line(us, 7, g.at(j, cols + 1), fetch(7, 2))

    def body_row(j, side):
        for c in range(8):
            for t in range(cols // 8):
                x = split(side(c, slice(t * 8, t * 8 + 8)))
                put(us, c, g.at(j, t * 8), x * keep(j) if c == 6 else x)

    def still(n, carry):
        for c in range(8):
            put(us, c, pl.multiple_of(g.at(-2, cols) + n * g.width, 8), calm[c])
        return carry

    lax.fori_loop(0, rows + 3, still, 0)
    body_row(-1, low)
    ends(-1, lambda c, w: corner_low(slice((c, 9 + c, 18)[w], (c, 9 + c, 18)[w] + 1)))

    def step(j, carry):
        ends(j, lambda c, w: (phlo[c, pl.ds(j, 1), :], phhi[c, pl.ds(j, 1), :], phhi[8, pl.ds(j, 1), :])[w])
        return carry

    lax.fori_loop(0, rows, step, 0)
    body_row(rows, high)
    ends(rows, lambda c, w: corner_high(slice((c, 9 + c, 18)[w], (c, 9 + c, 18)[w] + 1)))
    far = keep(rows + 1)
    for t in range(g.tiles):
        x = split(high(8, slice(t * 8, t * 8 + 8))) if t < cols // 8 else calm[1]
        put(us, 6, g.at(rows + 1, t * 8), x * far)
    put_line(us, 6, g.at(rows + 1, -1), corner_high(slice(8, 9)) * far)
    put_line(us, 6, g.at(rows + 1, cols), corner_high(slice(17, 18)) * far)

def arrive(g, us, row_ref, own, sem, j):
    for copy in row_copies(g, own, us, sem, j):
        copy.wait()
    if isinstance(j, int) and j == 0:
        for t in range(g.cols // 8):
            put(us, 6, g.at(0, t * 8), load(us, 6, g.at(0, t * 8)) * row_ref[2 * N_ROW + KEEP])


def cell_values(g, us, p, size):
    load = loader(size)
    rho, m0, m1, m2, energy, u5, u6, u7 = [load(us, c, p) for c in range(8)]
    b0 = 0.5 * (u5 + next_r(u5))
    b1 = 0.5 * (u6 + load(us, 6, p + g.width))
    b2 = 0.5 * (u7 + load(us, 7, p + 1))
    q = 1.0 / rho
    v0, v1, v2 = m0 * q, m1 * q, m2 * q
    square = b0 * b0 + b1 * b1 + b2 * b2
    pressure = G1 * (energy - 0.5 * (m0 * v0 + m1 * v1 + m2 * v2) - 0.5 * square)
    total = pressure + 0.5 * square
    soft = pressure * pressure + PRESSURE_SOFT * PRESSURE_SOFT
    inv_soft = lax.rsqrt(soft)
    c2 = (GAMMA * (soft * inv_soft) + square) * q
    return (m0, m1, m2), (v0, v1, v2), (b0, b1, b2), u5, q, pressure, total, energy + total, inv_soft, c2


def forward_kernel(g, row_ref, own, *refs):
    halos, rc, refs = refs[:6], refs[6], refs[7:]
    out, last_col, first_col, go_ahead, go_behind, us, cf, gf, ff, stage, sem, sem_out = refs
    for copy in row_copies(g, own, us, sem):
        copy.start()
    fill_state(g, us, row_ref, halos)
    w = g.width
    wide = w
    arrive(g, us, row_ref, own, sem, 0)

    def cells(n, carry):
        p = pl.multiple_of(g.at(-1, -8) + n * wide, 8)

        @pl.when((n > 0) & (n < g.rows))
        def _():
            arrive(g, us, row_ref, own, sem, n)

        m, v, b, u5, q, pressure, total, h, inv_soft, c2 = cell_values(g, us, p, wide)
        put(cf, 0, p, m[0] * v[0] - b[0] * b[0] + total)
        put(cf, 1, p, m[0] * v[1] - b[0] * b[1])
        put(cf, 2, p, m[0] * v[2] - b[0] * b[2])
        put(cf, 3, p, m[1] * v[1] - b[1] * b[1] + total)
        put(cf, 4, p, m[1] * v[2] - b[1] * b[2])
        put(cf, 5, p, m[2] * v[2] - b[2] * b[2] + total)
        vb = v[0] * b[0] + v[1] * b[1] + v[2] * b[2]
        for d in range(3):
            put(cf, 6 + d, p, h * v[d] - b[d] * vb)
            put(cf, 9 + d, p, v[d] * v[d] + c2)
        put(cf, 12, p, v[2] * b[1] - v[1] * b[2])
        put(cf, 13, p, v[0] * b[2] - v[2] * b[0])
        put(cf, 14, p, v[1] * b[0] - v[0] * b[1])
        m, v, b = [[x[0:1] for x in y] for y in (m, v, b)]
        bg = u5[0:1]
        gain = (1.0 - 0.5 * GAMMA) * (bg * bg - b[0] * b[0])
        vbg = vb[0:1] + v[0] * (bg - b[0])
        ghost = (
            m[0] * v[0] - bg * bg + total[0:1] + gain,
            m[0] * v[1] - bg * b[1],
            m[0] * v[2] - bg * b[2],
            (h[0:1] + gain) * v[0] - bg * vbg,
            v[0] * b[2] - v[2] * bg,
            v[1] * bg - v[0] * b[1],
        )
        for f, x in enumerate(ghost):
            gf[f, pl.ds(p, wide), :] = x[0]
        return carry

    lax.fori_loop(0, g.rows + 3, cells, 0)

    index = ((0, 1, 2), (1, 3, 4), (2, 4, 5))

    def face(d, p, shift, size):
        load = loader(size)
        fluxes = [load(us, 1 + d, p)] + [load(cf, index[d][c], p) for c in range(3)] + [load(cf, 6 + d, p)]
        speed = load(cf, 9 + d, p)
        state = [load(us, c, p) for c in range(5)]
        if shift is None:
            other = [next_r(x) for x in fluxes]
            speed2 = next_r(speed)
            state2 = [other[0] if c == 1 else next_r(state[c]) for c in range(5)]
        else:
            r = p + shift
            other = [load(us, 1 + d, r)] + [load(cf, index[d][c], r) for c in range(3)] + [load(cf, 6 + d, r)]
            speed2 = load(cf, 9 + d, r)
            state2 = [load(us, c, r) for c in range(5)]
        total = 0.5 * (speed + speed2)
        half = 0.5 * (total * lax.rsqrt(total))
        return fluxes, [0.5 * (fluxes[c] + other[c]) - half * (state2[c] - state[c]) for c in range(5)]

    def faces(n, carry):
        p = pl.multiple_of(g.at(-1, 0) + n * FACE_SLOTS, 8)
        for d, shift, base in ((1, w, 0), (2, 1, 5)):
            _, flux = face(d, p, shift, FACE_SLOTS)
            for c in range(5):
                put(ff, base + c, p, flux[c])
        return carry

    lax.fori_loop(0, (g.rows + 1) * g.width // FACE_SLOTS, faces, 0)

    size = g.cols
    load = loader(size)
    plane = planes_of(rc, size)

    def leave(j):
        return pltpu.make_async_copy(stage.at[:, j], out.at[:, j], sem_out.at[j])

    def combine(j, carry):
        p = pl.multiple_of(g.at(j, 0), 8)
        row = (j + 2) * N_ROW
        sh, sl, az, cot, ak, keep = [row_ref[row + i] for i in range(N_ROW)]
        cells_here, flux_r = face(0, p, None, size)
        ghost = [load(us, 1, p)[0:1]] + [gf[f, pl.ds(p, size), :][None] for f in range(4)]
        inv_v, kv = plane(INV_V), plane(K_V)
        rates = []
        for c in range(5):
            high = plane(R_HI2) * flux_r[c]
            first = 0.5 * plane(HALF_LO2)[0:1] * (2.0 / g.dt) * (ghost[c] + cells_here[c][0:1])
            low = prev_r(high, first)
            th = sh * load(ff, c, p) - sl * load(ff, c, p - w)
            ph = az * (load(ff, 5 + c, p) - load(ff, 5 + c, p - 1))
            rates.append(-(inv_v * (high - low) + kv * (th + ph)))
        tt = [load(cf, f, p) for f in range(1, 6)]
        mid = plane(INV_MID)
        rates[1] = rates[1] + (tt[2] + tt[4]) * mid
        rates[2] = rates[2] + (cot * tt[4] - tt[0]) * mid
        rates[3] = rates[3] - (tt[1] + cot * tt[3]) * mid
        ep, ept = load(cf, 14, p), load(cf, 14, p + w)
        x0 = load(cf, 14, p - w) + ep
        x1 = ep + ept
        g_here = gf[5, pl.ds(p, size), :][None]
        x0m = prev_r(x0, gf[5, pl.ds(p - w, size), :][None] + g_here)
        x1m = prev_r(x1, g_here + gf[5, pl.ds(p + w, size), :][None])
        z0 = 0.25 * (x0 + x0m)
        zr = 0.25 * (next_r(x0) + x0)
        z1 = 0.25 * (x1 + x1m)
        et = load(cf, 13, p)
        y0 = load(cf, 13, p - 1) + et
        y1 = et + load(cf, 13, p + 1)
        g_here = gf[4, pl.ds(p, size), :][None]
        y0m = prev_r(y0, gf[4, pl.ds(p - 1, size), :][None] + g_here)
        y1m = prev_r(y1, g_here + gf[4, pl.ds(p + 1, size), :][None])
        p0 = 0.25 * (y0 + y0m)
        pr = 0.25 * (next_r(y0) + y0)
        p1 = 0.25 * (y1 + y1m)
        er, era, erb = load(cf, 12, p), load(cf, 12, p - 1), load(cf, 12, p - w)
        r0 = 0.25 * (er + era + erb + load(cf, 12, p - w - 1))
        r1 = 0.25 * (load(cf, 12, p + 1) + er + load(cf, 12, p - w + 1) + erb)
        rt = 0.25 * (load(cf, 12, p + w) + load(cf, 12, p + w - 1) + er + era)
        lo, hi, shell = plane(LO), plane(HI), plane(INV_SHELL)
        rates.append(-plane(INV_LO) * (sh * z1 - sl * z0 - az * (p1 - p0)))
        rates.append(-shell * (g.dr * ak * (r1 - r0) - keep * (hi * zr - lo * z0)))
        rates.append(shell * ((g.dr / g.dth) * (rt - r0) - (hi * pr - lo * p0)))
        for c in range(8):
            new = load(us, c, p) + g.dt * rates[c]
            stage[c, j] = jnp.concatenate([new[0], new[1]], 1)
        leave(j).start()
        for c in range(8):
            last_col[c, pl.ds(j, 1), :] = stage[c, j, g.cols - 1 : g.cols, :]
            first_col[c, pl.ds(j, 1), :] = stage[c, j, 0:1, :]
        first_col[8, pl.ds(j, 1), :] = stage[7, j, 1:2, :]
        return carry

    lax.fori_loop(0, g.rows, combine, 0)

    send_rows(g, row_ref, lambda c, j: stage[c, j], go_ahead, go_behind)

    def settle(j, carry):
        leave(j).wait()
        return carry

    lax.fori_loop(0, g.rows, settle, 0)


def adjoint_kernel(g, received, row_ref, own, cot, *refs):
    halos, rc, refs = refs[:6], refs[6], refs[7:]
    if received:
        base, *got = refs[:7]
        refs = refs[7:]
    out, gphlo, gphhi, go_ahead, go_behind, us, cs, cf, ef, zf, ft, fp, stage, sem, sem_cot, sem_out, sem_base = refs
    w, rows, cols = g.width, g.rows, g.cols
    load = loader(8)
    for copy in row_copies(g, own, us, sem):
        copy.start()
    for copy in row_copies(g, cot, cs, sem_cot):
        copy.start()

    def enter(j):
        return pltpu.make_async_copy(base.at[:, j], stage.at[:, j], sem_base.at[j])

    if received:
        for j in range(rows):
            enter(j).start()
    zero = jnp.zeros((2, 8, LANES), jnp.float32)
    for j in (-2, -1, rows, rows + 1):
        for c in range(8):
            for t in range(g.tiles):
                put(cs, c, g.at(j, t * 8), zero)
    for c in range(8):
        put(cs, c, g.at(-2, -8), zero)

    def clear(j, carry):
        for c in range(8):
            put(cs, c, g.at(j, cols), zero)
        return carry

    lax.fori_loop(0, rows, clear, 0)
    fill_state(g, us, row_ref, halos)
    arrive(g, us, row_ref, own, sem, 0)

    def cells(n, carry):
        p = pl.multiple_of(g.at(-1, -8) + n * w, 8)

        @pl.when((n > 0) & (n < rows))
        def _():
            arrive(g, us, row_ref, own, sem, n)

        m, v, b, u5, q, pressure, total, h, inv_soft, c2 = cell_values(g, us, p, w)
        for d in range(3):
            put(cf, d, p, v[d])
            put(cf, 3 + d, p, b[d])
            put(cf, 6 + d, p, v[d] * v[d] + c2)
        put(cf, 9, p, h)
        put(cf, 10, p, q)
        put(cf, 11, p, GAMMA * q * (pressure * inv_soft))
        put(cf, 12, p, c2 * q)
        return carry

    lax.fori_loop(0, rows + 3, cells, 0)

    for copy in row_copies(g, cot, cs, sem_cot):
        copy.wait()
    if received:
        back_ahead, back_behind, from_right, from_left, lines_right, lines_left = got
        low, high = picker(g, row_ref, back_ahead, back_behind)
        bottom = row_ref[g.flags + BOTTOM]

        def add_line(c, slot, line):
            put_line(cs, c, slot, get_line(cs, c, slot) + line)

        def columns(j, carry):
            for c in range(8):
                add_line(c, g.at(j, 0), from_left[c, pl.ds(j, 1), :])
                add_line(c, g.at(j, cols - 1), from_right[c, pl.ds(j, 1), :])
            add_line(7, g.at(j, 1), from_left[8, pl.ds(j, 1), :])
            return carry

        lax.fori_loop(0, rows, columns, 0)
        for t in range(cols // 8):
            at = slice(t * 8, t * 8 + 8)
            for c in range(8):
                p = g.at(0, t * 8)
                put(cs, c, p, load(cs, c, p) + split(low(c, at)))
                p = g.at(rows - 1, t * 8)
                put(cs, c, p, load(cs, c, p) + split(high(c, at)))
            for j, share in ((1, 1.0 - bottom), (2, bottom)):
                p = g.at(j, t * 8)
                put(cs, 6, p, load(cs, 6, p) + share * split(low(8, at)))
        for j, right0, left0, second in ((0, 0, 0, 9), (rows - 1, 9, 10, 19)):
            for c in range(8):
                add_line(c, g.at(j, cols - 1), lines_right[right0 + c : right0 + c + 1, :])
                add_line(c, g.at(j, 0), lines_left[left0 + c : left0 + c + 1, :])
            add_line(7, g.at(j, 1), lines_left[second : second + 1, :])
        for lines, k in ((lines_right, cols - 1), (lines_left, 0)):
            for j, share in ((1, 1.0 - bottom), (2, bottom)):
                add_line(6, g.at(j, k), share * lines[8:9, :])

    for f in range(3):
        put(ef, f, g.at(-1, -8), zero)
    for f in range(2):
        zf[f, pl.ds(g.at(-1, -8), 8), :] = zero[0]

    def edges(n, carry):
        load = loader(w)
        plane = planes_of(rc, w)
        none = jnp.zeros((1, w, LANES), jnp.float32)
        p = pl.multiple_of(g.at(-1, 0) + n * w, 8)
        j = n - 1
        row = (j + 2) * N_ROW
        sl, az, ak, keep = [row_ref[row + i] for i in (SL, AZ, AK, KEEP)]
        sh_below = row_ref[row - N_ROW + SH]
        shell, lo, hi = plane(INV_SHELL), plane(LO), plane(HI)
        c5, c6, c7 = load(cs, 5, p), load(cs, 6, p), load(cs, 7, p)
        rb = ak * (c6 - load(cs, 6, p - 1)) + (1.0 / g.dth) * (load(cs, 7, p - w) - c7)
        put(ef, 0, p, (0.25 * g.dt * g.dr) * shell * rb)
        q6 = keep * c6 * shell
        zb = plane(INV_LO) * (sl * c5 - sh_below * load(cs, 5, p - w)) + prev_r(hi * q6, none) - lo * q6
        q7 = c7 * shell
        hq7 = hi * q7
        pb = plane(INV_LO) * az * (load(cs, 5, p - 1) - c5) + lo * q7 - prev_r(hq7, none)
        zl = 2.0 * hi[1:2] * q6[1:2]
        plast = -2.0 * hq7[1:2]
        put(ef, 1, p, (0.25 * g.dt) * (zb + next_r(zb, zl)))
        put(ef, 2, p, (0.25 * g.dt) * (pb + next_r(pb, plast)))
        zf[0, pl.ds(p, w), :] = (0.25 * g.dt) * zb[0]
        zf[1, pl.ds(p, w), :] = (0.25 * g.dt) * pb[0]
        return carry

    lax.fori_loop(0, rows + 3, edges, 0)

    size = PULL_SLOTS
    load = loader(size)
    plane = planes_of(rc, size)
    none = jnp.zeros((1, size, LANES), jnp.float32)
    groups = w // size
    for f in range(11):
        for t in range(g.tiles):
            put(ft, f, t * 8, zero)
        put(fp, f, 0, zero)

    def face_pull(halves, state, state2, speed, speed2, closed=None):
        total = 0.5 * (speed + speed2)
        inv = lax.rsqrt(total)
        a = total * inv
        if closed is not None:
            a = a * closed
        dot = halves[0] * (state2[0] - state[0])
        for c in range(1, 5):
            dot = dot + halves[c] * (state2[c] - state[c])
        return halves + [a * x for x in halves] + [-0.25 * inv * dot]

    def pull(n, carry):
        p = pl.multiple_of(g.at(-1, -8) + n * size, 8)
        j = n // groups - 1
        slot = pl.multiple_of(lax.rem(n, groups) * size, 8)
        row = (j + 2) * N_ROW
        sh, az, cot = [row_ref[row + i] for i in (SH, AZ, COT)]
        sl_above = row_ref[row + N_ROW + SL]
        state = [load(us, c, p) for c in range(5)]
        cc = [load(cs, c, p) for c in range(5)]
        kd = plane(HALF_KV)
        sides = []
        up = kd * sl_above
        down = kd * sh
        pw = pl.multiple_of(p + jnp.where(n >= (rows + 1) * groups, 0, w), 8)
        high = face_pull(
            [up * load(cs, c, pw) - down * cc[c] for c in range(5)],
            state,
            [load(us, c, pw) for c in range(5)],
            load(cf, 7, p),
            load(cf, 7, pw),
        )
        low = [load(ft, f, slot) for f in range(11)]
        for f in range(11):
            put(ft, f, slot, high[f])
        sides.append((high, low))
        kaz = kd * az
        high_p = face_pull(
            [kaz * (load(cs, c, p + 1) - cc[c]) for c in range(5)],
            state,
            [load(us, c, p + 1) for c in range(5)],
            load(cf, 8, p),
            load(cf, 8, p + 1),
        )
        for f in range(11):
            put(fp, f, 8, high_p[f])
        per_volume = [plane(INV_V) * x for x in cc]
        half_hi = plane(HALF_HI2)
        speed = load(cf, 6, p)
        high_r = face_pull(
            [half_hi * (next_r(x, none) - x) for x in per_volume],
            state,
            [next_r(x) for x in state],
            speed,
            next_r(speed),
            plane(OPEN),
        )
        first = [plane(HALF_LO2)[0:1] * x[0:1] for x in per_volume]
        low_r = [prev_r(high_r[f], first[f] if f < 5 else none) for f in range(11)]
        low_p = [load(fp, f, 7) for f in range(11)]
        for f in range(11):
            fp[f, :, 7:8, :] = fp[f, :, size + 7 : size + 8, :]
        sides.append((high_p, low_p))
        ft_, fp_ = [[hi_[c] + lo_[c] for c in range(5)] for hi_, lo_ in sides]
        fr_ = [plane(TOP) * high_r[c] + low_r[c] for c in range(5)]
        both = [(high_r, low_r)] + sides
        ub = []
        for c in range(5):
            ub.append(
                cc[c]
                + (both[0][0][5 + c] - both[0][1][5 + c])
                + (both[1][0][5 + c] - both[1][1][5 + c])
                + (both[2][0][5 + c] - both[2][1][5 + c])
            )
        sb = [hi_[10] + lo_[10] for hi_, lo_ in both]
        mid = plane(INV_MID) * g.dt
        w1, w2, w3 = cc[1] * mid, cc[2] * mid, cc[3] * mid
        s00, s11 = fr_[1], ft_[2] + w1
        s22 = fp_[3] + w1 + cot * w2
        s01 = fr_[2] + ft_[1] - w2
        s02 = fr_[3] + fp_[1] - w3
        s12 = ft_[3] + fp_[2] - cot * w3
        e0 = load(ef, 0, p) + load(ef, 0, p + 1) + load(ef, 0, p + w) + load(ef, 0, p + w + 1)
        e2 = load(ef, 1, p) + load(ef, 1, p + w)
        e1 = load(ef, 2, p) + load(ef, 2, p + 1)
        v = [load(cf, d, p) for d in range(3)]
        b = [load(cf, 3 + d, p) for d in range(3)]
        h, q = load(cf, 9, p), load(cf, 10, p)
        gg = (fr_[4], ft_[4], fp_[4])
        flow = v[0] * gg[0] + v[1] * gg[1] + v[2] * gg[2]
        beta = b[0] * gg[0] + b[1] * gg[1] + b[2] * gg[2]
        vb = v[0] * b[0] + v[1] * b[1] + v[2] * b[2]
        d00, d11, d22 = s00 + s00, s11 + s11, s22 + s22
        sv = (
            d00 * v[0] + s01 * v[1] + s02 * v[2],
            s01 * v[0] + d11 * v[1] + s12 * v[2],
            s02 * v[0] + s12 * v[1] + d22 * v[2],
        )
        sbm = (
            d00 * b[0] + s01 * b[1] + s02 * b[2],
            s01 * b[0] + d11 * b[1] + s12 * b[2],
            s02 * b[0] + s12 * b[1] + d22 * b[2],
        )
        c2b = sb[0] + sb[1] + sb[2]
        ptb = s00 + s11 + s22 + flow
        pb = c2b * load(cf, 11, p) + ptb
        pg = G1 * pb
        bbb = 2.0 * (c2b * q) + ptb - pg
        bxe = (b[1] * e2 - b[2] * e1, b[2] * e0 - b[0] * e2, b[0] * e1 - b[1] * e0)
        exv = (e1 * v[2] - e2 * v[1], e2 * v[0] - e0 * v[2], e0 * v[1] - e1 * v[0])
        rho_bar = ub[0] - c2b * load(cf, 12, p)
        m_bar, b_bar = [], []
        for d in range(3):
            vbar = h * gg[d] - beta * b[d] + 2.0 * (v[d] * sb[d]) - bxe[d]
            turn = q * vbar - pg * v[d]
            f0 = (fr_[0], ft_[0], fp_[0])[d]
            m_bar.append(ub[1 + d] + f0 + sv[d] + turn)
            rho_bar = rho_bar - v[d] * (0.5 * sv[d] + turn + 0.5 * (pg * v[d]))
            b_bar.append(b[d] * bbb - sbm[d] - vb * gg[d] - beta * v[d] - exv[d])
        e_bar = ub[4] + flow + pg

        first_lane = lax.broadcasted_iota(jnp.int32, (1, size, LANES), 2) == 0
        v, b = [[x[0:1] for x in y] for y in (v, b)]
        q, h = q[0:1], h[0:1]
        bg = load(us, 5, p)[0:1]
        h = h + (1.0 - 0.5 * GAMMA) * (bg * bg - b[0] * b[0])
        vbg = vb[0:1] + v[0] * (bg - b[0])
        s00, s01, s02, g0 = first[1], first[2], first[3], first[4]
        e2 = (zf[0, pl.ds(p, size), :] + zf[0, pl.ds(p + w, size), :])[None]
        e1 = (zf[1, pl.ds(p, size), :] + zf[1, pl.ds(p + 1, size), :])[None]
        flow = v[0] * g0
        beta = bg * g0
        pb = s00 + flow
        pg = G1 * pb
        bbb = pb - pg
        d00 = s00 + s00
        sv = (d00 * v[0] + s01 * v[1] + s02 * v[2], s01 * v[0], s02 * v[0])
        sbm = (d00 * bg + s01 * b[1] + s02 * b[2], s01 * bg, s02 * bg)
        vbar = (
            h * g0 - beta * bg - (b[1] * e2 - b[2] * e1),
            bg * e2 - beta * b[1],
            -(beta * b[2]) - bg * e1,
        )
        exv = (e1 * v[2] - e2 * v[1], e2 * v[0], -(e1 * v[0]))
        more = [None] * 8
        rho_more = none
        for d in range(3):
            turn = q * vbar[d] - pg * v[d]
            more[1 + d] = sv[d] + turn + (first[0] if d == 0 else 0.0)
            rho_more = rho_more - v[d] * (0.5 * sv[d] + turn + 0.5 * (pg * v[d]))
            bd = bg if d == 0 else b[d]
            more[5 + d] = bd * bbb - sbm[d] - beta * v[d] - exv[d]
        more[5] = more[5] - vbg * g0
        more[0] = rho_more
        more[4] = flow + pg

        def with_first(x, extra):
            return x + jnp.concatenate([jnp.where(first_lane, extra, 0.0), none], 0)

        put(us, 0, p, with_first(rho_bar, more[0]))
        for d in range(3):
            put(us, 1 + d, p, with_first(m_bar[d], more[1 + d]))
        put(us, 4, p, with_first(e_bar, more[4]))
        put(us, 5, p, load(cs, 5, p) + 0.5 * (plane(TOP) * b_bar[0] + prev_r(b_bar[0], 2.0 * more[5])))
        put(us, 6, p, with_first(b_bar[1], more[6]))
        put(us, 7, p, with_first(b_bar[2], more[7]))
        return carry

    lax.fori_loop(0, (rows + 2) * groups + 1, pull, 0)
    load = loader(8)

    def keep_of(j):
        return 0.5 * row_ref[(j + 2) * N_ROW + KEEP]

    def tile6(j, p):
        return keep_of(j) * (load(us, 6, p) + load(us, 6, p - w))

    def tile7(p):
        return 0.5 * (load(us, 7, p) + load(us, 7, p - 1))

    def join(x):
        return jnp.concatenate([x[0], x[1]], 1)

    def line_of(c, j, k):
        p = g.at(j, k)
        if c < 6:
            return get_line(us, c, p)
        if c == 6:
            here = get_line(us, 6, p)
            if isinstance(j, int) and j == -1:
                return keep_of(j) * here
            return keep_of(j) * (here + get_line(us, 6, p - w))
        here = get_line(us, 7, p)
        return 0.5 * here if k == -1 else 0.5 * (here + get_line(us, 7, p - 1))

    def leave(j):
        return pltpu.make_async_copy(stage.at[:, j], out.at[:, j], sem_out.at[j])

    def give(j, carry):
        if received:
            enter(j).wait()
        for t in range(cols // 8):
            p = g.at(j, t * 8)
            at = (j, slice(t * 8, t * 8 + 8))

            def leave_tile(c, x):
                stage[(c,) + at] = 0.5 * (stage[(c,) + at] + x) if received else x

            for c in range(6):
                leave_tile(c, join(load(us, c, p)))
            leave_tile(6, join(load(cs, 6, p) + tile6(j, p)))
            leave_tile(7, join(load(cs, 7, p) + tile7(p)))
        leave(j).start()
        for c in range(8):
            gphlo[c, pl.ds(j, 1), :] = line_of(c, j, -1)
            gphhi[c, pl.ds(j, 1), :] = line_of(c, j, cols)
        gphhi[8, pl.ds(j, 1), :] = 0.5 * get_line(us, 7, g.at(j, cols))
        return carry

    lax.fori_loop(0, rows, give, 0)

    bottom, top = row_ref[g.flags + BOTTOM], row_ref[g.flags + TOP_END]
    near = row_ref[g.flags + NEAR] > 0.5

    def toward_low(of):
        signs = [1.0 if f > 0 else 1.0 - 2.0 * bottom for f in FLIPS]
        face = of(6)
        return [of(c) * signs[c] for c in range(6)] + [face * (1.0 - bottom), of(7) * signs[7], face * -bottom]

    def toward_high(of, far):
        signs = [1.0 if f > 0 else 1.0 - 2.0 * top for f in FLIPS]
        face = of(6) * (1.0 - top) - far * top
        return [of(c) * signs[c] for c in range(6)] + [face, of(7) * signs[7], far * (1.0 - top)]

    def send(at, low_value, high_value):
        go_ahead[at] = jnp.where(near, high_value, low_value)
        go_behind[at] = jnp.where(near, low_value, high_value)

    for t in range(cols // 8):
        p0, p1 = g.at(-1, t * 8), g.at(rows, t * 8)

        def tile_low(c):
            if c == 6:
                return join(keep_of(-1) * load(us, 6, p0))
            return join(load(us, c, p0) if c < 6 else tile7(p0))

        def tile_high(c):
            return join(load(us, c, p1) if c < 6 else tile6(rows, p1) if c == 6 else tile7(p1))

        lows = toward_low(tile_low)
        highs = toward_high(tile_high, join(keep_of(rows + 1) * load(us, 6, p1)))
        for c in range(9):
            send((c, slice(t * 8, t * 8 + 8)), lows[c], highs[c])
    for k, base in ((-1, 0), (cols, 9)):
        lows = toward_low(lambda c: line_of(c, -1, k))
        highs = toward_high(lambda c: line_of(c, rows, k), keep_of(rows + 1) * get_line(us, 6, g.at(rows, k)))
        for c in range(9):
            send((9, slice(base + c, base + c + 1)), lows[c], highs[c])
    send(
        (9, slice(18, 19)),
        (0.5 - bottom) * get_line(us, 7, g.at(-1, cols)),
        (0.5 - top) * get_line(us, 7, g.at(rows, cols)),
    )

    def settle(j, carry):
        leave(j).wait()
        return carry

    lax.fori_loop(0, rows, settle, 0)


def polar_nine(g, pole, of, low):
    signs = [1.0 if f > 0 else 1.0 - 2.0 * pole for f in FLIPS]
    values = [of(c, 0 if low else g.rows - 1) * signs[c] for c in range(8)]
    if low:
        values[6] = of(6, 0) * (1.0 - pole) - of(6, 2) * pole
        return values + [of(6, 1)]
    return values + [-of(6, g.rows - 1)]


def sender(g, row_ref, go_ahead, go_behind):
    near = row_ref[g.flags + NEAR] > 0.5

    def send(at, low_value, high_value):
        go_ahead[at] = jnp.where(near, high_value, low_value)
        go_behind[at] = jnp.where(near, low_value, high_value)

    return send


def send_rows(g, row_ref, of, go_ahead, go_behind):
    bottom, top = row_ref[g.flags + BOTTOM], row_ref[g.flags + TOP_END]
    send = sender(g, row_ref, go_ahead, go_behind)
    for c, (x, y) in enumerate(zip(polar_nine(g, bottom, of, True), polar_nine(g, top, of, False))):
        send(c, x, y)


def pack_kernel(g, row_ref, state, last_col, first_col, go_ahead, go_behind, edge, left, right, sem):
    rows, cols = g.rows, g.cols
    copies = [
        pltpu.make_async_copy(state.at[:, pl.ds(0, 3)], edge.at[:, pl.ds(0, 3)], sem.at[0]),
        pltpu.make_async_copy(state.at[:, pl.ds(rows - 1, 1)], edge.at[:, pl.ds(3, 1)], sem.at[1]),
        pltpu.make_async_copy(state.at[:, :, pl.ds(0, 8)], left, sem.at[2]),
        pltpu.make_async_copy(state.at[:, :, pl.ds(cols - 8, 8)], right, sem.at[3]),
    ]
    for copy in copies:
        copy.start()
    for copy in copies[:2]:
        copy.wait()
    send_rows(g, row_ref, lambda c, j: edge[c, j if j < 3 else 3], go_ahead, go_behind)
    for copy in copies[2:]:
        copy.wait()

    def line(j, carry):
        for c in range(8):
            first_col[c, pl.ds(j, 1), :] = left[c, j, 0:1, :]
            last_col[c, pl.ds(j, 1), :] = right[c, j, 7:8, :]
        first_col[8, pl.ds(j, 1), :] = left[7, j, 1:2, :]
        return carry

    lax.fori_loop(0, rows, line, 0)


def pack_corner_kernel(g, row_ref, phlo, phhi, go_ahead, go_behind):
    bottom, top = row_ref[g.flags + BOTTOM], row_ref[g.flags + TOP_END]
    send = sender(g, row_ref, go_ahead, go_behind)
    for ref, base in ((phlo, 0), (phhi, 9)):
        of = lambda c, j: ref[c, j : j + 1, :]
        for c, (x, y) in enumerate(zip(polar_nine(g, bottom, of, True), polar_nine(g, top, of, False))):
            send(slice(base + c, base + c + 1), x, y)
    send(
        slice(18, 19),
        (1.0 - 2.0 * bottom) * phhi[8, 0:1, :],
        (1.0 - 2.0 * top) * phhi[8, g.rows - 1 : g.rows, :],
    )


def turn_kernel(g, row_ref, ahead, behind, to_left, to_right):
    low, high = picker(g, row_ref, ahead, behind)
    to_left[0:9, :] = low(9, slice(0, 9))
    to_left[9:18, :] = high(9, slice(0, 9))
    to_right[0:10, :] = low(9, slice(9, 19))
    to_right[10:20, :] = high(9, slice(9, 19))


def finish_kernel(
    g, row_ref, part, ahead, behind, from_right, from_left, lines_right, lines_left, out, edge, left, right, sem
):
    rows, cols = g.rows, g.cols
    inner = pl.ds(3, rows - 4)
    places = (
        ((slice(None), pl.ds(0, 3)), edge.at[:, pl.ds(0, 3)]),
        ((slice(None), pl.ds(rows - 1, 1)), edge.at[:, pl.ds(3, 1)]),
        ((slice(None), inner, pl.ds(0, 8)), left),
        ((slice(None), inner, pl.ds(cols - 8, 8)), right),
    )
    enter = [pltpu.make_async_copy(part.at[at], ref, sem.at[i]) for i, (at, ref) in enumerate(places)]
    leave = [pltpu.make_async_copy(ref, out.at[at], sem.at[4 + i]) for i, (at, ref) in enumerate(places)]
    for copy in enter:
        copy.start()
    low, high = picker(g, row_ref, ahead, behind)
    bottom = row_ref[g.flags + BOTTOM]
    for copy in enter[:2]:
        copy.wait()
    for c in range(8):
        edge[c, 0] += 0.5 * low(c)
        edge[c, 3] += 0.5 * high(c)
    for e, share in ((1, 0.5 - 0.5 * bottom), (2, 0.5 * bottom)):
        edge[6, e] += share * low(8)
        for lines, k in ((lines_right, cols - 1), (lines_left, 0)):
            edge[6, e, k : k + 1, :] += share * lines[8:9, :]
    for e, right0, left0, second in ((0, 0, 0, 9), (3, 9, 10, 19)):
        for c in range(8):
            edge[c, e, cols - 1 : cols, :] += 0.5 * lines_right[right0 + c : right0 + c + 1, :]
            edge[c, e, 0:1, :] += 0.5 * lines_left[left0 + c : left0 + c + 1, :]
        edge[7, e, 1:2, :] += 0.5 * lines_left[second : second + 1, :]

    def columns(ref0, ref1, e, j):
        for c in range(8):
            ref0[c, e, 0:1, :] += 0.5 * from_left[c, pl.ds(j, 1), :]
            k = ref1.shape[2]
            ref1[c, e, k - 1 : k, :] += 0.5 * from_right[c, pl.ds(j, 1), :]
        ref0[7, e, 1:2, :] += 0.5 * from_left[8, pl.ds(j, 1), :]

    for e, j in ((0, 0), (1, 1), (2, 2), (3, rows - 1)):
        columns(edge, edge, e, j)
    for copy in leave[:2]:
        copy.start()
    for copy in enter[2:]:
        copy.wait()

    def step(e, carry):
        columns(left, right, e, e + 3)
        return carry

    lax.fori_loop(0, rows - 4, step, 0)
    for copy in leave[2:]:
        copy.start()
    for copy in leave:
        copy.wait()


ANY = pl.BlockSpec(memory_space=pl.ANY)
VMEM = pl.BlockSpec(memory_space=pltpu.VMEM)
SMEM = pl.BlockSpec(memory_space=pltpu.SMEM)


def call(kernel, ins, outs, scratch, flops, limit, interpret=False):
    return pl.pallas_call(
        kernel,
        out_shape=[jax.ShapeDtypeStruct(s, jnp.float32) for _, s in outs],
        in_specs=[SMEM] + ins,
        out_specs=[s for s, _ in outs],
        scratch_shapes=scratch,
        compiler_params=pltpu.CompilerParams(vmem_limit_bytes=limit << 20),
        cost_estimate=pl.CostEstimate(flops=flops, bytes_accessed=16 << 20, transcendentals=0),
        interpret=interpret,
    )


def buffers(*shapes):
    return [pltpu.VMEM(s, jnp.float32) for s in shapes]


def sizes(g):
    return (
        (8, g.rows, g.cols, g.rads),
        [(8, g.rows, g.rads), (9, g.rows, g.rads)],
        (9, g.cols, g.rads),
        (24, g.rads),
    )


def forward(g, table, own, halos, planes, interpret=False):
    n = g.slots
    shape, sides, body, lines = sizes(g)
    scratch = buffers((8, 2, n, LANES), (15, 2, n, LANES), (6, n, LANES), (10, 2, n, LANES), shape)
    dma = pltpu.SemaphoreType.DMA
    scratch += [dma((g.rows, 2)), dma((g.rows,))]
    outs = [(ANY, shape)] + [(VMEM, s) for s in sides + [body, body]]
    run = call(functools.partial(forward_kernel, g), [ANY] + [VMEM] * 7, outs, scratch, 10**8, 48, interpret)
    return run(table, own, *halos, planes)


def adjoint(g, table, own, halos, cot, planes, received=(), interpret=False):
    n = g.slots
    shape, sides, body, lines = sizes(g)
    message = (10, g.cols, g.rads)
    outs = [(ANY, shape)] + [(VMEM, s) for s in sides + [message, message]]
    scratch = buffers(
        (8, 2, n, LANES),
        (8, 2, n, LANES),
        (13, 2, n, LANES),
        (3, 2, n, LANES),
        (2, n, LANES),
        (11, 2, g.width, LANES),
        (11, 2, 8 + PULL_SLOTS, LANES),
        shape,
    )
    dma = pltpu.SemaphoreType.DMA
    scratch += [dma((g.rows, 2)), dma((g.rows, 2)), dma((g.rows,)), dma((g.rows,))]
    ins = [ANY, ANY] + [VMEM] * 7 + ([ANY] + [VMEM] * 6 if received else [])
    run = call(functools.partial(adjoint_kernel, g, bool(received)), ins, outs, scratch, 3 * 10**8, 48, interpret)
    return run(table, own, cot, *halos, planes, *received)


def pack(g, table, state):
    shape, sides, body, lines = sizes(g)
    strip = (8, g.rows, 8, g.rads)
    scratch = buffers((8, 4, g.cols, g.rads), strip, strip) + [pltpu.SemaphoreType.DMA((4,))]
    outs = [(VMEM, s) for s in sides + [body, body]]
    return call(functools.partial(pack_kernel, g), [ANY], outs, scratch, 10**6, 58)(table, state)


def pack_corners(g, table, phlo, phhi):
    lines = sizes(g)[3]
    return call(functools.partial(pack_corner_kernel, g), [VMEM] * 2, [(VMEM, lines)] * 2, [], 10**6, 16)(
        table, phlo, phhi
    )


def turn(g, table, ahead, behind):
    lines = sizes(g)[3]
    return call(functools.partial(turn_kernel, g), [VMEM] * 2, [(VMEM, lines)] * 2, [], 10**6, 16)(
        table, ahead, behind
    )


def finish(g, table, part, *received):
    strip = (8, g.rows - 4, 8, g.rads)
    return pl.pallas_call(
        functools.partial(finish_kernel, g),
        out_shape=jax.ShapeDtypeStruct(part.shape, jnp.float32),
        in_specs=[SMEM, ANY] + [VMEM] * 6,
        out_specs=ANY,
        input_output_aliases={1: 0},
        scratch_shapes=buffers((8, 4, g.cols, g.rads), strip, strip) + [pltpu.SemaphoreType.DMA((8,))],
        compiler_params=pltpu.CompilerParams(vmem_limit_bytes=44 << 20),
        cost_estimate=pl.CostEstimate(flops=10**6, bytes_accessed=7 << 20, transcendentals=0),
    )(table, part, *received)


class Place:
    def __init__(self):
        self.n_th, self.n_ph = lax.axis_size("th"), lax.axis_size("ph")
        n_th, n_ph = self.n_th, self.n_ph
        half = n_ph // 2
        self.th, self.ph = lax.axis_index("th"), lax.axis_index("ph")
        self.at_bottom, self.at_top = self.th == 0, self.th == n_th - 1
        self.near = self.ph < half
        self.right = [(i, (i + 1) % n_ph) for i in range(n_ph)]
        self.left = [(j, i) for i, j in self.right]
        self.round = []
        for t in range(n_th):
            for p in range(half):
                self.round.append((t * n_ph + p, (t + 1) * n_ph + p if t < n_th - 1 else t * n_ph + p + half))
                self.round.append((t * n_ph + p + half, (t - 1) * n_ph + p + half if t > 0 else p))
        self.back = [(j, i) for i, j in self.round]

    def polar(self, ahead, behind):
        both = ("th", "ph")
        return lax.ppermute(ahead, both, self.round), lax.ppermute(behind, both, self.back)

    def sideways(self, to_right, to_left):
        return lax.ppermute(to_right, "ph", self.right), lax.ppermute(to_left, "ph", self.left)


def shards(state, cotangent):
    place = Place()
    _, rows, cols, rads = state.shape
    g = Grid(rows, cols, rads, rows * place.n_th, cols * place.n_ph)
    flags = jnp.stack([place.at_bottom, place.at_top, place.near]).astype(jnp.float32)
    table = lax.dynamic_slice_in_dim(jnp.asarray(g.row_table()), place.th * rows, rows + 5, 0).reshape(-1)
    table = jnp.concatenate([table, flags])
    planes = jnp.asarray(g.radial_planes())

    def halos_of(last, first, ahead, behind):
        phlo, phhi = place.sideways(last, first)
        body = place.polar(ahead, behind)
        return (phlo, phhi) + tuple(body) + tuple(place.polar(*pack_corners(g, table, phlo, phhi)))

    def give_back(parts):
        gphlo, gphhi, ahead, behind = parts
        from_left, from_right = place.sideways(gphhi, gphlo)
        ahead, behind = place.polar(ahead, behind)
        to_left, to_right = turn(g, table, ahead, behind)
        lines_left, lines_right = place.sideways(to_right, to_left)
        return ahead, behind, from_right, from_left, lines_right, lines_left

    halos_zero = halos_of(*pack(g, table, state))
    moved, *rims = forward(g, table, state, halos_zero, planes)
    halos_one = halos_of(*rims)
    part, *ghosts = adjoint(g, table, moved, halos_one, cotangent, planes)
    part, *ghosts = adjoint(g, table, state, halos_zero, part, planes, (cotangent,) + give_back(ghosts))
    return finish(g, table, part, *give_back(ghosts))


def solution(mesh):
    placed = (P(None, "th", "ph", None), P(None, "th", "ph", None))
    return jax.shard_map(
        shards, mesh=mesh, in_specs=placed, out_specs=P(None, "th", "ph", None), check_vma=False
    )
```

```python
import functools
import math

import jax
import jax.numpy as jnp
import numpy as np
from jax import lax
from jax.experimental import pallas as pl
from jax.experimental.pallas import tpu as pltpu
from jax.sharding import PartitionSpec as P

GAMMA = 5.0 / 3.0
R_INNER = 1.0
R_OUTER = 3.0
COURANT = 0.4
SPEED_BOUND = 5.0
PRESSURE_SOFT = 0.05
THETA_CUT = 0.1

G1 = GAMMA - 1.0
LANES = 128
PAD = 32
FACE_SLOTS = 32
FLIPS = (1.0, 1.0, -1.0, -1.0, 1.0, 1.0, -1.0, -1.0)
SH, SL, AZ, COT, AK, KEEP, N_ROW = 0, 1, 2, 3, 4, 5, 6
BOTTOM, TOP_END, NEAR = 0, 1, 2
INV_V, R_HI2, K_V, INV_MID, INV_LO, LO, HI, INV_SHELL, HALF_HI2, HALF_KV, HALF_LO2, TOP, OPEN = range(13)


class Grid:
    def __init__(self, rows, cols, rads, total_rows, total_cols):
        self.rows, self.cols, self.rads = rows, cols, rads
        self.width = cols + 8
        self.tiles = self.width // 8
        self.slots = PAD + (rows + 4) * self.width + PAD
        self.dth = (math.pi - 2.0 * THETA_CUT) / total_rows
        self.dph = 2.0 * math.pi / total_cols
        self.dr = (R_OUTER - R_INNER) / rads
        self.dt = COURANT * min(self.dr, R_INNER * math.sin(THETA_CUT) * self.dph) / SPEED_BOUND
        self.total_rows = total_rows

    def at(self, j, k):
        return PAD + (j + 2) * self.width + k

    def row_table(self):
        j = np.arange(-2, self.total_rows + 3, dtype=np.float64)
        low = THETA_CUT + j * self.dth
        high, mid = low + self.dth, low + 0.5 * self.dth
        drop = np.cos(low) - np.cos(high)
        keep = np.where((j == 0) | (j == self.total_rows), 0.0, 1.0)
        safe = np.where(np.abs(np.sin(low)) < 1e-6, 1.0, np.sin(low))
        table = np.zeros((len(j), N_ROW))
        table[:, SH] = np.sin(high) / drop
        table[:, SL] = np.sin(low) / drop
        table[:, AZ] = self.dth / (drop * self.dph)
        table[:, COT] = np.cos(mid) / np.sin(mid)
        table[:, AK] = keep / (safe * self.dph)
        table[:, KEEP] = keep
        return table.astype(np.float32)

    @property
    def flags(self):
        return (self.rows + 5) * N_ROW

    def radial_planes(self):
        i = np.arange(self.rads, dtype=np.float64)
        low = R_INNER + i * self.dr
        high, mid = low + self.dr, low + 0.5 * self.dr
        vol = (high**3 - low**3) / 3.0
        shell = 0.5 * (high**2 - low**2)
        top = np.where(i == self.rads - 1, 2.0, 1.0)
        planes = [None] * 13
        planes[INV_V] = 1.0 / vol
        planes[R_HI2] = high**2
        planes[K_V] = shell / vol
        planes[INV_MID] = 1.0 / mid
        planes[INV_LO] = 1.0 / low
        planes[LO] = low
        planes[HI] = high
        planes[INV_SHELL] = 1.0 / shell
        planes[HALF_HI2] = 0.5 * self.dt * high**2
        planes[HALF_KV] = 0.5 * self.dt * shell / vol
        planes[HALF_LO2] = 0.5 * self.dt * low**2
        planes[TOP] = top
        planes[OPEN] = 2.0 - top
        stack = np.stack(planes).astype(np.float32).reshape(13, 2, 1, LANES)
        return np.broadcast_to(stack, (13, 2, 8, LANES)).copy()


def lane_index(x):
    return lax.broadcasted_iota(jnp.int32, x.shape, 2)


def next_r(x, last=None):
    turned = pltpu.roll(x, LANES - 1, 2)
    end = x[1:2] if last is None else last
    return jnp.where(lane_index(x) == LANES - 1, jnp.concatenate([turned[1:2], end], 0), turned)


def prev_r(x, first):
    turned = pltpu.roll(x, 1, 2)
    return jnp.where(lane_index(x) == 0, jnp.concatenate([first, turned[0:1]], 0), turned)


def split(x):
    return jnp.stack([x[:, :LANES], x[:, LANES:]])


def load(ref, field, slot, size=8):
    return ref[field, :, pl.ds(slot, size), :]


def put(ref, field, slot, value):
    ref[field, :, pl.ds(slot, value.shape[1]), :] = value


def loader(size):
    return lambda ref, field, slot: load(ref, field, slot, size)


def planes_of(rc, size):
    return lambda i: jnp.concatenate([rc[i]] * (size // 8), 1)


def put_line(ref, field, slot, line):
    ref[field, 0, pl.ds(slot, 1), :] = line[:, :LANES]
    ref[field, 1, pl.ds(slot, 1), :] = line[:, LANES:]


def get_line(ref, field, slot):
    return jnp.concatenate([ref[field, 0, pl.ds(slot, 1), :], ref[field, 1, pl.ds(slot, 1), :]], 1)


def put_column(g, ref, field, k, value):
    ref[field, :, pl.ds(g.at(0, k), g.rows, stride=g.width), :] = value


def column_of(g, ref, field, k, row=0):
    return ref[field, :, pl.ds(g.at(row, k), g.rows, stride=g.width), :]


def picker(g, row_ref, ahead, behind):
    near = row_ref[g.flags + NEAR] > 0.5

    def low(*at):
        return jnp.where(near, ahead[at], behind[at])

    def high(*at):
        return jnp.where(near, behind[at], ahead[at])

    return low, high


def row_copies(g, hbm, ref, sem, row=None, parts=slice(None)):
    for j in range(g.rows) if row is None else (row,):
        for h in range(2):
            yield pltpu.make_async_copy(
                hbm.at[parts, j, :, pl.ds(h * LANES, LANES)], ref.at[:, h, pl.ds(g.at(j, 0), g.cols), :], sem.at[j, h]
            )


def fill_state(g, us, row_ref, halos):
    rows, cols = g.rows, g.cols
    phlo, phhi, ahead, behind, corner_ahead, corner_behind = halos
    low, high = picker(g, row_ref, ahead, behind)
    corner_low, corner_high = picker(g, row_ref, corner_ahead, corner_behind)
    calm = [jnp.full((2, 8, LANES), 1.0 if c == 0 else 0.0, jnp.float32) for c in range(8)]

    def keep(j):
        return row_ref[(j + 2) * N_ROW + KEEP]

    def ends(j, fetch):
        for c in range(8):
            scale = keep(j) if c == 6 else None
            for which, k in ((0, -1), (1, cols)):
                line = fetch(c, which)
                put_line(us, c, g.at(j, k), line if scale is None else line * scale)
        put_line(us, 7, g.at(j, cols + 1), fetch(7, 2))

    def body_row(j, side):
        for c in range(8):
            for t in range(cols // 8):
                x = split(side(c, slice(t * 8, t * 8 + 8)))
                put(us, c, g.at(j, t * 8), x * keep(j) if c == 6 else x)

    def still(n, carry):
        for c in range(8):
            put(us, c, pl.multiple_of(g.at(-2, cols) + n * g.width, 8), calm[c])
        return carry

    lax.fori_loop(0, rows + 3, still, 0)
    body_row(-1, low)
    ends(-1, lambda c, w: corner_low(slice((c, 9 + c, 18)[w], (c, 9 + c, 18)[w] + 1)))

    for c in range(8):
        put_column(g, us, c, -1, split(phlo[c]))
        put_column(g, us, c, cols, split(phhi[c]))
    put_column(g, us, 7, cols + 1, split(phhi[8]))
    for ref, k in ((phlo, -1), (phhi, cols)):
        put_line(us, 6, g.at(0, k), ref[6, 0:1, :] * keep(0))
    body_row(rows, high)
    ends(rows, lambda c, w: corner_high(slice((c, 9 + c, 18)[w], (c, 9 + c, 18)[w] + 1)))
    far = keep(rows + 1)
    for t in range(g.tiles):
        x = split(high(8, slice(t * 8, t * 8 + 8))) if t < cols // 8 else calm[1]
        put(us, 6, g.at(rows + 1, t * 8), x * far)
    put_line(us, 6, g.at(rows + 1, -1), corner_high(slice(8, 9)) * far)
    put_line(us, 6, g.at(rows + 1, cols), corner_high(slice(17, 18)) * far)

def arrive(g, us, row_ref, own, sem, j):
    for copy in row_copies(g, own, us, sem, j):
        copy.wait()
    if isinstance(j, int) and j == 0:
        for t in range(g.cols // 8):
            put(us, 6, g.at(0, t * 8), load(us, 6, g.at(0, t * 8)) * row_ref[2 * N_ROW + KEEP])


def cell_values(g, us, p, size):
    load = loader(size)
    rho, m0, m1, m2, energy, u5, u6, u7 = [load(us, c, p) for c in range(8)]
    b0 = 0.5 * (u5 + next_r(u5))
    b1 = 0.5 * (u6 + load(us, 6, p + g.width))
    b2 = 0.5 * (u7 + load(us, 7, p + 1))
    q = 1.0 / rho
    v0, v1, v2 = m0 * q, m1 * q, m2 * q
    square = b0 * b0 + b1 * b1 + b2 * b2
    pressure = G1 * (energy - 0.5 * (m0 * v0 + m1 * v1 + m2 * v2) - 0.5 * square)
    total = pressure + 0.5 * square
    soft = pressure * pressure + PRESSURE_SOFT * PRESSURE_SOFT
    inv_soft = lax.rsqrt(soft)
    c2 = (GAMMA * (soft * inv_soft) + square) * q
    return (m0, m1, m2), (v0, v1, v2), (b0, b1, b2), u5, q, pressure, total, energy + total, inv_soft, c2


def forward_kernel(g, row_ref, own, *refs):
    halos, rc, refs = refs[:6], refs[6], refs[7:]
    out, last_col, first_col, go_ahead, go_behind, us, cf, gf, ff, stage, sem, sem_out = refs
    for copy in row_copies(g, own, us, sem):
        copy.start()
    fill_state(g, us, row_ref, halos)
    w = g.width
    wide = w
    arrive(g, us, row_ref, own, sem, 0)

    def cells(n, carry):
        p = pl.multiple_of(g.at(-1, -8) + n * wide, 8)

        @pl.when((n > 0) & (n < g.rows))
        def _():
            arrive(g, us, row_ref, own, sem, n)

        m, v, b, u5, q, pressure, total, h, inv_soft, c2 = cell_values(g, us, p, wide)
        put(cf, 0, p, m[0] * v[0] - b[0] * b[0] + total)
        put(cf, 1, p, m[0] * v[1] - b[0] * b[1])
        put(cf, 2, p, m[0] * v[2] - b[0] * b[2])
        put(cf, 3, p, m[1] * v[1] - b[1] * b[1] + total)
        put(cf, 4, p, m[1] * v[2] - b[1] * b[2])
        put(cf, 5, p, m[2] * v[2] - b[2] * b[2] + total)
        vb = v[0] * b[0] + v[1] * b[1] + v[2] * b[2]
        for d in range(3):
            put(cf, 6 + d, p, h * v[d] - b[d] * vb)
            put(cf, 9 + d, p, v[d] * v[d] + c2)
        put(cf, 12, p, v[2] * b[1] - v[1] * b[2])
        put(cf, 13, p, v[0] * b[2] - v[2] * b[0])
        put(cf, 14, p, v[1] * b[0] - v[0] * b[1])
        m, v, b = [[x[0:1] for x in y] for y in (m, v, b)]
        bg = u5[0:1]
        gain = (1.0 - 0.5 * GAMMA) * (bg * bg - b[0] * b[0])
        vbg = vb[0:1] + v[0] * (bg - b[0])
        ghost = (
            m[0] * v[0] - bg * bg + total[0:1] + gain,
            m[0] * v[1] - bg * b[1],
            m[0] * v[2] - bg * b[2],
            (h[0:1] + gain) * v[0] - bg * vbg,
            v[0] * b[2] - v[2] * bg,
            v[1] * bg - v[0] * b[1],
        )
        for f, x in enumerate(ghost):
            gf[f, pl.ds(p, wide), :] = x[0]
        return carry

    lax.fori_loop(0, g.rows + 3, cells, 0)

    index = ((0, 1, 2), (1, 3, 4), (2, 4, 5))

    def face(d, p, shift, size):
        load = loader(size)
        fluxes = [load(us, 1 + d, p)] + [load(cf, index[d][c], p) for c in range(3)] + [load(cf, 6 + d, p)]
        speed = load(cf, 9 + d, p)
        state = [load(us, c, p) for c in range(5)]
        if shift is None:
            other = [next_r(x) for x in fluxes]
            speed2 = next_r(speed)
            state2 = [other[0] if c == 1 else next_r(state[c]) for c in range(5)]
        else:
            r = p + shift
            other = [load(us, 1 + d, r)] + [load(cf, index[d][c], r) for c in range(3)] + [load(cf, 6 + d, r)]
            speed2 = load(cf, 9 + d, r)
            state2 = [load(us, c, r) for c in range(5)]
        total = 0.5 * (speed + speed2)
        half = 0.5 * (total * lax.rsqrt(total))
        return fluxes, [0.5 * (fluxes[c] + other[c]) - half * (state2[c] - state[c]) for c in range(5)]

    def faces(n, carry):
        p = pl.multiple_of(g.at(-1, 0) + n * FACE_SLOTS, 8)
        for d, shift, base in ((1, w, 0), (2, 1, 5)):
            _, flux = face(d, p, shift, FACE_SLOTS)
            for c in range(5):
                put(ff, base + c, p, flux[c])
        return carry

    lax.fori_loop(0, (g.rows + 1) * g.width // FACE_SLOTS, faces, 0)

    size = g.cols
    load = loader(size)
    plane = planes_of(rc, size)

    def leave(j):
        return pltpu.make_async_copy(stage.at[:, j], out.at[:, j], sem_out.at[j])

    def combine(j, carry):
        p = pl.multiple_of(g.at(j, 0), 8)
        row = (j + 2) * N_ROW
        sh, sl, az, cot, ak, keep = [row_ref[row + i] for i in range(N_ROW)]
        cells_here, flux_r = face(0, p, None, size)
        ghost = [load(us, 1, p)[0:1]] + [gf[f, pl.ds(p, size), :][None] for f in range(4)]
        inv_v, kv = plane(INV_V), plane(K_V)
        rates = []
        for c in range(5):
            high = plane(R_HI2) * flux_r[c]
            first = 0.5 * plane(HALF_LO2)[0:1] * (2.0 / g.dt) * (ghost[c] + cells_here[c][0:1])
            low = prev_r(high, first)
            th = sh * load(ff, c, p) - sl * load(ff, c, p - w)
            ph = az * (load(ff, 5 + c, p) - load(ff, 5 + c, p - 1))
            rates.append(-(inv_v * (high - low) + kv * (th + ph)))
        tt = [load(cf, f, p) for f in range(1, 6)]
        mid = plane(INV_MID)
        rates[1] = rates[1] + (tt[2] + tt[4]) * mid
        rates[2] = rates[2] + (cot * tt[4] - tt[0]) * mid
        rates[3] = rates[3] - (tt[1] + cot * tt[3]) * mid
        ep, ept = load(cf, 14, p), load(cf, 14, p + w)
        x0 = load(cf, 14, p - w) + ep
        x1 = ep + ept
        g_here = gf[5, pl.ds(p, size), :][None]
        x0m = prev_r(x0, gf[5, pl.ds(p - w, size), :][None] + g_here)
        x1m = prev_r(x1, g_here + gf[5, pl.ds(p + w, size), :][None])
        z0 = 0.25 * (x0 + x0m)
        zr = 0.25 * (next_r(x0) + x0)
        z1 = 0.25 * (x1 + x1m)
        et = load(cf, 13, p)
        y0 = load(cf, 13, p - 1) + et
        y1 = et + load(cf, 13, p + 1)
        g_here = gf[4, pl.ds(p, size), :][None]
        y0m = prev_r(y0, gf[4, pl.ds(p - 1, size), :][None] + g_here)
        y1m = prev_r(y1, g_here + gf[4, pl.ds(p + 1, size), :][None])
        p0 = 0.25 * (y0 + y0m)
        pr = 0.25 * (next_r(y0) + y0)
        p1 = 0.25 * (y1 + y1m)
        er, era, erb = load(cf, 12, p), load(cf, 12, p - 1), load(cf, 12, p - w)
        r0 = 0.25 * (er + era + erb + load(cf, 12, p - w - 1))
        r1 = 0.25 * (load(cf, 12, p + 1) + er + load(cf, 12, p - w + 1) + erb)
        rt = 0.25 * (load(cf, 12, p + w) + load(cf, 12, p + w - 1) + er + era)
        lo, hi, shell = plane(LO), plane(HI), plane(INV_SHELL)
        rates.append(-plane(INV_LO) * (sh * z1 - sl * z0 - az * (p1 - p0)))
        rates.append(-shell * (g.dr * ak * (r1 - r0) - keep * (hi * zr - lo * z0)))
        rates.append(shell * ((g.dr / g.dth) * (rt - r0) - (hi * pr - lo * p0)))
        for c in range(8):
            new = load(us, c, p) + g.dt * rates[c]
            stage[c, j] = jnp.concatenate([new[0], new[1]], 1)
        leave(j).start()
        for c in range(8):
            last_col[c, pl.ds(j, 1), :] = stage[c, j, g.cols - 1 : g.cols, :]
            first_col[c, pl.ds(j, 1), :] = stage[c, j, 0:1, :]
        first_col[8, pl.ds(j, 1), :] = stage[7, j, 1:2, :]
        return carry

    lax.fori_loop(0, g.rows, combine, 0)

    send_rows(g, row_ref, lambda c, j: stage[c, j], go_ahead, go_behind)

    def settle(j, carry):
        leave(j).wait()
        return carry

    lax.fori_loop(0, g.rows, settle, 0)


def cell_pass(g, us, row_ref, own, sem, cf):
    w, rows = g.width, g.rows
    arrive(g, us, row_ref, own, sem, 0)

    def cells(n, carry):
        p = pl.multiple_of(g.at(-1, -8) + n * w, 8)

        @pl.when((n > 0) & (n < rows))
        def _():
            arrive(g, us, row_ref, own, sem, n)

        m, v, b, u5, q, pressure, total, h, inv_soft, c2 = cell_values(g, us, p, w)
        for d in range(3):
            put(cf, d, p, v[d])
            put(cf, 3 + d, p, b[d])
            put(cf, 6 + d, p, v[d] * v[d] + c2)
        put(cf, 9, p, h)
        put(cf, 10, p, q)
        put(cf, 11, p, GAMMA * q * (pressure * inv_soft))
        put(cf, 12, p, c2 * q)
        return carry

    lax.fori_loop(0, rows + 3, cells, 0)


def edge_pass(g, row_ref, rc, cs, base, ef, zf):
    w, rows = g.width, g.rows
    zero = jnp.zeros((2, 8, LANES), jnp.float32)
    for f in range(3):
        put(ef, f, g.at(-1, -8), zero)
    for f in range(2):
        zf[f, pl.ds(g.at(-1, -8), 8), :] = zero[0]

    def edges(n, carry):
        load = loader(w)
        plane = planes_of(rc, w)
        none = jnp.zeros((1, w, LANES), jnp.float32)
        p = pl.multiple_of(g.at(-1, 0) + n * w, 8)
        j = n - 1
        row = (j + 2) * N_ROW
        sl, az, ak, keep = [row_ref[row + i] for i in (SL, AZ, AK, KEEP)]
        sh_below = row_ref[row - N_ROW + SH]
        shell, lo, hi = plane(INV_SHELL), plane(LO), plane(HI)
        c5, c6, c7 = load(cs, base, p), load(cs, base + 1, p), load(cs, base + 2, p)
        rb = ak * (c6 - load(cs, base + 1, p - 1)) + (1.0 / g.dth) * (load(cs, base + 2, p - w) - c7)
        put(ef, 0, p, (0.25 * g.dt * g.dr) * shell * rb)
        q6 = keep * c6 * shell
        zb = plane(INV_LO) * (sl * c5 - sh_below * load(cs, base, p - w)) + prev_r(hi * q6, none) - lo * q6
        q7 = c7 * shell
        hq7 = hi * q7
        pb = plane(INV_LO) * az * (load(cs, base, p - 1) - c5) + lo * q7 - prev_r(hq7, none)
        zl = 2.0 * hi[1:2] * q6[1:2]
        plast = -2.0 * hq7[1:2]
        put(ef, 1, p, (0.25 * g.dt) * (zb + next_r(zb, zl)))
        put(ef, 2, p, (0.25 * g.dt) * (pb + next_r(pb, plast)))
        zf[0, pl.ds(p, w), :] = (0.25 * g.dt) * zb[0]
        zf[1, pl.ds(p, w), :] = (0.25 * g.dt) * pb[0]
        return carry

    lax.fori_loop(0, rows + 3, edges, 0)


def clear_ghosts(g, cs, count):
    zero = jnp.zeros((2, 8, LANES), jnp.float32)
    for j in (-2, -1, g.rows, g.rows + 1):
        for c in range(count):
            for t in range(g.tiles):
                put(cs, c, g.at(j, t * 8), zero)
    for c in range(count):
        put(cs, c, g.at(-2, -8), zero)

    def clear(j, carry):
        for c in range(count):
            put(cs, c, g.at(j, g.cols), zero)
        return carry

    lax.fori_loop(0, g.rows, clear, 0)


def edge_kernel(g, row_ref, cot, rc, ef_out, zf_out, cs, ef, zf, sem, sem_out):
    for copy in row_copies(g, cot, cs, sem, parts=pl.ds(5, 3)):
        copy.start()
    clear_ghosts(g, cs, 3)
    for copy in row_copies(g, cot, cs, sem, parts=pl.ds(5, 3)):
        copy.wait()
    edge_pass(g, row_ref, rc, cs, 0, ef, zf)
    leave = [pltpu.make_async_copy(ef, ef_out, sem_out.at[0]), pltpu.make_async_copy(zf, zf_out, sem_out.at[1])]
    for copy in leave:
        copy.start()
    for copy in leave:
        copy.wait()


def cell_pull(load, plane, us, cf, p, fr_, ft_, fp_, ub, sb, sources, cot, e, first, ghost_e):
    none = jnp.zeros_like(first[0])
    w1, w2, w3 = sources
    e0, e1, e2 = e
    s00, s11 = fr_[1], ft_[2] + w1
    s22 = fp_[3] + w1 + cot * w2
    s01 = fr_[2] + ft_[1] - w2
    s02 = fr_[3] + fp_[1] - w3
    s12 = ft_[3] + fp_[2] - cot * w3
    v = [load(cf, d, p) for d in range(3)]
    b = [load(cf, 3 + d, p) for d in range(3)]
    h, q = load(cf, 9, p), load(cf, 10, p)
    gg = (fr_[4], ft_[4], fp_[4])
    flow = v[0] * gg[0] + v[1] * gg[1] + v[2] * gg[2]
    beta = b[0] * gg[0] + b[1] * gg[1] + b[2] * gg[2]
    vb = v[0] * b[0] + v[1] * b[1] + v[2] * b[2]
    d00, d11, d22 = s00 + s00, s11 + s11, s22 + s22
    sv = (
        d00 * v[0] + s01 * v[1] + s02 * v[2],
        s01 * v[0] + d11 * v[1] + s12 * v[2],
        s02 * v[0] + s12 * v[1] + d22 * v[2],
    )
    sbm = (
        d00 * b[0] + s01 * b[1] + s02 * b[2],
        s01 * b[0] + d11 * b[1] + s12 * b[2],
        s02 * b[0] + s12 * b[1] + d22 * b[2],
    )
    c2b = sb[0] + sb[1] + sb[2]
    ptb = s00 + s11 + s22 + flow
    pb = c2b * load(cf, 11, p) + ptb
    pg = G1 * pb
    bbb = 2.0 * (c2b * q) + ptb - pg
    bxe = (b[1] * e2 - b[2] * e1, b[2] * e0 - b[0] * e2, b[0] * e1 - b[1] * e0)
    exv = (e1 * v[2] - e2 * v[1], e2 * v[0] - e0 * v[2], e0 * v[1] - e1 * v[0])
    rho_bar = ub[0] - c2b * load(cf, 12, p)
    m_bar, b_bar = [], []
    for d in range(3):
        vbar = h * gg[d] - beta * b[d] + 2.0 * (v[d] * sb[d]) - bxe[d]
        turn = q * vbar - pg * v[d]
        f0 = (fr_[0], ft_[0], fp_[0])[d]
        m_bar.append(ub[1 + d] + f0 + sv[d] + turn)
        rho_bar = rho_bar - v[d] * (0.5 * sv[d] + turn + 0.5 * (pg * v[d]))
        b_bar.append(b[d] * bbb - sbm[d] - vb * gg[d] - beta * v[d] - exv[d])
    e_bar = ub[4] + flow + pg

    first_lane = lax.broadcasted_iota(jnp.int32, none.shape, 2) == 0
    v, b = [[x[0:1] for x in y] for y in (v, b)]
    q, h = q[0:1], h[0:1]
    bg = load(us, 5, p)[0:1]
    h = h + (1.0 - 0.5 * GAMMA) * (bg * bg - b[0] * b[0])
    vbg = vb[0:1] + v[0] * (bg - b[0])
    s00, s01, s02, g0 = first[1], first[2], first[3], first[4]
    e1, e2 = ghost_e
    flow = v[0] * g0
    beta = bg * g0
    pb = s00 + flow
    pg = G1 * pb
    bbb = pb - pg
    d00 = s00 + s00
    sv = (d00 * v[0] + s01 * v[1] + s02 * v[2], s01 * v[0], s02 * v[0])
    sbm = (d00 * bg + s01 * b[1] + s02 * b[2], s01 * bg, s02 * bg)
    vbar = (
        h * g0 - beta * bg - (b[1] * e2 - b[2] * e1),
        bg * e2 - beta * b[1],
        -(beta * b[2]) - bg * e1,
    )
    exv = (e1 * v[2] - e2 * v[1], e2 * v[0], -(e1 * v[0]))
    more = [None] * 8
    rho_more = none
    for d in range(3):
        turn = q * vbar[d] - pg * v[d]
        more[1 + d] = sv[d] + turn + (first[0] if d == 0 else 0.0)
        rho_more = rho_more - v[d] * (0.5 * sv[d] + turn + 0.5 * (pg * v[d]))
        bd = bg if d == 0 else b[d]
        more[5 + d] = bd * bbb - sbm[d] - beta * v[d] - exv[d]
    more[5] = more[5] - vbg * g0
    more[0] = rho_more
    more[4] = flow + pg

    def with_first(x, extra):
        return x + jnp.concatenate([jnp.where(first_lane, extra, 0.0), none], 0)

    radial = 0.5 * (plane(TOP) * b_bar[0] + prev_r(b_bar[0], 2.0 * more[5]))
    values = [with_first(rho_bar, more[0])] + [with_first(m_bar[d], more[1 + d]) for d in range(3)]
    return values + [
        with_first(e_bar, more[4]),
        radial,
        with_first(b_bar[1], more[6]),
        with_first(b_bar[2], more[7]),
    ]


def face_pull(halves, state, state2, speed, speed2, closed=None):
    total = 0.5 * (speed + speed2)
    inv = lax.rsqrt(total)
    a = total * inv
    if closed is not None:
        a = a * closed
    dot = halves[0] * (state2[0] - state[0])
    for c in range(1, 5):
        dot = dot + halves[c] * (state2[c] - state[c])
    return halves + [a * x for x in halves] + [-0.25 * inv * dot]


def adjoint_kernel(g, received, row_ref, own, cot, *refs):
    halos, rc, refs = refs[:6], refs[6], refs[7:]
    if received:
        base, *got = refs[:7]
        refs = refs[7:]
    else:
        ef_in, zf_in = refs[:2]
        refs = refs[2:]
    out, gphlo, gphhi, go_ahead, go_behind, us, cs, cf, ef, zf, ft, fp, stage, line_lo, held, az_col, *refs = refs
    sem, sem_cot, sem_out, sem_base = refs
    w, rows, cols = g.width, g.rows, g.cols
    load = loader(8)
    for copy in row_copies(g, own, us, sem):
        copy.start()
    for copy in row_copies(g, cot, cs, sem_cot):
        copy.start()

    def enter(j):
        return pltpu.make_async_copy(base.at[:, j], stage.at[:, j], sem_base.at[j])

    if received:
        for j in range(rows):
            enter(j).start()
    zero = jnp.zeros((2, 8, LANES), jnp.float32)
    clear_ghosts(g, cs, 8)
    if not received:
        enter_edges = [
            pltpu.make_async_copy(ef_in, ef, sem_base.at[0]),
            pltpu.make_async_copy(zf_in, zf, sem_base.at[1]),
        ]
        for copy in enter_edges:
            copy.start()
    fill_state(g, us, row_ref, halos)
    cell_pass(g, us, row_ref, own, sem, cf)
    for copy in row_copies(g, cot, cs, sem_cot):
        copy.wait()
    if received:
        back_ahead, back_behind, from_right, from_left, lines_right, lines_left = got
        low, high = picker(g, row_ref, back_ahead, back_behind)
        bottom = row_ref[g.flags + BOTTOM]

        def add_line(c, slot, line):
            put_line(cs, c, slot, get_line(cs, c, slot) + line)

        for k, ref in ((0, from_left), (cols - 1, from_right)):
            for c in range(8):
                put_column(g, cs, c, k, column_of(g, cs, c, k) + split(ref[c]))
        put_column(g, cs, 7, 1, column_of(g, cs, 7, 1) + split(from_left[8]))
        for t in range(cols // 8):
            at = slice(t * 8, t * 8 + 8)
            for c in range(8):
                p = g.at(0, t * 8)
                put(cs, c, p, load(cs, c, p) + split(low(c, at)))
                p = g.at(rows - 1, t * 8)
                put(cs, c, p, load(cs, c, p) + split(high(c, at)))
            for j, share in ((1, 1.0 - bottom), (2, bottom)):
                p = g.at(j, t * 8)
                put(cs, 6, p, load(cs, 6, p) + share * split(low(8, at)))
        for j, right0, left0, second in ((0, 0, 0, 9), (rows - 1, 9, 10, 19)):
            for c in range(8):
                add_line(c, g.at(j, cols - 1), lines_right[right0 + c : right0 + c + 1, :])
                add_line(c, g.at(j, 0), lines_left[left0 + c : left0 + c + 1, :])
            add_line(7, g.at(j, 1), lines_left[second : second + 1, :])
        for lines, k in ((lines_right, cols - 1), (lines_left, 0)):
            for j, share in ((1, 1.0 - bottom), (2, bottom)):
                add_line(6, g.at(j, k), share * lines[8:9, :])

    if received:
        edge_pass(g, row_ref, rc, cs, 5, ef, zf)
    else:
        for copy in enter_edges:
            copy.wait()

    size = cols
    load = loader(size)
    plane = planes_of(rc, size)
    none = jnp.zeros((1, size, LANES), jnp.float32)
    for f in range(11):
        for t in range(cols // 8):
            put(ft, f, t * 8, zero)

    def spread(j, carry):
        az_col[pl.ds(j, 1), :] = jnp.full((1, LANES), row_ref[(j + 2) * N_ROW + AZ], jnp.float32)
        return carry

    lax.fori_loop(0, rows, spread, 0)
    along = planes_of(rc, rows)

    def down(ref, field, slot):
        return ref[field, :, pl.ds(slot, rows, stride=w), :]

    def down_ghost(field, slot):
        return zf[field, pl.ds(slot, rows, stride=w), :][None]

    def column(k):
        p = g.at(0, k)
        left, right = (p, p + 1) if k < 0 else (p - 1, p)
        sign, source = (1.0, right) if k < 0 else (-1.0, left)
        kaz = (sign * along(HALF_KV)) * az_col[...][None]
        face = face_pull(
            [kaz * down(cs, c, source) for c in range(5)],
            [down(us, c, left) for c in range(5)],
            [down(us, c, right) for c in range(5)],
            down(cf, 8, left),
            down(cf, 8, right),
        )
        nil = jnp.zeros((2, rows, LANES), jnp.float32)
        nils = [nil] * 5
        ub = face[5:10] if k < 0 else [-x for x in face[5:10]]
        edge = p + 1 if k < 0 else p
        e = (down(ef, 0, edge) + down(ef, 0, edge + w), down(ef, 2, edge), nil)
        ghost_e = (down_ghost(1, edge), nil[0:1])
        first = [nil[0:1]] * 5
        values = cell_pull(
            down, along, us, cf, p, nils, nils, face[:5], ub, [nil, nil, face[10]], [nil] * 3, 0.0, e, first, ghost_e
        )
        return face, values

    face, values = column(-1)
    for f in range(11):
        line_lo[f] = jnp.zeros((2, rows + 8, LANES), jnp.float32)
        line_lo[f, :, 1 : rows + 1, :] = face[f]
    _, values_hi = column(cols)
    for c in range(8):
        us[c, :, pl.ds(g.at(0, -1), rows, stride=w), :] = values[c]
        held[c] = values_hi[c]
    for j in (-1, rows):
        for k in (-1, cols):
            p = g.at(j, k)
            e0 = get_line(ef, 0, p) + get_line(ef, 0, p + 1) + get_line(ef, 0, p + w) + get_line(ef, 0, p + w + 1)
            v1, v2, b1, b2, q = [get_line(cf, f, p) for f in (1, 2, 4, 5, 10)]
            m1, m2 = -(q * b2 * e0), q * b1 * e0
            blank = jnp.zeros_like(e0)
            for c, x in enumerate((-(v1 * m1 + v2 * m2), blank, m1, m2, blank, blank, e0 * v2, -(e0 * v1))):
                put_line(us, c, p, x)

    def pull(n, carry):
        p = pl.multiple_of(g.at(-1, 0) + n * w, 8)
        row = (n + 1) * N_ROW
        sh, az = [row_ref[row + i] for i in (SH, AZ)]
        sl_above = row_ref[row + N_ROW + SL]
        state = [load(us, c, p) for c in range(5)]
        cc = [load(cs, c, p) for c in range(5)]
        kd = plane(HALF_KV)
        kaz = kd * az
        face = face_pull(
            [kaz * (load(cs, c, p + 1) - cc[c]) for c in range(5)],
            state,
            [load(us, c, p + 1) for c in range(5)],
            load(cf, 8, p),
            load(cf, 8, p + 1),
        )
        for f in range(11):
            put(fp, f, 8, face[f])
            fp[f, :, 7:8, :] = line_lo[f, :, pl.ds(n, 1), :]
        up = kd * sl_above
        down_by = kd * sh
        pw = pl.multiple_of(p + jnp.where(n > rows, 0, w), 8)
        face = face_pull(
            [up * load(cs, c, pw) - down_by * cc[c] for c in range(5)],
            state,
            [load(us, c, pw) for c in range(5)],
            load(cf, 7, p),
            load(cf, 7, pw),
        )
        ft_ = [face[c] + load(ft, c, 0) for c in range(5)]
        ub = [cc[c] + face[5 + c] - load(ft, 5 + c, 0) for c in range(5)]
        sb1 = face[10] + load(ft, 10, 0)
        for f in range(11):
            put(ft, f, 0, face[f])
        per_volume = [plane(INV_V) * x for x in cc]
        half_hi = plane(HALF_HI2)
        speed = load(cf, 6, p)
        face = face_pull(
            [half_hi * (next_r(x, none) - x) for x in per_volume],
            state,
            [next_r(x) for x in state],
            speed,
            next_r(speed),
            plane(OPEN),
        )
        first = [plane(HALF_LO2)[0:1] * x[0:1] for x in per_volume]
        fr_ = [plane(TOP) * face[c] + prev_r(face[c], first[c]) for c in range(5)]
        ub = [ub[c] + (face[5 + c] - prev_r(face[5 + c], none)) for c in range(5)]
        sb0 = face[10] + prev_r(face[10], none)
        fp_ = [load(fp, c, 8) + load(fp, c, 7) for c in range(5)]
        ub = [ub[c] + (load(fp, 5 + c, 8) - load(fp, 5 + c, 7)) for c in range(5)]
        sb = [sb0, sb1, load(fp, 10, 8) + load(fp, 10, 7)]
        mid = plane(INV_MID) * g.dt
        sources = (cc[1] * mid, cc[2] * mid, cc[3] * mid)
        e = (
            load(ef, 0, p) + load(ef, 0, p + 1) + load(ef, 0, p + w) + load(ef, 0, p + w + 1),
            load(ef, 2, p) + load(ef, 2, p + 1),
            load(ef, 1, p) + load(ef, 1, p + w),
        )
        ghost_e = (
            (zf[1, pl.ds(p, size), :] + zf[1, pl.ds(p + 1, size), :])[None],
            (zf[0, pl.ds(p, size), :] + zf[0, pl.ds(p + w, size), :])[None],
        )
        cot = row_ref[row + COT]
        values = cell_pull(load, plane, us, cf, p, fr_, ft_, fp_, ub, sb, sources, cot, e, first, ghost_e)
        values[5] = values[5] + load(cs, 5, p)
        for c in range(8):
            put(us, c, p, values[c])
        return carry

    lax.fori_loop(0, rows + 2, pull, 0)
    for c in range(8):
        us[c, :, pl.ds(g.at(0, cols), rows, stride=w), :] = held[c]
    load = loader(8)

    def keep_of(j):
        return 0.5 * row_ref[(j + 2) * N_ROW + KEEP]

    def tile6(j, p):
        return keep_of(j) * (load(us, 6, p) + load(us, 6, p - w))

    def tile7(p):
        return 0.5 * (load(us, 7, p) + load(us, 7, p - 1))

    def join(x):
        return jnp.concatenate([x[0], x[1]], 1)

    def line_of(c, j, k):
        p = g.at(j, k)
        if c < 6:
            return get_line(us, c, p)
        if c == 6:
            here = get_line(us, 6, p)
            if isinstance(j, int) and j == -1:
                return keep_of(j) * here
            return keep_of(j) * (here + get_line(us, 6, p - w))
        here = get_line(us, 7, p)
        return 0.5 * here if k == -1 else 0.5 * (here + get_line(us, 7, p - 1))

    def leave(j):
        return pltpu.make_async_copy(stage.at[:, j], out.at[:, j], sem_out.at[j])

    def give(j, carry):
        if received:
            enter(j).wait()
        for t in range(cols // 8):
            p = g.at(j, t * 8)
            at = (j, slice(t * 8, t * 8 + 8))

            def leave_tile(c, x):
                stage[(c,) + at] = 0.5 * (stage[(c,) + at] + x) if received else x

            for c in range(6):
                leave_tile(c, join(load(us, c, p)))
            leave_tile(6, join(load(cs, 6, p) + tile6(j, p)))
            leave_tile(7, join(load(cs, 7, p) + tile7(p)))
        leave(j).start()
        return carry

    lax.fori_loop(0, rows, give, 0)
    for ref, k in ((gphlo, -1), (gphhi, cols)):
        for c in range(6):
            ref[c] = join(column_of(g, us, c, k))
        faces = join(0.5 * (column_of(g, us, 6, k) + column_of(g, us, 6, k, -1)))
        ref[6] = faces
        ref[6, 0:1, :] = faces[0:1] * row_ref[2 * N_ROW + KEEP]
    here = column_of(g, us, 7, cols)
    gphlo[7] = join(0.5 * column_of(g, us, 7, -1))
    gphhi[7] = join(0.5 * (here + column_of(g, us, 7, cols - 1)))
    gphhi[8] = join(0.5 * here)

    bottom, top = row_ref[g.flags + BOTTOM], row_ref[g.flags + TOP_END]
    near = row_ref[g.flags + NEAR] > 0.5

    def toward_low(of):
        signs = [1.0 if f > 0 else 1.0 - 2.0 * bottom for f in FLIPS]
        face = of(6)
        return [of(c) * signs[c] for c in range(6)] + [face * (1.0 - bottom), of(7) * signs[7], face * -bottom]

    def toward_high(of, far):
        signs = [1.0 if f > 0 else 1.0 - 2.0 * top for f in FLIPS]
        face = of(6) * (1.0 - top) - far * top
        return [of(c) * signs[c] for c in range(6)] + [face, of(7) * signs[7], far * (1.0 - top)]

    def send(at, low_value, high_value):
        go_ahead[at] = jnp.where(near, high_value, low_value)
        go_behind[at] = jnp.where(near, low_value, high_value)

    for t in range(cols // 8):
        p0, p1 = g.at(-1, t * 8), g.at(rows, t * 8)

        def tile_low(c):
            if c == 6:
                return join(keep_of(-1) * load(us, 6, p0))
            return join(load(us, c, p0) if c < 6 else tile7(p0))

        def tile_high(c):
            return join(load(us, c, p1) if c < 6 else tile6(rows, p1) if c == 6 else tile7(p1))

        lows = toward_low(tile_low)
        highs = toward_high(tile_high, join(keep_of(rows + 1) * load(us, 6, p1)))
        for c in range(9):
            send((c, slice(t * 8, t * 8 + 8)), lows[c], highs[c])
    for k, base in ((-1, 0), (cols, 9)):
        lows = toward_low(lambda c: line_of(c, -1, k))
        highs = toward_high(lambda c: line_of(c, rows, k), keep_of(rows + 1) * get_line(us, 6, g.at(rows, k)))
        for c in range(9):
            send((9, slice(base + c, base + c + 1)), lows[c], highs[c])
    send(
        (9, slice(18, 19)),
        (0.5 - bottom) * get_line(us, 7, g.at(-1, cols)),
        (0.5 - top) * get_line(us, 7, g.at(rows, cols)),
    )

    def settle(j, carry):
        leave(j).wait()
        return carry

    lax.fori_loop(0, rows, settle, 0)


def polar_nine(g, pole, of, low):
    signs = [1.0 if f > 0 else 1.0 - 2.0 * pole for f in FLIPS]
    values = [of(c, 0 if low else g.rows - 1) * signs[c] for c in range(8)]
    if low:
        values[6] = of(6, 0) * (1.0 - pole) - of(6, 2) * pole
        return values + [of(6, 1)]
    return values + [-of(6, g.rows - 1)]


def sender(g, row_ref, go_ahead, go_behind):
    near = row_ref[g.flags + NEAR] > 0.5

    def send(at, low_value, high_value):
        go_ahead[at] = jnp.where(near, high_value, low_value)
        go_behind[at] = jnp.where(near, low_value, high_value)

    return send


def send_rows(g, row_ref, of, go_ahead, go_behind):
    bottom, top = row_ref[g.flags + BOTTOM], row_ref[g.flags + TOP_END]
    send = sender(g, row_ref, go_ahead, go_behind)
    for c, (x, y) in enumerate(zip(polar_nine(g, bottom, of, True), polar_nine(g, top, of, False))):
        send(c, x, y)


def pack_kernel(g, row_ref, state, last_col, first_col, go_ahead, go_behind, edge, left, right, sem):
    rows, cols = g.rows, g.cols
    copies = [
        pltpu.make_async_copy(state.at[:, pl.ds(0, 3)], edge.at[:, pl.ds(0, 3)], sem.at[0]),
        pltpu.make_async_copy(state.at[:, pl.ds(rows - 1, 1)], edge.at[:, pl.ds(3, 1)], sem.at[1]),
        pltpu.make_async_copy(state.at[:, :, pl.ds(0, 8)], left, sem.at[2]),
        pltpu.make_async_copy(state.at[:, :, pl.ds(cols - 8, 8)], right, sem.at[3]),
    ]
    for copy in copies:
        copy.start()
    for copy in copies[:2]:
        copy.wait()
    send_rows(g, row_ref, lambda c, j: edge[c, j if j < 3 else 3], go_ahead, go_behind)
    for copy in copies[2:]:
        copy.wait()

    def line(j, carry):
        for c in range(8):
            first_col[c, pl.ds(j, 1), :] = left[c, j, 0:1, :]
            last_col[c, pl.ds(j, 1), :] = right[c, j, 7:8, :]
        first_col[8, pl.ds(j, 1), :] = left[7, j, 1:2, :]
        return carry

    lax.fori_loop(0, rows, line, 0)


def pack_corner_kernel(g, row_ref, phlo, phhi, go_ahead, go_behind):
    bottom, top = row_ref[g.flags + BOTTOM], row_ref[g.flags + TOP_END]
    send = sender(g, row_ref, go_ahead, go_behind)
    for ref, base in ((phlo, 0), (phhi, 9)):
        of = lambda c, j: ref[c, j : j + 1, :]
        for c, (x, y) in enumerate(zip(polar_nine(g, bottom, of, True), polar_nine(g, top, of, False))):
            send(slice(base + c, base + c + 1), x, y)
    send(
        slice(18, 19),
        (1.0 - 2.0 * bottom) * phhi[8, 0:1, :],
        (1.0 - 2.0 * top) * phhi[8, g.rows - 1 : g.rows, :],
    )


def turn_kernel(g, row_ref, ahead, behind, to_left, to_right):
    low, high = picker(g, row_ref, ahead, behind)
    to_left[0:9, :] = low(9, slice(0, 9))
    to_left[9:18, :] = high(9, slice(0, 9))
    to_right[0:10, :] = low(9, slice(9, 19))
    to_right[10:20, :] = high(9, slice(9, 19))


def finish_kernel(
    g, row_ref, part, ahead, behind, from_right, from_left, lines_right, lines_left, out, edge, left, right, sem
):
    rows, cols = g.rows, g.cols
    inner = pl.ds(3, rows - 4)
    places = (
        ((slice(None), pl.ds(0, 3)), edge.at[:, pl.ds(0, 3)]),
        ((slice(None), pl.ds(rows - 1, 1)), edge.at[:, pl.ds(3, 1)]),
        ((slice(None), inner, pl.ds(0, 8)), left),
        ((slice(None), inner, pl.ds(cols - 8, 8)), right),
    )
    enter = [pltpu.make_async_copy(part.at[at], ref, sem.at[i]) for i, (at, ref) in enumerate(places)]
    leave = [pltpu.make_async_copy(ref, out.at[at], sem.at[4 + i]) for i, (at, ref) in enumerate(places)]
    for copy in enter:
        copy.start()
    low, high = picker(g, row_ref, ahead, behind)
    bottom = row_ref[g.flags + BOTTOM]
    for copy in enter[:2]:
        copy.wait()
    for c in range(8):
        edge[c, 0] += 0.5 * low(c)
        edge[c, 3] += 0.5 * high(c)
    for e, share in ((1, 0.5 - 0.5 * bottom), (2, 0.5 * bottom)):
        edge[6, e] += share * low(8)
        for lines, k in ((lines_right, cols - 1), (lines_left, 0)):
            edge[6, e, k : k + 1, :] += share * lines[8:9, :]
    for e, right0, left0, second in ((0, 0, 0, 9), (3, 9, 10, 19)):
        for c in range(8):
            edge[c, e, cols - 1 : cols, :] += 0.5 * lines_right[right0 + c : right0 + c + 1, :]
            edge[c, e, 0:1, :] += 0.5 * lines_left[left0 + c : left0 + c + 1, :]
        edge[7, e, 1:2, :] += 0.5 * lines_left[second : second + 1, :]

    def columns(ref0, ref1, e, j):
        for c in range(8):
            ref0[c, e, 0:1, :] += 0.5 * from_left[c, pl.ds(j, 1), :]
            k = ref1.shape[2]
            ref1[c, e, k - 1 : k, :] += 0.5 * from_right[c, pl.ds(j, 1), :]
        ref0[7, e, 1:2, :] += 0.5 * from_left[8, pl.ds(j, 1), :]

    for e, j in ((0, 0), (1, 1), (2, 2), (3, rows - 1)):
        columns(edge, edge, e, j)
    for copy in leave[:2]:
        copy.start()
    for copy in enter[2:]:
        copy.wait()

    def step(e, carry):
        columns(left, right, e, e + 3)
        return carry

    lax.fori_loop(0, rows - 4, step, 0)
    for copy in leave[2:]:
        copy.start()
    for copy in leave:
        copy.wait()


ANY = pl.BlockSpec(memory_space=pl.ANY)
VMEM = pl.BlockSpec(memory_space=pltpu.VMEM)
SMEM = pl.BlockSpec(memory_space=pltpu.SMEM)


def call(kernel, ins, outs, scratch, flops, limit, interpret=False):
    return pl.pallas_call(
        kernel,
        out_shape=[jax.ShapeDtypeStruct(s, jnp.float32) for _, s in outs],
        in_specs=[SMEM] + ins,
        out_specs=[s for s, _ in outs],
        scratch_shapes=scratch,
        compiler_params=pltpu.CompilerParams(vmem_limit_bytes=limit << 20),
        cost_estimate=pl.CostEstimate(flops=flops, bytes_accessed=16 << 20, transcendentals=0),
        interpret=interpret,
    )


def buffers(*shapes):
    return [pltpu.VMEM(s, jnp.float32) for s in shapes]


def sizes(g):
    return (
        (8, g.rows, g.cols, g.rads),
        [(8, g.rows, g.rads), (9, g.rows, g.rads)],
        (9, g.cols, g.rads),
        (24, g.rads),
    )


def forward(g, table, own, halos, planes, interpret=False):
    n = g.slots
    shape, sides, body, lines = sizes(g)
    scratch = buffers((8, 2, n, LANES), (15, 2, n, LANES), (6, n, LANES), (10, 2, n, LANES), shape)
    dma = pltpu.SemaphoreType.DMA
    scratch += [dma((g.rows, 2)), dma((g.rows,))]
    outs = [(ANY, shape)] + [(VMEM, s) for s in sides + [body, body]]
    run = call(functools.partial(forward_kernel, g), [ANY] + [VMEM] * 7, outs, scratch, 10**8, 48, interpret)
    return run(table, own, *halos, planes)


def adjoint(g, table, own, halos, cot, planes, more, received, interpret=False):
    n = g.slots
    shape, sides, body, lines = sizes(g)
    message = (10, g.cols, g.rads)
    outs = [(ANY, shape)] + [(VMEM, s) for s in sides + [message, message]]
    scratch = buffers(
        (8, 2, n, LANES),
        (8, 2, n, LANES),
        (13, 2, n, LANES),
        (3, 2, n, LANES),
        (2, n, LANES),
        (11, 2, g.cols, LANES),
        (11, 2, 8 + g.cols, LANES),
        shape,
        (11, 2, g.rows + 8, LANES),
        (8, 2, g.rows, LANES),
        (g.rows, LANES),
    )
    dma = pltpu.SemaphoreType.DMA
    scratch += [dma((g.rows, 2)), dma((g.rows, 2)), dma((g.rows,)), dma((g.rows,))]
    ins = [ANY, ANY] + [VMEM] * 7 + ([ANY] + [VMEM] * 6 if received else [ANY, ANY])
    run = call(functools.partial(adjoint_kernel, g, received), ins, outs, scratch, 3 * 10**8, 48, interpret)
    return run(table, own, cot, *halos, planes, *more)


def edges_of(g, table, cot, planes):
    n = g.slots
    outs = [(ANY, (3, 2, n, LANES)), (ANY, (2, n, LANES))]
    scratch = buffers((3, 2, n, LANES), *[s for _, s in outs])
    scratch += [pltpu.SemaphoreType.DMA((g.rows, 2)), pltpu.SemaphoreType.DMA((2,))]
    return call(functools.partial(edge_kernel, g), [ANY, VMEM], outs, scratch, 10**8, 16)(table, cot, planes)


def pack(g, table, state):
    shape, sides, body, lines = sizes(g)
    strip = (8, g.rows, 8, g.rads)
    scratch = buffers((8, 4, g.cols, g.rads), strip, strip) + [pltpu.SemaphoreType.DMA((4,))]
    outs = [(VMEM, s) for s in sides + [body, body]]
    return call(functools.partial(pack_kernel, g), [ANY], outs, scratch, 10**6, 58)(table, state)


def pack_corners(g, table, phlo, phhi):
    lines = sizes(g)[3]
    return call(functools.partial(pack_corner_kernel, g), [VMEM] * 2, [(VMEM, lines)] * 2, [], 10**6, 16)(
        table, phlo, phhi
    )


def turn(g, table, ahead, behind):
    lines = sizes(g)[3]
    return call(functools.partial(turn_kernel, g), [VMEM] * 2, [(VMEM, lines)] * 2, [], 10**6, 16)(
        table, ahead, behind
    )


def finish(g, table, part, *received):
    strip = (8, g.rows - 4, 8, g.rads)
    return pl.pallas_call(
        functools.partial(finish_kernel, g),
        out_shape=jax.ShapeDtypeStruct(part.shape, jnp.float32),
        in_specs=[SMEM, ANY] + [VMEM] * 6,
        out_specs=ANY,
        input_output_aliases={1: 0},
        scratch_shapes=buffers((8, 4, g.cols, g.rads), strip, strip) + [pltpu.SemaphoreType.DMA((8,))],
        compiler_params=pltpu.CompilerParams(vmem_limit_bytes=44 << 20),
        cost_estimate=pl.CostEstimate(flops=10**6, bytes_accessed=7 << 20, transcendentals=0),
    )(table, part, *received)


class Place:
    def __init__(self):
        self.n_th, self.n_ph = lax.axis_size("th"), lax.axis_size("ph")
        n_th, n_ph = self.n_th, self.n_ph
        half = n_ph // 2
        self.th, self.ph = lax.axis_index("th"), lax.axis_index("ph")
        self.at_bottom, self.at_top = self.th == 0, self.th == n_th - 1
        self.near = self.ph < half
        self.right = [(i, (i + 1) % n_ph) for i in range(n_ph)]
        self.left = [(j, i) for i, j in self.right]
        self.round = []
        for t in range(n_th):
            for p in range(half):
                self.round.append((t * n_ph + p, (t + 1) * n_ph + p if t < n_th - 1 else t * n_ph + p + half))
                self.round.append((t * n_ph + p + half, (t - 1) * n_ph + p + half if t > 0 else p))
        self.back = [(j, i) for i, j in self.round]

    def polar(self, ahead, behind):
        both = ("th", "ph")
        return lax.ppermute(ahead, both, self.round), lax.ppermute(behind, both, self.back)

    def sideways(self, to_right, to_left):
        return lax.ppermute(to_right, "ph", self.right), lax.ppermute(to_left, "ph", self.left)


def shards(state, cotangent):
    place = Place()
    _, rows, cols, rads = state.shape
    g = Grid(rows, cols, rads, rows * place.n_th, cols * place.n_ph)
    flags = jnp.stack([place.at_bottom, place.at_top, place.near]).astype(jnp.float32)
    table = lax.dynamic_slice_in_dim(jnp.asarray(g.row_table()), place.th * rows, rows + 5, 0).reshape(-1)
    table = jnp.concatenate([table, flags])
    planes = jnp.asarray(g.radial_planes())

    def halos_of(rims, beside=None):
        last, first, ahead, behind = rims
        phlo, phhi = place.sideways(last, first)
        body = place.polar(ahead, behind)
        done = None
        if beside is not None:
            phlo, phhi, done = lax.optimization_barrier((phlo, phhi, beside(first)))
        return (phlo, phhi) + tuple(body) + tuple(place.polar(*pack_corners(g, table, phlo, phhi))), done

    def give_back(parts):
        gphlo, gphhi, ahead, behind = parts
        from_left, from_right = place.sideways(gphhi, gphlo)
        ahead, behind = place.polar(ahead, behind)
        to_left, to_right = turn(g, table, ahead, behind)
        lines_left, lines_right = place.sideways(to_right, to_left)
        return ahead, behind, from_right, from_left, lines_right, lines_left

    def edges_beside(rim):
        return edges_of(g, table, lax.optimization_barrier((cotangent, rim))[0], planes)

    halos_zero, edges = halos_of(pack(g, table, state), edges_beside)
    moved, *rims = forward(g, table, state, halos_zero, planes)
    halos_one, _ = halos_of(rims)
    part, *ghosts = adjoint(g, table, moved, halos_one, cotangent, planes, edges, False)
    more = (cotangent,) + give_back(ghosts)
    part, *ghosts = adjoint(g, table, state, halos_zero, part, planes, more, True)
    return finish(g, table, part, *give_back(ghosts))


def solution(mesh):
    placed = (P(None, "th", "ph", None), P(None, "th", "ph", None))
    return jax.shard_map(
        shards, mesh=mesh, in_specs=placed, out_specs=P(None, "th", "ph", None), check_vma=False
    )
```

```python
import functools
import math

import jax
import jax.numpy as jnp
import numpy as np
from jax import lax
from jax.experimental import pallas as pl
from jax.experimental.pallas import tpu as pltpu
from jax.sharding import PartitionSpec as P

GAMMA = 5.0 / 3.0
R_INNER = 1.0
R_OUTER = 3.0
COURANT = 0.4
SPEED_BOUND = 5.0
PRESSURE_SOFT = 0.05
THETA_CUT = 0.1

G1 = GAMMA - 1.0
LANES = 128
PAD = 32
FACE_SLOTS = 32
FLIPS = (1.0, 1.0, -1.0, -1.0, 1.0, 1.0, -1.0, -1.0)
SH, SL, AZ, COT, AK, KEEP, N_ROW = 0, 1, 2, 3, 4, 5, 6
BOTTOM, TOP_END, NEAR = 0, 1, 2
INV_V, R_HI2, K_V, INV_MID, INV_LO, LO, HI, INV_SHELL, HALF_HI2, HALF_KV, HALF_LO2, TOP, OPEN = range(13)


class Grid:
    def __init__(self, rows, cols, rads, total_rows, total_cols):
        self.rows, self.cols, self.rads = rows, cols, rads
        self.width = cols + 8
        self.tiles = self.width // 8
        self.slots = PAD + (rows + 4) * self.width + PAD
        self.dth = (math.pi - 2.0 * THETA_CUT) / total_rows
        self.dph = 2.0 * math.pi / total_cols
        self.dr = (R_OUTER - R_INNER) / rads
        self.dt = COURANT * min(self.dr, R_INNER * math.sin(THETA_CUT) * self.dph) / SPEED_BOUND
        self.total_rows = total_rows

    def at(self, j, k):
        return PAD + (j + 2) * self.width + k

    def row_table(self):
        j = np.arange(-2, self.total_rows + 3, dtype=np.float64)
        low = THETA_CUT + j * self.dth
        high, mid = low + self.dth, low + 0.5 * self.dth
        drop = np.cos(low) - np.cos(high)
        keep = np.where((j == 0) | (j == self.total_rows), 0.0, 1.0)
        safe = np.where(np.abs(np.sin(low)) < 1e-6, 1.0, np.sin(low))
        table = np.zeros((len(j), N_ROW))
        table[:, SH] = np.sin(high) / drop
        table[:, SL] = np.sin(low) / drop
        table[:, AZ] = self.dth / (drop * self.dph)
        table[:, COT] = np.cos(mid) / np.sin(mid)
        table[:, AK] = keep / (safe * self.dph)
        table[:, KEEP] = keep
        return table.astype(np.float32)

    @property
    def flags(self):
        return (self.rows + 5) * N_ROW

    def radial_planes(self):
        i = np.arange(self.rads, dtype=np.float64)
        low = R_INNER + i * self.dr
        high, mid = low + self.dr, low + 0.5 * self.dr
        vol = (high**3 - low**3) / 3.0
        shell = 0.5 * (high**2 - low**2)
        top = np.where(i == self.rads - 1, 2.0, 1.0)
        planes = [None] * 13
        planes[INV_V] = 1.0 / vol
        planes[R_HI2] = high**2
        planes[K_V] = shell / vol
        planes[INV_MID] = 1.0 / mid
        planes[INV_LO] = 1.0 / low
        planes[LO] = low
        planes[HI] = high
        planes[INV_SHELL] = 1.0 / shell
        planes[HALF_HI2] = 0.5 * self.dt * high**2
        planes[HALF_KV] = 0.5 * self.dt * shell / vol
        planes[HALF_LO2] = 0.5 * self.dt * low**2
        planes[TOP] = top
        planes[OPEN] = 2.0 - top
        stack = np.stack(planes).astype(np.float32).reshape(13, 2, 1, LANES)
        return np.broadcast_to(stack, (13, 2, 8, LANES)).copy()


def lane_index(x):
    return lax.broadcasted_iota(jnp.int32, x.shape, 2)


def next_r(x, last=None):
    turned = pltpu.roll(x, LANES - 1, 2)
    end = x[1:2] if last is None else last
    return jnp.where(lane_index(x) == LANES - 1, jnp.concatenate([turned[1:2], end], 0), turned)


def prev_r(x, first):
    turned = pltpu.roll(x, 1, 2)
    return jnp.where(lane_index(x) == 0, jnp.concatenate([first, turned[0:1]], 0), turned)


def split(x):
    return jnp.stack([x[:, :LANES], x[:, LANES:]])


def load(ref, field, slot, size=8):
    return ref[field, :, pl.ds(slot, size), :]


def put(ref, field, slot, value):
    ref[field, :, pl.ds(slot, value.shape[1]), :] = value


def loader(size):
    return lambda ref, field, slot: load(ref, field, slot, size)


def planes_of(rc, size):
    return lambda i: jnp.concatenate([rc[i]] * (size // 8), 1)


def put_line(ref, field, slot, line):
    ref[field, 0, pl.ds(slot, 1), :] = line[:, :LANES]
    ref[field, 1, pl.ds(slot, 1), :] = line[:, LANES:]


def get_line(ref, field, slot):
    return jnp.concatenate([ref[field, 0, pl.ds(slot, 1), :], ref[field, 1, pl.ds(slot, 1), :]], 1)


def put_column(g, ref, field, k, value):
    ref[field, :, pl.ds(g.at(0, k), g.rows, stride=g.width), :] = value


def column_of(g, ref, field, k, row=0):
    return ref[field, :, pl.ds(g.at(row, k), g.rows, stride=g.width), :]


def picker(g, row_ref, ahead, behind):
    near = row_ref[g.flags + NEAR] > 0.5

    def low(*at):
        return jnp.where(near, ahead[at], behind[at])

    def high(*at):
        return jnp.where(near, behind[at], ahead[at])

    return low, high


def row_copies(g, hbm, ref, sem, row=None, parts=slice(None)):
    for j in range(g.rows) if row is None else (row,):
        for h in range(2):
            yield pltpu.make_async_copy(
                hbm.at[parts, j, :, pl.ds(h * LANES, LANES)], ref.at[:, h, pl.ds(g.at(j, 0), g.cols), :], sem.at[j, h]
            )


def fill_state(g, us, row_ref, halos):
    rows, cols = g.rows, g.cols
    phlo, phhi, ahead, behind, corner_ahead, corner_behind = halos
    low, high = picker(g, row_ref, ahead, behind)
    corner_low, corner_high = picker(g, row_ref, corner_ahead, corner_behind)
    calm = [jnp.full((2, 8, LANES), 1.0 if c == 0 else 0.0, jnp.float32) for c in range(8)]

    def keep(j):
        return row_ref[(j + 2) * N_ROW + KEEP]

    def ends(j, fetch):
        for c in range(8):
            scale = keep(j) if c == 6 else None
            for which, k in ((0, -1), (1, cols)):
                line = fetch(c, which)
                put_line(us, c, g.at(j, k), line if scale is None else line * scale)
        put_line(us, 7, g.at(j, cols + 1), fetch(7, 2))

    def body_row(j, side):
        for c in range(8):
            for t in range(cols // 8):
                x = split(side(c, slice(t * 8, t * 8 + 8)))
                put(us, c, g.at(j, t * 8), x * keep(j) if c == 6 else x)

    def still(n, carry):
        for c in range(8):
            put(us, c, pl.multiple_of(g.at(-2, cols) + n * g.width, 8), calm[c])
        return carry

    lax.fori_loop(0, rows + 3, still, 0)
    body_row(-1, low)
    ends(-1, lambda c, w: corner_low(slice((c, 9 + c, 18)[w], (c, 9 + c, 18)[w] + 1)))

    for c in range(8):
        put_column(g, us, c, -1, split(phlo[c]))
        put_column(g, us, c, cols, split(phhi[c]))
    put_column(g, us, 7, cols + 1, split(phhi[8]))
    for ref, k in ((phlo, -1), (phhi, cols)):
        put_line(us, 6, g.at(0, k), ref[6, 0:1, :] * keep(0))
    body_row(rows, high)
    ends(rows, lambda c, w: corner_high(slice((c, 9 + c, 18)[w], (c, 9 + c, 18)[w] + 1)))
    far = keep(rows + 1)
    for t in range(g.tiles):
        x = split(high(8, slice(t * 8, t * 8 + 8))) if t < cols // 8 else calm[1]
        put(us, 6, g.at(rows + 1, t * 8), x * far)
    put_line(us, 6, g.at(rows + 1, -1), corner_high(slice(8, 9)) * far)
    put_line(us, 6, g.at(rows + 1, cols), corner_high(slice(17, 18)) * far)

def arrive(g, us, row_ref, own, sem, j):
    for copy in row_copies(g, own, us, sem, j):
        copy.wait()
    if isinstance(j, int) and j == 0:
        for t in range(g.cols // 8):
            put(us, 6, g.at(0, t * 8), load(us, 6, g.at(0, t * 8)) * row_ref[2 * N_ROW + KEEP])


def cell_values(g, us, p, size):
    load = loader(size)
    rho, m0, m1, m2, energy, u5, u6, u7 = [load(us, c, p) for c in range(8)]
    b0 = 0.5 * (u5 + next_r(u5))
    b1 = 0.5 * (u6 + load(us, 6, p + g.width))
    b2 = 0.5 * (u7 + load(us, 7, p + 1))
    q = 1.0 / rho
    v0, v1, v2 = m0 * q, m1 * q, m2 * q
    square = b0 * b0 + b1 * b1 + b2 * b2
    pressure = G1 * (energy - 0.5 * (m0 * v0 + m1 * v1 + m2 * v2) - 0.5 * square)
    total = pressure + 0.5 * square
    soft = pressure * pressure + PRESSURE_SOFT * PRESSURE_SOFT
    inv_soft = lax.rsqrt(soft)
    c2 = (GAMMA * (soft * inv_soft) + square) * q
    return (m0, m1, m2), (v0, v1, v2), (b0, b1, b2), u5, q, pressure, total, energy + total, inv_soft, c2


def forward_kernel(g, row_ref, own, *refs):
    halos, rc, refs = refs[:6], refs[6], refs[7:]
    out, last_col, first_col, go_ahead, go_behind, us, cf, gf, ff, stage, sem, sem_out = refs
    for copy in row_copies(g, own, us, sem):
        copy.start()
    fill_state(g, us, row_ref, halos)
    w = g.width
    wide = w
    arrive(g, us, row_ref, own, sem, 0)

    def cells(n, carry):
        p = pl.multiple_of(g.at(-1, -8) + n * wide, 8)

        @pl.when((n > 0) & (n < g.rows))
        def _():
            arrive(g, us, row_ref, own, sem, n)

        m, v, b, u5, q, pressure, total, h, inv_soft, c2 = cell_values(g, us, p, wide)
        put(cf, 0, p, m[0] * v[0] - b[0] * b[0] + total)
        put(cf, 1, p, m[0] * v[1] - b[0] * b[1])
        put(cf, 2, p, m[0] * v[2] - b[0] * b[2])
        put(cf, 3, p, m[1] * v[1] - b[1] * b[1] + total)
        put(cf, 4, p, m[1] * v[2] - b[1] * b[2])
        put(cf, 5, p, m[2] * v[2] - b[2] * b[2] + total)
        vb = v[0] * b[0] + v[1] * b[1] + v[2] * b[2]
        for d in range(3):
            put(cf, 6 + d, p, h * v[d] - b[d] * vb)
            put(cf, 9 + d, p, v[d] * v[d] + c2)
        put(cf, 12, p, v[2] * b[1] - v[1] * b[2])
        put(cf, 13, p, v[0] * b[2] - v[2] * b[0])
        put(cf, 14, p, v[1] * b[0] - v[0] * b[1])
        m, v, b = [[x[0:1] for x in y] for y in (m, v, b)]
        bg = u5[0:1]
        gain = (1.0 - 0.5 * GAMMA) * (bg * bg - b[0] * b[0])
        vbg = vb[0:1] + v[0] * (bg - b[0])
        ghost = (
            m[0] * v[0] - bg * bg + total[0:1] + gain,
            m[0] * v[1] - bg * b[1],
            m[0] * v[2] - bg * b[2],
            (h[0:1] + gain) * v[0] - bg * vbg,
            v[0] * b[2] - v[2] * bg,
            v[1] * bg - v[0] * b[1],
        )
        for f, x in enumerate(ghost):
            gf[f, pl.ds(p, wide), :] = x[0]
        return carry

    lax.fori_loop(0, g.rows + 3, cells, 0)

    index = ((0, 1, 2), (1, 3, 4), (2, 4, 5))

    def face(d, p, shift, size):
        load = loader(size)
        fluxes = [load(us, 1 + d, p)] + [load(cf, index[d][c], p) for c in range(3)] + [load(cf, 6 + d, p)]
        speed = load(cf, 9 + d, p)
        state = [load(us, c, p) for c in range(5)]
        if shift is None:
            other = [next_r(x) for x in fluxes]
            speed2 = next_r(speed)
            state2 = [other[0] if c == 1 else next_r(state[c]) for c in range(5)]
        else:
            r = p + shift
            other = [load(us, 1 + d, r)] + [load(cf, index[d][c], r) for c in range(3)] + [load(cf, 6 + d, r)]
            speed2 = load(cf, 9 + d, r)
            state2 = [load(us, c, r) for c in range(5)]
        total = 0.5 * (speed + speed2)
        half = 0.5 * (total * lax.rsqrt(total))
        return fluxes, [0.5 * (fluxes[c] + other[c]) - half * (state2[c] - state[c]) for c in range(5)]

    def faces(n, carry):
        p = pl.multiple_of(g.at(-1, 0) + n * FACE_SLOTS, 8)
        for d, shift, base in ((1, w, 0), (2, 1, 5)):
            _, flux = face(d, p, shift, FACE_SLOTS)
            for c in range(5):
                put(ff, base + c, p, flux[c])
        return carry

    lax.fori_loop(0, (g.rows + 1) * g.width // FACE_SLOTS, faces, 0)

    size = g.cols
    load = loader(size)
    plane = planes_of(rc, size)

    def leave(j):
        return pltpu.make_async_copy(stage.at[:, j], out.at[:, j], sem_out.at[j])

    def combine(j, carry):
        p = pl.multiple_of(g.at(j, 0), 8)
        row = (j + 2) * N_ROW
        sh, sl, az, cot, ak, keep = [row_ref[row + i] for i in range(N_ROW)]
        cells_here, flux_r = face(0, p, None, size)
        ghost = [load(us, 1, p)[0:1]] + [gf[f, pl.ds(p, size), :][None] for f in range(4)]
        inv_v, kv = plane(INV_V), plane(K_V)
        rates = []
        for c in range(5):
            high = plane(R_HI2) * flux_r[c]
            first = 0.5 * plane(HALF_LO2)[0:1] * (2.0 / g.dt) * (ghost[c] + cells_here[c][0:1])
            low = prev_r(high, first)
            th = sh * load(ff, c, p) - sl * load(ff, c, p - w)
            ph = az * (load(ff, 5 + c, p) - load(ff, 5 + c, p - 1))
            rates.append(-(inv_v * (high - low) + kv * (th + ph)))
        tt = [load(cf, f, p) for f in range(1, 6)]
        mid = plane(INV_MID)
        rates[1] = rates[1] + (tt[2] + tt[4]) * mid
        rates[2] = rates[2] + (cot * tt[4] - tt[0]) * mid
        rates[3] = rates[3] - (tt[1] + cot * tt[3]) * mid
        ep, ept = load(cf, 14, p), load(cf, 14, p + w)
        x0 = load(cf, 14, p - w) + ep
        x1 = ep + ept
        g_here = gf[5, pl.ds(p, size), :][None]
        x0m = prev_r(x0, gf[5, pl.ds(p - w, size), :][None] + g_here)
        x1m = prev_r(x1, g_here + gf[5, pl.ds(p + w, size), :][None])
        z0 = 0.25 * (x0 + x0m)
        zr = 0.25 * (next_r(x0) + x0)
        z1 = 0.25 * (x1 + x1m)
        et = load(cf, 13, p)
        y0 = load(cf, 13, p - 1) + et
        y1 = et + load(cf, 13, p + 1)
        g_here = gf[4, pl.ds(p, size), :][None]
        y0m = prev_r(y0, gf[4, pl.ds(p - 1, size), :][None] + g_here)
        y1m = prev_r(y1, g_here + gf[4, pl.ds(p + 1, size), :][None])
        p0 = 0.25 * (y0 + y0m)
        pr = 0.25 * (next_r(y0) + y0)
        p1 = 0.25 * (y1 + y1m)
        er, era, erb = load(cf, 12, p), load(cf, 12, p - 1), load(cf, 12, p - w)
        r0 = 0.25 * (er + era + erb + load(cf, 12, p - w - 1))
        r1 = 0.25 * (load(cf, 12, p + 1) + er + load(cf, 12, p - w + 1) + erb)
        rt = 0.25 * (load(cf, 12, p + w) + load(cf, 12, p + w - 1) + er + era)
        lo, hi, shell = plane(LO), plane(HI), plane(INV_SHELL)
        rates.append(-plane(INV_LO) * (sh * z1 - sl * z0 - az * (p1 - p0)))
        rates.append(-shell * (g.dr * ak * (r1 - r0) - keep * (hi * zr - lo * z0)))
        rates.append(shell * ((g.dr / g.dth) * (rt - r0) - (hi * pr - lo * p0)))
        for c in range(8):
            new = load(us, c, p) + g.dt * rates[c]
            stage[c, j] = jnp.concatenate([new[0], new[1]], 1)
        leave(j).start()
        for c in range(8):
            last_col[c, pl.ds(j, 1), :] = stage[c, j, g.cols - 1 : g.cols, :]
            first_col[c, pl.ds(j, 1), :] = stage[c, j, 0:1, :]
        first_col[8, pl.ds(j, 1), :] = stage[7, j, 1:2, :]
        return carry

    lax.fori_loop(0, g.rows, combine, 0)

    send_rows(g, row_ref, lambda c, j: stage[c, j], go_ahead, go_behind)

    def settle(j, carry):
        leave(j).wait()
        return carry

    lax.fori_loop(0, g.rows, settle, 0)


def cell_pass(g, us, row_ref, own, sem, cf):
    w, rows = g.width, g.rows
    arrive(g, us, row_ref, own, sem, 0)

    def cells(n, carry):
        p = pl.multiple_of(g.at(-1, -8) + n * w, 8)

        @pl.when((n > 0) & (n < rows))
        def _():
            arrive(g, us, row_ref, own, sem, n)

        m, v, b, u5, q, pressure, total, h, inv_soft, c2 = cell_values(g, us, p, w)
        for d in range(3):
            put(cf, d, p, v[d])
            put(cf, 3 + d, p, b[d])
            put(cf, 6 + d, p, v[d] * v[d] + c2)
        put(cf, 9, p, h)
        put(cf, 10, p, q)
        put(cf, 11, p, GAMMA * q * (pressure * inv_soft))
        put(cf, 12, p, c2 * q)
        return carry

    lax.fori_loop(0, rows + 3, cells, 0)


def edge_pass(g, row_ref, rc, cs, base, ef, zf):
    w, rows = g.width, g.rows
    zero = jnp.zeros((2, 8, LANES), jnp.float32)
    for f in range(3):
        put(ef, f, g.at(-1, -8), zero)
    for f in range(2):
        zf[f, pl.ds(g.at(-1, -8), 8), :] = zero[0]

    def edges(n, carry):
        load = loader(w)
        plane = planes_of(rc, w)
        none = jnp.zeros((1, w, LANES), jnp.float32)
        p = pl.multiple_of(g.at(-1, 0) + n * w, 8)
        j = n - 1
        row = (j + 2) * N_ROW
        sl, az, ak, keep = [row_ref[row + i] for i in (SL, AZ, AK, KEEP)]
        sh_below = row_ref[row - N_ROW + SH]
        shell, lo, hi = plane(INV_SHELL), plane(LO), plane(HI)
        c5, c6, c7 = load(cs, base, p), load(cs, base + 1, p), load(cs, base + 2, p)
        rb = ak * (c6 - load(cs, base + 1, p - 1)) + (1.0 / g.dth) * (load(cs, base + 2, p - w) - c7)
        put(ef, 0, p, (0.25 * g.dt * g.dr) * shell * rb)
        q6 = keep * c6 * shell
        zb = plane(INV_LO) * (sl * c5 - sh_below * load(cs, base, p - w)) + prev_r(hi * q6, none) - lo * q6
        q7 = c7 * shell
        hq7 = hi * q7
        pb = plane(INV_LO) * az * (load(cs, base, p - 1) - c5) + lo * q7 - prev_r(hq7, none)
        zl = 2.0 * hi[1:2] * q6[1:2]
        plast = -2.0 * hq7[1:2]
        put(ef, 1, p, (0.25 * g.dt) * (zb + next_r(zb, zl)))
        put(ef, 2, p, (0.25 * g.dt) * (pb + next_r(pb, plast)))
        zf[0, pl.ds(p, w), :] = (0.25 * g.dt) * zb[0]
        zf[1, pl.ds(p, w), :] = (0.25 * g.dt) * pb[0]
        return carry

    lax.fori_loop(0, rows + 3, edges, 0)


def clear_ghosts(g, cs, count):
    zero = jnp.zeros((2, 8, LANES), jnp.float32)
    for j in (-2, -1, g.rows, g.rows + 1):
        for c in range(count):
            for t in range(g.tiles):
                put(cs, c, g.at(j, t * 8), zero)
    for c in range(count):
        put(cs, c, g.at(-2, -8), zero)

    def clear(j, carry):
        for c in range(count):
            put(cs, c, g.at(j, g.cols), zero)
        return carry

    lax.fori_loop(0, g.rows, clear, 0)


def edge_kernel(g, row_ref, cot, rc, ef, zf, cs, sem):
    for copy in row_copies(g, cot, cs, sem, parts=pl.ds(5, 3)):
        copy.start()
    clear_ghosts(g, cs, 3)
    for copy in row_copies(g, cot, cs, sem, parts=pl.ds(5, 3)):
        copy.wait()
    edge_pass(g, row_ref, rc, cs, 0, ef, zf)


def cell_pull(load, plane, us, cf, p, fr_, ft_, fp_, ub, sb, sources, cot, e, first, ghost_e):
    none = jnp.zeros_like(first[0])
    w1, w2, w3 = sources
    e0, e1, e2 = e
    s00, s11 = fr_[1], ft_[2] + w1
    s22 = fp_[3] + w1 + cot * w2
    s01 = fr_[2] + ft_[1] - w2
    s02 = fr_[3] + fp_[1] - w3
    s12 = ft_[3] + fp_[2] - cot * w3
    v = [load(cf, d, p) for d in range(3)]
    b = [load(cf, 3 + d, p) for d in range(3)]
    h, q = load(cf, 9, p), load(cf, 10, p)
    gg = (fr_[4], ft_[4], fp_[4])
    flow = v[0] * gg[0] + v[1] * gg[1] + v[2] * gg[2]
    beta = b[0] * gg[0] + b[1] * gg[1] + b[2] * gg[2]
    vb = v[0] * b[0] + v[1] * b[1] + v[2] * b[2]
    d00, d11, d22 = s00 + s00, s11 + s11, s22 + s22
    sv = (
        d00 * v[0] + s01 * v[1] + s02 * v[2],
        s01 * v[0] + d11 * v[1] + s12 * v[2],
        s02 * v[0] + s12 * v[1] + d22 * v[2],
    )
    sbm = (
        d00 * b[0] + s01 * b[1] + s02 * b[2],
        s01 * b[0] + d11 * b[1] + s12 * b[2],
        s02 * b[0] + s12 * b[1] + d22 * b[2],
    )
    c2b = sb[0] + sb[1] + sb[2]
    ptb = s00 + s11 + s22 + flow
    pb = c2b * load(cf, 11, p) + ptb
    pg = G1 * pb
    bbb = 2.0 * (c2b * q) + ptb - pg
    bxe = (b[1] * e2 - b[2] * e1, b[2] * e0 - b[0] * e2, b[0] * e1 - b[1] * e0)
    exv = (e1 * v[2] - e2 * v[1], e2 * v[0] - e0 * v[2], e0 * v[1] - e1 * v[0])
    rho_bar = ub[0] - c2b * load(cf, 12, p)
    m_bar, b_bar = [], []
    for d in range(3):
        vbar = h * gg[d] - beta * b[d] + 2.0 * (v[d] * sb[d]) - bxe[d]
        turn = q * vbar - pg * v[d]
        f0 = (fr_[0], ft_[0], fp_[0])[d]
        m_bar.append(ub[1 + d] + f0 + sv[d] + turn)
        rho_bar = rho_bar - v[d] * (0.5 * sv[d] + turn + 0.5 * (pg * v[d]))
        b_bar.append(b[d] * bbb - sbm[d] - vb * gg[d] - beta * v[d] - exv[d])
    e_bar = ub[4] + flow + pg

    first_lane = lax.broadcasted_iota(jnp.int32, none.shape, 2) == 0
    v, b = [[x[0:1] for x in y] for y in (v, b)]
    q, h = q[0:1], h[0:1]
    bg = load(us, 5, p)[0:1]
    h = h + (1.0 - 0.5 * GAMMA) * (bg * bg - b[0] * b[0])
    vbg = vb[0:1] + v[0] * (bg - b[0])
    s00, s01, s02, g0 = first[1], first[2], first[3], first[4]
    e1, e2 = ghost_e
    flow = v[0] * g0
    beta = bg * g0
    pb = s00 + flow
    pg = G1 * pb
    bbb = pb - pg
    d00 = s00 + s00
    sv = (d00 * v[0] + s01 * v[1] + s02 * v[2], s01 * v[0], s02 * v[0])
    sbm = (d00 * bg + s01 * b[1] + s02 * b[2], s01 * bg, s02 * bg)
    vbar = (
        h * g0 - beta * bg - (b[1] * e2 - b[2] * e1),
        bg * e2 - beta * b[1],
        -(beta * b[2]) - bg * e1,
    )
    exv = (e1 * v[2] - e2 * v[1], e2 * v[0], -(e1 * v[0]))
    more = [None] * 8
    rho_more = none
    for d in range(3):
        turn = q * vbar[d] - pg * v[d]
        more[1 + d] = sv[d] + turn + (first[0] if d == 0 else 0.0)
        rho_more = rho_more - v[d] * (0.5 * sv[d] + turn + 0.5 * (pg * v[d]))
        bd = bg if d == 0 else b[d]
        more[5 + d] = bd * bbb - sbm[d] - beta * v[d] - exv[d]
    more[5] = more[5] - vbg * g0
    more[0] = rho_more
    more[4] = flow + pg

    def with_first(x, extra):
        return x + jnp.concatenate([jnp.where(first_lane, extra, 0.0), none], 0)

    radial = 0.5 * (plane(TOP) * b_bar[0] + prev_r(b_bar[0], 2.0 * more[5]))
    values = [with_first(rho_bar, more[0])] + [with_first(m_bar[d], more[1 + d]) for d in range(3)]
    return values + [
        with_first(e_bar, more[4]),
        radial,
        with_first(b_bar[1], more[6]),
        with_first(b_bar[2], more[7]),
    ]


def face_pull(halves, state, state2, speed, speed2, closed=None):
    total = 0.5 * (speed + speed2)
    inv = lax.rsqrt(total)
    a = total * inv
    if closed is not None:
        a = a * closed
    dot = halves[0] * (state2[0] - state[0])
    for c in range(1, 5):
        dot = dot + halves[c] * (state2[c] - state[c])
    return halves + [a * x for x in halves] + [-0.25 * inv * dot]


def adjoint_kernel(g, received, row_ref, own, cot, *refs):
    halos, rc, refs = refs[:6], refs[6], refs[7:]
    if received:
        base, *got = refs[:7]
        refs = refs[7:]
    else:
        ef, zf, *refs = refs
    out, gphlo, gphhi, go_ahead, go_behind, *refs = refs
    if received:
        edge, left, right, *refs = refs
    us, cs, cf, ft, fp, stage, line_lo, held, az_col, *refs = refs
    if received:
        ef, zf, *refs = refs
    sem, sem_cot, sem_out, sem_base = refs
    w, rows, cols = g.width, g.rows, g.cols
    load = loader(8)
    for copy in row_copies(g, own, us, sem):
        copy.start()
    for copy in row_copies(g, cot, cs, sem_cot):
        copy.start()

    def enter(j):
        return pltpu.make_async_copy(base.at[:, j], stage.at[:, j], sem_base.at[j])

    if received:
        for j in range(rows):
            enter(j).start()
    zero = jnp.zeros((2, 8, LANES), jnp.float32)
    clear_ghosts(g, cs, 8)
    fill_state(g, us, row_ref, halos)
    cell_pass(g, us, row_ref, own, sem, cf)
    for copy in row_copies(g, cot, cs, sem_cot):
        copy.wait()
    if received:
        back_ahead, back_behind, from_right, from_left, lines_right, lines_left = got
        low, high = picker(g, row_ref, back_ahead, back_behind)
        bottom = row_ref[g.flags + BOTTOM]

        def add_line(c, slot, line):
            put_line(cs, c, slot, get_line(cs, c, slot) + line)

        for k, ref in ((0, from_left), (cols - 1, from_right)):
            for c in range(8):
                put_column(g, cs, c, k, column_of(g, cs, c, k) + split(ref[c]))
        put_column(g, cs, 7, 1, column_of(g, cs, 7, 1) + split(from_left[8]))
        for t in range(cols // 8):
            at = slice(t * 8, t * 8 + 8)
            for c in range(8):
                p = g.at(0, t * 8)
                put(cs, c, p, load(cs, c, p) + split(low(c, at)))
                p = g.at(rows - 1, t * 8)
                put(cs, c, p, load(cs, c, p) + split(high(c, at)))
            for j, share in ((1, 1.0 - bottom), (2, bottom)):
                p = g.at(j, t * 8)
                put(cs, 6, p, load(cs, 6, p) + share * split(low(8, at)))
        for j, right0, left0, second in ((0, 0, 0, 9), (rows - 1, 9, 10, 19)):
            for c in range(8):
                add_line(c, g.at(j, cols - 1), lines_right[right0 + c : right0 + c + 1, :])
                add_line(c, g.at(j, 0), lines_left[left0 + c : left0 + c + 1, :])
            add_line(7, g.at(j, 1), lines_left[second : second + 1, :])
        for lines, k in ((lines_right, cols - 1), (lines_left, 0)):
            for j, share in ((1, 1.0 - bottom), (2, bottom)):
                add_line(6, g.at(j, k), share * lines[8:9, :])

    if received:
        edge_pass(g, row_ref, rc, cs, 5, ef, zf)

    size = cols
    load = loader(size)
    plane = planes_of(rc, size)
    none = jnp.zeros((1, size, LANES), jnp.float32)
    for f in range(11):
        for t in range(cols // 8):
            put(ft, f, t * 8, zero)

    def spread(j, carry):
        az_col[pl.ds(j, 1), :] = jnp.full((1, LANES), row_ref[(j + 2) * N_ROW + AZ], jnp.float32)
        return carry

    lax.fori_loop(0, rows, spread, 0)
    along = planes_of(rc, rows)

    def down(ref, field, slot):
        return ref[field, :, pl.ds(slot, rows, stride=w), :]

    def down_ghost(field, slot):
        return zf[field, pl.ds(slot, rows, stride=w), :][None]

    def column(k):
        p = g.at(0, k)
        left, right = (p, p + 1) if k < 0 else (p - 1, p)
        sign, source = (1.0, right) if k < 0 else (-1.0, left)
        kaz = (sign * along(HALF_KV)) * az_col[...][None]
        face = face_pull(
            [kaz * down(cs, c, source) for c in range(5)],
            [down(us, c, left) for c in range(5)],
            [down(us, c, right) for c in range(5)],
            down(cf, 8, left),
            down(cf, 8, right),
        )
        nil = jnp.zeros((2, rows, LANES), jnp.float32)
        nils = [nil] * 5
        ub = face[5:10] if k < 0 else [-x for x in face[5:10]]
        edge = p + 1 if k < 0 else p
        e = (down(ef, 0, edge) + down(ef, 0, edge + w), down(ef, 2, edge), nil)
        ghost_e = (down_ghost(1, edge), nil[0:1])
        first = [nil[0:1]] * 5
        values = cell_pull(
            down, along, us, cf, p, nils, nils, face[:5], ub, [nil, nil, face[10]], [nil] * 3, 0.0, e, first, ghost_e
        )
        return face, values

    face, values = column(-1)
    for f in range(11):
        line_lo[f] = jnp.zeros((2, rows + 8, LANES), jnp.float32)
        line_lo[f, :, 1 : rows + 1, :] = face[f]
    _, values_hi = column(cols)
    for c in range(8):
        us[c, :, pl.ds(g.at(0, -1), rows, stride=w), :] = values[c]
        held[c] = values_hi[c]
    for j in (-1, rows):
        for k in (-1, cols):
            p = g.at(j, k)
            e0 = get_line(ef, 0, p) + get_line(ef, 0, p + 1) + get_line(ef, 0, p + w) + get_line(ef, 0, p + w + 1)
            v1, v2, b1, b2, q = [get_line(cf, f, p) for f in (1, 2, 4, 5, 10)]
            m1, m2 = -(q * b2 * e0), q * b1 * e0
            blank = jnp.zeros_like(e0)
            for c, x in enumerate((-(v1 * m1 + v2 * m2), blank, m1, m2, blank, blank, e0 * v2, -(e0 * v1))):
                put_line(us, c, p, x)

    def pull(n, carry):
        p = pl.multiple_of(g.at(-1, 0) + n * w, 8)
        row = (n + 1) * N_ROW
        sh, az = [row_ref[row + i] for i in (SH, AZ)]
        sl_above = row_ref[row + N_ROW + SL]
        state = [load(us, c, p) for c in range(5)]
        cc = [load(cs, c, p) for c in range(5)]
        kd = plane(HALF_KV)
        kaz = kd * az
        face = face_pull(
            [kaz * (load(cs, c, p + 1) - cc[c]) for c in range(5)],
            state,
            [load(us, c, p + 1) for c in range(5)],
            load(cf, 8, p),
            load(cf, 8, p + 1),
        )
        for f in range(11):
            put(fp, f, 8, face[f])
            fp[f, :, 7:8, :] = line_lo[f, :, pl.ds(n, 1), :]
        up = kd * sl_above
        down_by = kd * sh
        pw = pl.multiple_of(p + jnp.where(n > rows, 0, w), 8)
        face = face_pull(
            [up * load(cs, c, pw) - down_by * cc[c] for c in range(5)],
            state,
            [load(us, c, pw) for c in range(5)],
            load(cf, 7, p),
            load(cf, 7, pw),
        )
        ft_ = [face[c] + load(ft, c, 0) for c in range(5)]
        ub = [cc[c] + face[5 + c] - load(ft, 5 + c, 0) for c in range(5)]
        sb1 = face[10] + load(ft, 10, 0)
        for f in range(11):
            put(ft, f, 0, face[f])
        per_volume = [plane(INV_V) * x for x in cc]
        half_hi = plane(HALF_HI2)
        speed = load(cf, 6, p)
        face = face_pull(
            [half_hi * (next_r(x, none) - x) for x in per_volume],
            state,
            [next_r(x) for x in state],
            speed,
            next_r(speed),
            plane(OPEN),
        )
        first = [plane(HALF_LO2)[0:1] * x[0:1] for x in per_volume]
        fr_ = [plane(TOP) * face[c] + prev_r(face[c], first[c]) for c in range(5)]
        ub = [ub[c] + (face[5 + c] - prev_r(face[5 + c], none)) for c in range(5)]
        sb0 = face[10] + prev_r(face[10], none)
        fp_ = [load(fp, c, 8) + load(fp, c, 7) for c in range(5)]
        ub = [ub[c] + (load(fp, 5 + c, 8) - load(fp, 5 + c, 7)) for c in range(5)]
        sb = [sb0, sb1, load(fp, 10, 8) + load(fp, 10, 7)]
        mid = plane(INV_MID) * g.dt
        sources = (cc[1] * mid, cc[2] * mid, cc[3] * mid)
        e = (
            load(ef, 0, p) + load(ef, 0, p + 1) + load(ef, 0, p + w) + load(ef, 0, p + w + 1),
            load(ef, 2, p) + load(ef, 2, p + 1),
            load(ef, 1, p) + load(ef, 1, p + w),
        )
        ghost_e = (
            (zf[1, pl.ds(p, size), :] + zf[1, pl.ds(p + 1, size), :])[None],
            (zf[0, pl.ds(p, size), :] + zf[0, pl.ds(p + w, size), :])[None],
        )
        cot = row_ref[row + COT]
        values = cell_pull(load, plane, us, cf, p, fr_, ft_, fp_, ub, sb, sources, cot, e, first, ghost_e)
        values[5] = values[5] + load(cs, 5, p)
        for c in range(8):
            put(us, c, p, values[c])
        return carry

    lax.fori_loop(0, rows + 2, pull, 0)
    for c in range(8):
        us[c, :, pl.ds(g.at(0, cols), rows, stride=w), :] = held[c]
    load = loader(8)

    def keep_of(j):
        return 0.5 * row_ref[(j + 2) * N_ROW + KEEP]

    def tile6(j, p):
        return keep_of(j) * (load(us, 6, p) + load(us, 6, p - w))

    def tile7(p):
        return 0.5 * (load(us, 7, p) + load(us, 7, p - 1))

    def join(x):
        return jnp.concatenate([x[0], x[1]], 1)

    def line_of(c, j, k):
        p = g.at(j, k)
        if c < 6:
            return get_line(us, c, p)
        if c == 6:
            here = get_line(us, 6, p)
            if isinstance(j, int) and j == -1:
                return keep_of(j) * here
            return keep_of(j) * (here + get_line(us, 6, p - w))
        here = get_line(us, 7, p)
        return 0.5 * here if k == -1 else 0.5 * (here + get_line(us, 7, p - 1))

    def leave(j):
        return pltpu.make_async_copy(stage.at[:, j], out.at[:, j], sem_out.at[j])

    def give(j, carry):
        if received:
            enter(j).wait()
        for t in range(cols // 8):
            p = g.at(j, t * 8)
            at = (j, slice(t * 8, t * 8 + 8))

            def leave_tile(c, x):
                stage[(c,) + at] = 0.5 * (stage[(c,) + at] + x) if received else x

            for c in range(6):
                leave_tile(c, join(load(us, c, p)))
            leave_tile(6, join(load(cs, 6, p) + tile6(j, p)))
            leave_tile(7, join(load(cs, 7, p) + tile7(p)))
        leave(j).start()
        return carry

    lax.fori_loop(0, rows, give, 0)
    if received:
        for e, j in enumerate((0, 1, 2, rows - 1)):
            for c in range(8):
                edge[c, e] = stage[c, j]

        def strips(e, carry):
            for c in range(8):
                left[c, e] = stage[c, e + 3, 0:8, :]
                right[c, e] = stage[c, e + 3, cols - 8 : cols, :]
            return carry

        lax.fori_loop(0, rows - 4, strips, 0)
    for ref, k in ((gphlo, -1), (gphhi, cols)):
        for c in range(6):
            ref[c] = join(column_of(g, us, c, k))
        faces = join(0.5 * (column_of(g, us, 6, k) + column_of(g, us, 6, k, -1)))
        ref[6] = faces
        ref[6, 0:1, :] = faces[0:1] * row_ref[2 * N_ROW + KEEP]
    here = column_of(g, us, 7, cols)
    gphlo[7] = join(0.5 * column_of(g, us, 7, -1))
    gphhi[7] = join(0.5 * (here + column_of(g, us, 7, cols - 1)))
    gphhi[8] = join(0.5 * here)

    bottom, top = row_ref[g.flags + BOTTOM], row_ref[g.flags + TOP_END]
    near = row_ref[g.flags + NEAR] > 0.5

    def toward_low(of):
        signs = [1.0 if f > 0 else 1.0 - 2.0 * bottom for f in FLIPS]
        face = of(6)
        return [of(c) * signs[c] for c in range(6)] + [face * (1.0 - bottom), of(7) * signs[7], face * -bottom]

    def toward_high(of, far):
        signs = [1.0 if f > 0 else 1.0 - 2.0 * top for f in FLIPS]
        face = of(6) * (1.0 - top) - far * top
        return [of(c) * signs[c] for c in range(6)] + [face, of(7) * signs[7], far * (1.0 - top)]

    def send(at, low_value, high_value):
        go_ahead[at] = jnp.where(near, high_value, low_value)
        go_behind[at] = jnp.where(near, low_value, high_value)

    for t in range(cols // 8):
        p0, p1 = g.at(-1, t * 8), g.at(rows, t * 8)

        def tile_low(c):
            if c == 6:
                return join(keep_of(-1) * load(us, 6, p0))
            return join(load(us, c, p0) if c < 6 else tile7(p0))

        def tile_high(c):
            return join(load(us, c, p1) if c < 6 else tile6(rows, p1) if c == 6 else tile7(p1))

        lows = toward_low(tile_low)
        highs = toward_high(tile_high, join(keep_of(rows + 1) * load(us, 6, p1)))
        for c in range(9):
            send((c, slice(t * 8, t * 8 + 8)), lows[c], highs[c])
    for k, base in ((-1, 0), (cols, 9)):
        lows = toward_low(lambda c: line_of(c, -1, k))
        highs = toward_high(lambda c: line_of(c, rows, k), keep_of(rows + 1) * get_line(us, 6, g.at(rows, k)))
        for c in range(9):
            send((9, slice(base + c, base + c + 1)), lows[c], highs[c])
    send(
        (9, slice(18, 19)),
        (0.5 - bottom) * get_line(us, 7, g.at(-1, cols)),
        (0.5 - top) * get_line(us, 7, g.at(rows, cols)),
    )

    def settle(j, carry):
        leave(j).wait()
        return carry

    lax.fori_loop(0, rows, settle, 0)


def polar_nine(g, pole, of, low):
    signs = [1.0 if f > 0 else 1.0 - 2.0 * pole for f in FLIPS]
    values = [of(c, 0 if low else g.rows - 1) * signs[c] for c in range(8)]
    if low:
        values[6] = of(6, 0) * (1.0 - pole) - of(6, 2) * pole
        return values + [of(6, 1)]
    return values + [-of(6, g.rows - 1)]


def sender(g, row_ref, go_ahead, go_behind):
    near = row_ref[g.flags + NEAR] > 0.5

    def send(at, low_value, high_value):
        go_ahead[at] = jnp.where(near, high_value, low_value)
        go_behind[at] = jnp.where(near, low_value, high_value)

    return send


def send_rows(g, row_ref, of, go_ahead, go_behind):
    bottom, top = row_ref[g.flags + BOTTOM], row_ref[g.flags + TOP_END]
    send = sender(g, row_ref, go_ahead, go_behind)
    for c, (x, y) in enumerate(zip(polar_nine(g, bottom, of, True), polar_nine(g, top, of, False))):
        send(c, x, y)


def pack_kernel(g, row_ref, state, last_col, first_col, go_ahead, go_behind, edge, left, right, sem):
    rows, cols = g.rows, g.cols
    copies = [
        pltpu.make_async_copy(state.at[:, pl.ds(0, 3)], edge.at[:, pl.ds(0, 3)], sem.at[0]),
        pltpu.make_async_copy(state.at[:, pl.ds(rows - 1, 1)], edge.at[:, pl.ds(3, 1)], sem.at[1]),
        pltpu.make_async_copy(state.at[:, :, pl.ds(0, 8)], left, sem.at[2]),
        pltpu.make_async_copy(state.at[:, :, pl.ds(cols - 8, 8)], right, sem.at[3]),
    ]
    for copy in copies:
        copy.start()
    for copy in copies[:2]:
        copy.wait()
    send_rows(g, row_ref, lambda c, j: edge[c, j if j < 3 else 3], go_ahead, go_behind)
    for copy in copies[2:]:
        copy.wait()

    def line(j, carry):
        for c in range(8):
            first_col[c, pl.ds(j, 1), :] = left[c, j, 0:1, :]
            last_col[c, pl.ds(j, 1), :] = right[c, j, 7:8, :]
        first_col[8, pl.ds(j, 1), :] = left[7, j, 1:2, :]
        return carry

    lax.fori_loop(0, rows, line, 0)


def pack_corner_kernel(g, row_ref, phlo, phhi, go_ahead, go_behind):
    bottom, top = row_ref[g.flags + BOTTOM], row_ref[g.flags + TOP_END]
    send = sender(g, row_ref, go_ahead, go_behind)
    for ref, base in ((phlo, 0), (phhi, 9)):
        of = lambda c, j: ref[c, j : j + 1, :]
        for c, (x, y) in enumerate(zip(polar_nine(g, bottom, of, True), polar_nine(g, top, of, False))):
            send(slice(base + c, base + c + 1), x, y)
    send(
        slice(18, 19),
        (1.0 - 2.0 * bottom) * phhi[8, 0:1, :],
        (1.0 - 2.0 * top) * phhi[8, g.rows - 1 : g.rows, :],
    )


def turn_kernel(g, row_ref, ahead, behind, to_left, to_right):
    low, high = picker(g, row_ref, ahead, behind)
    to_left[0:9, :] = low(9, slice(0, 9))
    to_left[9:18, :] = high(9, slice(0, 9))
    to_right[0:10, :] = low(9, slice(9, 19))
    to_right[10:20, :] = high(9, slice(9, 19))


def finish_kernel(g, row_ref, part, *refs):
    given, refs = refs[:3], refs[3:]
    ahead, behind, from_right, from_left, lines_right, lines_left, out, edge, left, right, sem = refs
    rows, cols = g.rows, g.cols
    inner = pl.ds(3, rows - 4)
    places = (
        ((slice(None), pl.ds(0, 3)), edge.at[:, pl.ds(0, 3)]),
        ((slice(None), pl.ds(rows - 1, 1)), edge.at[:, pl.ds(3, 1)]),
        ((slice(None), inner, pl.ds(0, 8)), left),
        ((slice(None), inner, pl.ds(cols - 8, 8)), right),
    )
    leave = [pltpu.make_async_copy(ref, out.at[at], sem.at[i]) for i, (at, ref) in enumerate(places)]
    for c in range(8):
        edge[c] = given[0][c]
    low, high = picker(g, row_ref, ahead, behind)
    bottom = row_ref[g.flags + BOTTOM]
    for c in range(8):
        edge[c, 0] += 0.5 * low(c)
        edge[c, 3] += 0.5 * high(c)
    for e, share in ((1, 0.5 - 0.5 * bottom), (2, 0.5 * bottom)):
        edge[6, e] += share * low(8)
        for lines, k in ((lines_right, cols - 1), (lines_left, 0)):
            edge[6, e, k : k + 1, :] += share * lines[8:9, :]
    for e, right0, left0, second in ((0, 0, 0, 9), (3, 9, 10, 19)):
        for c in range(8):
            edge[c, e, cols - 1 : cols, :] += 0.5 * lines_right[right0 + c : right0 + c + 1, :]
            edge[c, e, 0:1, :] += 0.5 * lines_left[left0 + c : left0 + c + 1, :]
        edge[7, e, 1:2, :] += 0.5 * lines_left[second : second + 1, :]

    def columns(ref0, ref1, e, j):
        for c in range(8):
            ref0[c, e, 0:1, :] += 0.5 * from_left[c, pl.ds(j, 1), :]
            k = ref1.shape[2]
            ref1[c, e, k - 1 : k, :] += 0.5 * from_right[c, pl.ds(j, 1), :]
        ref0[7, e, 1:2, :] += 0.5 * from_left[8, pl.ds(j, 1), :]

    for e, j in ((0, 0), (1, 1), (2, 2), (3, rows - 1)):
        columns(edge, edge, e, j)
    for copy in leave[:2]:
        copy.start()

    def step(e, carry):
        for c in range(8):
            left[c, e] = given[1][c, e]
            right[c, e] = given[2][c, e]
        columns(left, right, e, e + 3)
        return carry

    lax.fori_loop(0, rows - 4, step, 0)
    for copy in leave[2:]:
        copy.start()
    for copy in leave:
        copy.wait()


ANY = pl.BlockSpec(memory_space=pl.ANY)
VMEM = pl.BlockSpec(memory_space=pltpu.VMEM)
SMEM = pl.BlockSpec(memory_space=pltpu.SMEM)


def call(kernel, ins, outs, scratch, flops, limit, interpret=False):
    return pl.pallas_call(
        kernel,
        out_shape=[jax.ShapeDtypeStruct(s, jnp.float32) for _, s in outs],
        in_specs=[SMEM] + ins,
        out_specs=[s for s, _ in outs],
        scratch_shapes=scratch,
        compiler_params=pltpu.CompilerParams(vmem_limit_bytes=limit << 20),
        cost_estimate=pl.CostEstimate(flops=flops, bytes_accessed=16 << 20, transcendentals=0),
        interpret=interpret,
    )


def buffers(*shapes):
    return [pltpu.VMEM(s, jnp.float32) for s in shapes]


def rim_shapes(g):
    strip = (8, g.rows - 4, 8, g.rads)
    return [(8, 4, g.cols, g.rads), strip, strip]


def sizes(g):
    return (
        (8, g.rows, g.cols, g.rads),
        [(8, g.rows, g.rads), (9, g.rows, g.rads)],
        (9, g.cols, g.rads),
        (24, g.rads),
    )


def forward(g, table, own, halos, planes, interpret=False):
    n = g.slots
    shape, sides, body, lines = sizes(g)
    scratch = buffers((8, 2, n, LANES), (15, 2, n, LANES), (6, n, LANES), (10, 2, n, LANES), shape)
    dma = pltpu.SemaphoreType.DMA
    scratch += [dma((g.rows, 2)), dma((g.rows,))]
    outs = [(ANY, shape)] + [(VMEM, s) for s in sides + [body, body]]
    run = call(functools.partial(forward_kernel, g), [ANY] + [VMEM] * 7, outs, scratch, 10**8, 48, interpret)
    return run(table, own, *halos, planes)


def adjoint(g, table, own, halos, cot, planes, more, received, interpret=False):
    n = g.slots
    shape, sides, body, lines = sizes(g)
    message = (10, g.cols, g.rads)
    outs = [(ANY, shape)] + [(VMEM, s) for s in sides + [message, message]]
    if received:
        outs += [(VMEM, s) for s in rim_shapes(g)]
    scratch = buffers(
        (8, 2, n, LANES),
        (8, 2, n, LANES),
        (13, 2, n, LANES),
        (11, 2, g.cols, LANES),
        (11, 2, 8 + g.cols, LANES),
        shape,
        (11, 2, g.rows + 8, LANES),
        (8, 2, g.rows, LANES),
        (g.rows, LANES),
    )
    if received:
        scratch += buffers((3, 2, n, LANES), (2, n, LANES))
    dma = pltpu.SemaphoreType.DMA
    scratch += [dma((g.rows, 2)), dma((g.rows, 2)), dma((g.rows,)), dma((g.rows,))]
    ins = [ANY, ANY] + [VMEM] * 7 + ([ANY] + [VMEM] * 6 if received else [VMEM] * 2)
    run = call(functools.partial(adjoint_kernel, g, received), ins, outs, scratch, 3 * 10**8, 48, interpret)
    return run(table, own, cot, *halos, planes, *more)


def edges_of(g, table, cot, planes):
    n = g.slots
    outs = [(VMEM, (3, 2, n, LANES)), (VMEM, (2, n, LANES))]
    scratch = buffers((3, 2, n, LANES)) + [pltpu.SemaphoreType.DMA((g.rows, 2))]
    return call(functools.partial(edge_kernel, g), [ANY, VMEM], outs, scratch, 10**8, 16)(table, cot, planes)


def pack(g, table, state):
    shape, sides, body, lines = sizes(g)
    strip = (8, g.rows, 8, g.rads)
    scratch = buffers((8, 4, g.cols, g.rads), strip, strip) + [pltpu.SemaphoreType.DMA((4,))]
    outs = [(VMEM, s) for s in sides + [body, body]]
    return call(functools.partial(pack_kernel, g), [ANY], outs, scratch, 10**6, 58)(table, state)


def pack_corners(g, table, phlo, phhi):
    lines = sizes(g)[3]
    return call(functools.partial(pack_corner_kernel, g), [VMEM] * 2, [(VMEM, lines)] * 2, [], 10**6, 16)(
        table, phlo, phhi
    )


def turn(g, table, ahead, behind):
    lines = sizes(g)[3]
    return call(functools.partial(turn_kernel, g), [VMEM] * 2, [(VMEM, lines)] * 2, [], 10**6, 16)(
        table, ahead, behind
    )


def finish(g, table, part, *more):
    return pl.pallas_call(
        functools.partial(finish_kernel, g),
        out_shape=jax.ShapeDtypeStruct(part.shape, jnp.float32),
        in_specs=[SMEM, ANY] + [VMEM] * 9,
        out_specs=ANY,
        input_output_aliases={1: 0},
        scratch_shapes=buffers(*rim_shapes(g)) + [pltpu.SemaphoreType.DMA((4,))],
        compiler_params=pltpu.CompilerParams(vmem_limit_bytes=44 << 20),
        cost_estimate=pl.CostEstimate(flops=10**6, bytes_accessed=7 << 20, transcendentals=0),
    )(table, part, *more)


class Place:
    def __init__(self):
        self.n_th, self.n_ph = lax.axis_size("th"), lax.axis_size("ph")
        n_th, n_ph = self.n_th, self.n_ph
        half = n_ph // 2
        self.th, self.ph = lax.axis_index("th"), lax.axis_index("ph")
        self.at_bottom, self.at_top = self.th == 0, self.th == n_th - 1
        self.near = self.ph < half
        self.right = [(i, (i + 1) % n_ph) for i in range(n_ph)]
        self.left = [(j, i) for i, j in self.right]
        self.round = []
        for t in range(n_th):
            for p in range(half):
                self.round.append((t * n_ph + p, (t + 1) * n_ph + p if t < n_th - 1 else t * n_ph + p + half))
                self.round.append((t * n_ph + p + half, (t - 1) * n_ph + p + half if t > 0 else p))
        self.back = [(j, i) for i, j in self.round]

    def polar(self, ahead, behind):
        both = ("th", "ph")
        return lax.ppermute(ahead, both, self.round), lax.ppermute(behind, both, self.back)

    def sideways(self, to_right, to_left):
        return lax.ppermute(to_right, "ph", self.right), lax.ppermute(to_left, "ph", self.left)


def shards(state, cotangent):
    place = Place()
    _, rows, cols, rads = state.shape
    g = Grid(rows, cols, rads, rows * place.n_th, cols * place.n_ph)
    every = g.row_table()
    tables = np.zeros((2 * place.n_th, g.flags + 3), np.float32)
    for n in range(2 * place.n_th):
        t = n // 2
        tables[n, : g.flags] = every[t * rows : t * rows + rows + 5].reshape(-1)
        tables[n, g.flags :] = (t == 0, t == place.n_th - 1, n % 2)
    which = 2 * place.th + place.near.astype(jnp.int32)
    table = lax.dynamic_index_in_dim(jnp.asarray(tables), which, 0, keepdims=False)
    planes = jnp.asarray(g.radial_planes())

    def halos_of(rims, beside=None):
        last, first, ahead, behind = rims
        phlo, phhi = place.sideways(last, first)
        body = place.polar(ahead, behind)
        done = None
        if beside is not None:
            phlo, phhi, done = lax.optimization_barrier((phlo, phhi, beside(first)))
        return (phlo, phhi) + tuple(body) + tuple(place.polar(*pack_corners(g, table, phlo, phhi))), done

    def give_back(parts):
        gphlo, gphhi, ahead, behind = parts
        from_left, from_right = place.sideways(gphhi, gphlo)
        ahead, behind = place.polar(ahead, behind)
        to_left, to_right = turn(g, table, ahead, behind)
        lines_left, lines_right = place.sideways(to_right, to_left)
        return ahead, behind, from_right, from_left, lines_right, lines_left

    def edges_beside(rim):
        return edges_of(g, table, lax.optimization_barrier((cotangent, rim))[0], planes)

    halos_zero, edges = halos_of(pack(g, table, state), edges_beside)
    moved, *rims = forward(g, table, state, halos_zero, planes)
    halos_one, _ = halos_of(rims)
    part, *ghosts = adjoint(g, table, moved, halos_one, cotangent, planes, edges, False)
    more = (cotangent,) + give_back(ghosts)
    part, *ghosts = adjoint(g, table, state, halos_zero, part, planes, more, True)
    return finish(g, table, part, *ghosts[4:], *give_back(ghosts[:4]))


def solution(mesh):
    placed = (P(None, "th", "ph", None), P(None, "th", "ph", None))
    return jax.shard_map(
        shards, mesh=mesh, in_specs=placed, out_specs=P(None, "th", "ph", None), check_vma=False
    )
```
